32 devices in a mesh: field: 2 (over y), expo: 8 (over z, core), strip: 2 (over x).
Axes of the slice: x: 2, y: 2, z: 4, core: 2. Of those that a mesh axis runs over, the one named last changes fastest.
Arguments:
- science: bfloat16 [128, 64, 512], P(('field', 'expo'), 'strip'), parts along dimension 0, may hold values from -6 to 6
- inv_var: bfloat16 [128, 64, 512], P(('field', 'expo'), 'strip'), parts along dimension 0, may hold values from 0.25 to 4
- psf_rows: float32 [128, 9], P(('field', 'expo')), parts along dimension 0, may hold values from 0.2 to 1
- psf_cols: float32 [128, 9], P(('field', 'expo')), parts along dimension 0, may hold values from 0.2 to 1
- row_shift: int32 [128, 8], P(('field', 'expo')), parts along dimension 0, may hold values from 0 to 16
- col_shift: int32 [128, 8], P(('field', 'expo')), parts along dimension 0, may hold values from -16 to 16
- exposure_ok: int32 [128], P(('field', 'expo')), parts along dimension 0, may hold values 0 or 1
Outputs:
- likelihood: float32 [2, 16, 32, 512], P('strip', 'field', 'expo'), parts along dimension 1
The draws below stay inside these ranges and needn't reach their ends.
There are 2 independent parts, one for each index of `field`. The reference program is written for one: setup_inputs(seed, part) draws one part's arguments, and reference() takes and returns one part's arrays. A program takes and returns all parts, laid end to end along the dimension named above; each array names one. Nothing has to cross between parts.
Inputs may be any that keep to these rules, and one draw needn't show every extreme that they name: `row_shift`: every shift lies in 0..16, so S[e, v, r] reads map rows r to r + 16 only, never lower rows.
All inputs are finite; a program needn't handle non-finite values. No bound on the sum of `exposure_ok` on one device may be relied on, other than what follows from the above.
Results may differ from the reference program's by a relative error of at most 0.0017.
Values may be sent and summed in bfloat16 or wider, within the bound.
No kernel may reach another device: no remote copies, remote signals or barrier semaphores. Data moves between devices by JAX's collectives and lax.ppermute only.
A program may use at most 64 MiB of HBM per device.

```python
import math
import jax
import jax.numpy as jnp
from jax import lax

COLS = 512
VELS = 8
PSF_RAD = 4
TAPS = 9
SHIFT = 16
ROWS_DEV = 32
EXPOSURES = 64
ROWS = 64
N_STRIP = 2


def place_ends(drawn, stream_key, least, top_value):
    longest = drawn.shape.index(max(drawn.shape))
    spots = []
    for shift in (0, 1):
        where = [jax.random.randint(jax.random.fold_in(stream_key, axis), (), 0, length) for axis, length in enumerate(drawn.shape)]
        where[longest] = (where[longest] + shift) % drawn.shape[longest]
        spots.append(tuple(where))
    return drawn.at[spots[0]].set(least).at[spots[1]].set(top_value)


def block_levels(own_key, extent, pieces, least, largest):
    def one(dim, shards_of):
        steps = jax.random.uniform(jax.random.fold_in(jax.random.fold_in(own_key, 6), dim), (shards_of,), jnp.float32, least / len(pieces), largest / len(pieces))
        return jnp.repeat(jnp.exp(steps), extent[dim] // shards_of).reshape((-1,) + (1,) * (len(extent) - dim - 1))

    gain = one(*pieces[0])
    for cut in pieces[1:]:
        gain = gain * one(*cut)
    return gain


def noise(stream_key, extent, spread, limit, split=(), dtype=jnp.bfloat16):
    loudness = block_levels(stream_key, extent, split, -0.22, 0.18) if split else 1.0
    array = jax.random.normal(stream_key, extent, jnp.float32) * spread * loudness
    return jnp.minimum(jnp.maximum(array, -limit), limit).astype(dtype)


def setup_inputs(seed: int = 0, part: int = 0) -> dict:
    key_list = jax.random.split(jax.random.key(seed), 8)
    own_keys = jax.random.split(jax.random.fold_in(key_list[7], part), 8)
    science = noise(own_keys[0], (EXPOSURES, ROWS, COLS), 1.0, 6.0, ((0, 8), (1, 2)))
    inv_var = jnp.clip(jnp.exp(math.log(4.0) - 2.7725887 * jax.random.uniform(own_keys[1], (EXPOSURES, ROWS, COLS), jnp.float32) ** block_levels(own_keys[1], (EXPOSURES, ROWS, COLS), ((0, 8), (1, 2)), -0.2, 0.2)), 0.25, 4.0).astype(jnp.bfloat16)
    psf_rows = jnp.clip(0.2 + 0.8 * jax.random.uniform(own_keys[2], (EXPOSURES, TAPS), jnp.float32) ** block_levels(own_keys[2], (EXPOSURES, TAPS), ((0, 8),), -0.2, 0.2), 0.2, 1.0)
    psf_cols = jnp.clip(0.2 + 0.8 * jax.random.uniform(own_keys[3], (EXPOSURES, TAPS), jnp.float32) ** block_levels(own_keys[3], (EXPOSURES, TAPS), ((0, 8),), -0.2, 0.2), 0.2, 1.0)
    row_shift = place_ends(jax.random.randint(own_keys[4], (EXPOSURES, VELS), 0, SHIFT + 1), jax.random.fold_in(own_keys[4], 1), 0, SHIFT).astype(jnp.int32)
    col_shift = place_ends(jax.random.randint(own_keys[5], (EXPOSURES, VELS), 0 - SHIFT, SHIFT + 1), jax.random.fold_in(own_keys[5], 1), 0 - SHIFT, SHIFT).astype(jnp.int32)
    exposure_ok = place_ends((jax.random.randint(own_keys[6], (EXPOSURES,), 0, 4) < 3).astype(jnp.int32), jax.random.fold_in(own_keys[6], 1), 0, 1)
    return dict(science=science, inv_var=inv_var, psf_rows=psf_rows, psf_cols=psf_cols, row_shift=row_shift, col_shift=col_shift, exposure_ok=exposure_ok)


def filter_one(picture, row_taps, col_taps, out_rows):
    columns = picture.shape[2]
    tap_count = row_taps.shape[1]
    radius = tap_count // 2
    padded = jnp.pad(picture, ((0, 0), (0, 0), (radius, radius)))
    colpass = col_taps[:, 0, None, None] * padded[:, :, 0:columns]
    for b in range(1, tap_count):
        colpass = colpass + col_taps[:, b, None, None] * padded[:, :, b:b + columns]
    result = row_taps[:, 0, None, None] * colpass[:, 0:out_rows]
    for a in range(1, tap_count):
        result = result + row_taps[:, a, None, None] * colpass[:, a:a + out_rows]
    return result.astype(jnp.bfloat16)

def matched_pair(science, inv_var, psf_rows, psf_cols, out_rows):
    science_f = science.astype(jnp.float32)
    inverse = inv_var.astype(jnp.float32)
    signal_map = filter_one(science_f * inverse, psf_rows, psf_cols, out_rows)
    depth_map = filter_one(inverse, psf_rows * psf_rows, psf_cols * psf_cols, out_rows)
    return (signal_map, depth_map)

def reference(science, inv_var, psf_rows, psf_cols, row_shift, col_shift, exposure_ok):
    radius = PSF_RAD

    def windows(signal_map, depth_map, shifts_row, shifts_col):
        stacked = jnp.stack([signal_map, depth_map])
        padded = jnp.pad(stacked, ((0, 0), (0, SHIFT), (SHIFT, SHIFT)))

        def cut_one(row_at, col_at):
            return lax.dynamic_slice(padded, (jnp.zeros((), jnp.int32), row_at.astype(jnp.int32), (col_at + SHIFT).astype(jnp.int32)), (2, ROWS, COLS))
        return jax.vmap(cut_one)(shifts_row, shifts_col).astype(jnp.float32)

    def shifted(scan_item):
        sci_one, inv_one, rows_one, cols_one, shifts_row, shifts_col, usable = scan_item
        sci_pad = jnp.pad(sci_one[None], ((0, 0), (radius, radius), (0, 0)))
        inv_pad = jnp.pad(inv_one[None], ((0, 0), (radius, radius), (0, 0)))
        signal_map, depth_map = matched_pair(sci_pad, inv_pad, rows_one[None], cols_one[None], ROWS)
        return (windows(signal_map[0], depth_map[0], shifts_row, shifts_col), usable.astype(jnp.float32))
    scan_items = (science, inv_var, psf_rows, psf_cols, row_shift, col_shift, exposure_ok)

    def first_step(running, scan_item):
        windows_now, usable = shifted(scan_item)
        return (running + usable * windows_now, None)
    zeros_init = jnp.zeros((VELS, 2, ROWS, COLS), jnp.float32)
    firsts, _ = lax.scan(first_step, zeros_init, scan_items)
    flux_est = firsts[:, 0] / (firsts[:, 1] + 1.0)

    def second_step(running, scan_item):
        windows_now, usable = shifted(scan_item)
        signal = windows_now[:, 0]
        depth = windows_now[:, 1]
        residual = signal - flux_est * depth
        weight = usable / (1.0 + residual * residual / (depth + 1.0))
        return (running + jnp.stack([weight * signal, weight * depth], 1), None)
    robust, _ = lax.scan(second_step, zeros_init, scan_items)
    likelihood = robust[:, 0] / jnp.sqrt(robust[:, 1] + 1.0)
    return likelihood.reshape(VELS, N_STRIP, ROWS_DEV, COLS).transpose(1, 0, 2, 3)
```

```python
import functools

import jax
import jax.numpy as jnp
from jax import lax
from jax.experimental import pallas as pl
from jax.experimental.pallas import tpu as pltpu
from jax.sharding import PartitionSpec as P

SHIFT = 16
LANES = 128
SUBLANES = 8

SMEM = pl.BlockSpec(memory_space=pltpu.SMEM)
VMEM = pl.BlockSpec(memory_space=pltpu.VMEM)


def partner(index, step, count):
    if count & (count - 1) == 0:
        return index ^ step
    return (index + step) % count


def chunk_pairs(step, chunks, subs):
    return [
        (j * subs + k, partner(j, step, chunks) * subs + k) for j in range(chunks) for k in range(subs)
    ]


def sub_pairs(step, chunks, subs):
    return [
        (j * subs + k, j * subs + partner(k, step, subs)) for j in range(chunks) for k in range(subs)
    ]


def filter_kernel(
    radius, chunks, info, row_taps, col_taps, row_shift, col_shift, usable, science, inv_var, above, below, *rest
):
    sends, (pixels, colpass, maps, edges, params) = rest[:chunks], rest[chunks:]
    exposures, rows, columns = science.shape
    taps = 2 * radius + 1
    halo = above.shape[2]
    reach = rows + SHIFT
    third = reach // 2
    tiles = columns // LANES
    lead = SUBLANES
    span = pixels.shape[1]
    lane = lax.broadcasted_iota(jnp.int32, (SUBLANES, LANES), 1)
    has_above = info[0] > 0
    has_below = info[1] > 0
    own = info[2]
    zero = jnp.zeros((SUBLANES, LANES), jnp.float32)

    params[...] = jnp.zeros_like(params)
    vels = row_shift.shape[1]
    params[:, 0:vels] = row_shift[...].astype(jnp.float32)
    params[:, vels : 2 * vels] = col_shift[...].astype(jnp.float32)
    params[:, 2 * vels : 2 * vels + 1] = usable[...].astype(jnp.float32)

    def one_exposure(e, carry):
        for kind, cells in ((0, science), (1, inv_var)):
            pixels[kind, lead : lead + rows] = cells[e].astype(jnp.float32)
            top = above[kind, e, halo - lead : halo].astype(jnp.float32)
            pixels[kind, 0:lead] = jnp.where(has_above, top, 0.0)
            low = below[kind, e].astype(jnp.float32)
            pixels[kind, lead + rows : lead + rows + halo] = jnp.where(has_below, low, 0.0)
        for g in range(span // SUBLANES):
            at = pl.ds(g * SUBLANES, SUBLANES)
            inverse = pixels[1, at]
            product = pixels[0, at] * inverse
            for m, picture in ((0, product), (1, inverse)):
                cut = [picture[:, t * LANES : (t + 1) * LANES] for t in range(tiles)]
                totals = [None] * tiles
                for b in range(taps):
                    step = b - radius
                    tap = col_taps[e, b]
                    if m == 1:
                        tap = tap * tap
                    if step == 0:
                        moved = cut
                    else:
                        turned = [pltpu.roll(c, (-step) % LANES, 1) for c in cut]
                        if step > 0:
                            turned = turned + [zero]
                            moved = [
                                jnp.where(lane < LANES - step, turned[t], turned[t + 1]) for t in range(tiles)
                            ]
                        else:
                            turned = [zero] + turned
                            moved = [
                                jnp.where(lane >= -step, turned[t + 1], turned[t]) for t in range(tiles)
                            ]
                    for t in range(tiles):
                        term = tap * moved[t]
                        totals[t] = term if totals[t] is None else totals[t] + term
                for t in range(tiles):
                    colpass[m, t, at] = totals[t]

        def padded_group(m, g):
            out = []
            for t in range(tiles):
                total = None
                for a in range(taps):
                    tap = row_taps[e, a]
                    if m == 1:
                        tap = tap * tap
                    term = tap * colpass[m, t, pl.ds(g * SUBLANES + lead - radius + a, SUBLANES)]
                    total = term if total is None else total + term
                if g * SUBLANES >= rows:
                    total = jnp.where(has_below, total, 0.0)
                out.append(pltpu.roll(total, SHIFT, 1))
            out = [zero] + out + [zero]
            return [jnp.where(lane < SHIFT, out[t], out[t + 1]) for t in range(tiles + 1)]

        for g in range(third // SUBLANES):
            parts = [padded_group(m, g + h * (third // SUBLANES)) for m in (0, 1) for h in (0, 1)]
            for t in range(tiles):
                for q, part in enumerate(parts):
                    at = (q // 2) * exposures * reach + e * reach + (q % 2) * third + g * SUBLANES
                    maps[t, pl.ds(pl.multiple_of(at, SUBLANES), SUBLANES)] = part[t]
                packed = parts[0][t + 1]
                for q in range(1, 4):
                    packed = jnp.where(lane < 2 * SHIFT * q, packed, pltpu.roll(parts[q][t + 1], 2 * SHIFT * q, 1))
                at = e * third + g * SUBLANES
                edges[t, pl.ds(pl.multiple_of(at, SUBLANES), SUBLANES)] = packed
        return carry

    lax.fori_loop(0, exposures, one_exposure, 0)
    main = 2 * exposures * reach
    edge = exposures * third
    for step in range(chunks):
        to = partner(own, step, chunks)
        sends[step][0:main] = maps[to].astype(jnp.bfloat16)
        sends[step][main : main + edge] = edges[to].astype(jnp.bfloat16)
        sends[step][main + edge : main + edge + exposures] = params[...].astype(jnp.bfloat16)


def stack_kernel(
    groups, chunks, exposures, rows, vels, share, info, *rest
):
    blocks = rest[:groups]
    outs = rest[groups : groups + chunks]
    main, side, windows, edge, whole_params, scalars, result, sem = rest[groups + chunks :]
    reach = rows + SHIFT
    third = reach // 2
    own = info[0]
    first_vel = info[1]
    main_rows = 2 * exposures * reach
    edge_rows = exposures * third
    total = groups * exposures
    for g in range(groups):
        whole_params[g * exposures : (g + 1) * exposures] = (
            blocks[g][main_rows + edge_rows : main_rows + edge_rows + exposures].astype(jnp.float32).astype(jnp.int32)
        )
    fetch = pltpu.make_async_copy(whole_params, scalars, sem)
    fetch.start()
    fetch.wait()
    for g in range(groups):
        edge[...] = blocks[g][main_rows : main_rows + edge_rows].astype(jnp.float32)

        def unpack(e, carry, g=g):
            at = g * exposures + e
            keep = scalars[at, 2 * vels].astype(jnp.float32)
            for m in (0, 1):
                start = pl.multiple_of(m * exposures * reach + e * reach, reach)
                main[at, m] = blocks[g][pl.ds(start, reach)].astype(jnp.float32) * keep
            packed = edge[pl.ds(pl.multiple_of(e * third, SUBLANES), third)] * keep
            for q in range(4):
                piece = packed if q == 0 else pltpu.roll(packed, LANES - 2 * SHIFT * q, 1)
                side[at, q // 2, (q % 2) * third : (q % 2 + 1) * third] = piece
            return carry

        lax.fori_loop(0, exposures, unpack, 0)

    lane = lax.broadcasted_iota(jnp.int32, (rows, LANES), 1)
    zeros = jnp.zeros((rows, LANES), jnp.float32)

    def one_velocity(v, carry):
        def gather(e, sums):
            row_at = scalars[e, first_vel + v]
            col_at = scalars[e, vels + first_vel + v] + SHIFT
            turn = lax.rem(LANES - col_at, LANES)
            from_side = lane < col_at
            out = []
            for m in (0, 1):
                cells = jnp.where(
                    from_side, side[e, m, pl.ds(row_at, rows)], main[e, m, pl.ds(row_at, rows)]
                )
                cells = pltpu.roll(cells, turn, 1)
                windows[e, m] = cells
                out.append(sums[m] + cells)
            return tuple(out)

        signal_sum, depth_sum = lax.fori_loop(0, total, gather, (zeros, zeros), unroll=2)
        flux = signal_sum / (depth_sum + 1.0)

        def reweigh(e, sums):
            signal = windows[e, 0]
            depth = windows[e, 1]
            residual = signal - flux * depth
            base = depth + 1.0
            weight = base / (base + residual * residual)
            return sums[0] + weight * signal, sums[1] + weight * depth

        robust = lax.fori_loop(0, total, reweigh, (zeros, zeros), unroll=2)
        result[v] = robust[0] / jnp.sqrt(robust[1] + 1.0)
        return carry

    lax.fori_loop(0, share, one_velocity, 0)
    block = rows // chunks
    for step in range(chunks):
        to = partner(own, step, chunks)
        outs[step][...] = result[:, pl.ds(pl.multiple_of(to * block, block), block)]


def columns_kernel(chunks, subs, info, *rest):
    pieces = rest[:chunks]
    outs = rest[chunks : chunks + subs]
    held, wide = rest[chunks + subs :]
    own_chunk, own_sub = info[0], info[1]
    for step in range(chunks):
        held[step] = pieces[step][...]
    rows = wide.shape[2]
    for c in range(chunks):
        piece = held[partner(own_chunk, c, chunks)]
        for k in range(subs):
            wide[k, :, :, c * LANES : (c + 1) * LANES] = piece[:, k * rows : (k + 1) * rows]
    for step in range(subs):
        outs[step][...] = wide[partner(own_sub, step, subs)]


def velocities_kernel(subs, info, *rest):
    pieces = rest[:subs]
    out, held = rest[subs:]
    own_sub = info[1]
    for step in range(subs):
        held[step] = pieces[step][...]
    share = held.shape[1]
    for k in range(subs):
        out[k * share : (k + 1) * share] = held[partner(own_sub, k, subs)]


def per_device(science, inv_var, psf_rows, psf_cols, row_shift, col_shift, exposure_ok):
    exposures, rows, columns = science.shape
    vels = row_shift.shape[1]
    radius = psf_rows.shape[1] // 2
    strips = lax.axis_size("strip")
    members = lax.axis_size("expo")
    chunks = columns // LANES
    subs = members // chunks
    share = vels // subs
    reach = rows + SHIFT
    halo = -(-(radius + SHIFT) // SUBLANES) * SUBLANES
    strip = lax.axis_index("strip")
    me = lax.axis_index("expo")
    own_chunk = me // subs
    own_sub = me % subs

    head = jnp.stack([science[:, :halo], inv_var[:, :halo]])
    tail = jnp.stack([science[:, rows - halo :], inv_var[:, rows - halo :]])
    if strips == 2:
        met = lax.ppermute(jnp.where(strip == 0, tail, head), "strip", [(0, 1), (1, 0)])
        above = below = met
    else:
        above = lax.ppermute(tail, "strip", [(i, i + 1) for i in range(strips - 1)])
        below = lax.ppermute(head, "strip", [(i + 1, i) for i in range(strips - 1)])
    info = jnp.stack([strip > 0, strip < strips - 1, own_chunk]).astype(jnp.int32)

    main_rows = 2 * exposures * reach
    edge_rows = exposures * reach // 2
    sent_rows = main_rows + edge_rows + exposures
    span = rows + halo + SUBLANES
    sent = jax.ShapeDtypeStruct((sent_rows, LANES), jnp.bfloat16)
    sends = pl.pallas_call(
        functools.partial(filter_kernel, radius, chunks),
        out_shape=[sent] * chunks,
        in_specs=[SMEM] * 3 + [VMEM] * 7,
        out_specs=[VMEM] * chunks,
        scratch_shapes=[
            pltpu.VMEM((2, span, columns), jnp.float32),
            pltpu.VMEM((2, chunks, span, LANES), jnp.float32),
            pltpu.VMEM((chunks, main_rows, LANES), jnp.float32),
            pltpu.VMEM((chunks, edge_rows, LANES), jnp.float32),
            pltpu.VMEM((exposures, LANES), jnp.float32),
        ],
        name="filter_maps",
    )(info, psf_rows, psf_cols, row_shift, col_shift, exposure_ok[:, None], science, inv_var, above, below)

    blocks = [sends[0]]
    for step in range(1, chunks):
        blocks.append(lax.ppermute(sends[step], "expo", chunk_pairs(step, chunks, subs)))
    for step in range(1, subs):
        pairs = sub_pairs(step, chunks, subs)
        blocks += [lax.ppermute(block, "expo", pairs) for block in blocks[:chunks]]

    groups = len(blocks)
    block_rows = rows // chunks
    piece = jax.ShapeDtypeStruct((share, block_rows, LANES), jnp.float32)
    where = jnp.stack([own_chunk, own_sub * share]).astype(jnp.int32)
    total = groups * exposures
    pieces = pl.pallas_call(
        functools.partial(stack_kernel, groups, chunks, exposures, rows, vels, share),
        out_shape=[piece] * chunks,
        in_specs=[SMEM] + [VMEM] * groups,
        out_specs=[VMEM] * chunks,
        scratch_shapes=[
            pltpu.VMEM((total, 2, reach, LANES), jnp.float32),
            pltpu.VMEM((total, 2, reach, LANES), jnp.float32),
            pltpu.VMEM((total, 2, rows, LANES), jnp.float32),
            pltpu.VMEM((edge_rows, LANES), jnp.float32),
            pltpu.VMEM((total, LANES), jnp.int32),
            pltpu.SMEM((total, LANES), jnp.int32),
            pltpu.VMEM((share, rows, LANES), jnp.float32),
            pltpu.SemaphoreType.DMA(()),
        ],
        name="stack_twice",
    )(where, *blocks)

    held = [pieces[0]]
    for step in range(1, chunks):
        held.append(lax.ppermute(pieces[step], "expo", chunk_pairs(step, chunks, subs)))
    place = jnp.stack([own_chunk, own_sub]).astype(jnp.int32)
    out_rows = block_rows // subs
    wide = jax.ShapeDtypeStruct((share, out_rows, columns), jnp.float32)
    parts = pl.pallas_call(
        functools.partial(columns_kernel, chunks, subs),
        out_shape=[wide] * subs,
        in_specs=[SMEM] + [VMEM] * chunks,
        out_specs=[VMEM] * subs,
        scratch_shapes=[
            pltpu.VMEM((chunks, share, block_rows, LANES), jnp.float32),
            pltpu.VMEM((subs, share, out_rows, columns), jnp.float32),
        ],
        name="join_columns",
    )(place, *held)
    met = [parts[0]]
    for step in range(1, subs):
        met.append(lax.ppermute(parts[step], "expo", sub_pairs(step, chunks, subs)))
    likelihood = pl.pallas_call(
        functools.partial(velocities_kernel, subs),
        out_shape=jax.ShapeDtypeStruct((vels, out_rows, columns), jnp.float32),
        in_specs=[SMEM] + [VMEM] * subs,
        out_specs=VMEM,
        scratch_shapes=[pltpu.VMEM((subs, share, out_rows, columns), jnp.float32)],
        name="join_velocities",
    )(place, *met)
    return likelihood[None]


def solution(mesh):
    in_specs = (
        P(("field", "expo"), "strip", None),
        P(("field", "expo"), "strip", None),
        P(("field", "expo"), None),
        P(("field", "expo"), None),
        P(("field", "expo"), None),
        P(("field", "expo"), None),
        P(("field", "expo")),
    )
    out_specs = P("strip", "field", "expo", None)
    return jax.shard_map(
        per_device, mesh=mesh, in_specs=in_specs, out_specs=out_specs, check_vma=False
    )
```

```python
import functools

import jax
import jax.numpy as jnp
from jax import lax
from jax.experimental import pallas as pl
from jax.experimental.pallas import tpu as pltpu
from jax.sharding import PartitionSpec as P

SHIFT = 16
LANES = 128
SUBLANES = 8
UNROLL = 8

SMEM = pl.BlockSpec(memory_space=pltpu.SMEM)
VMEM = pl.BlockSpec(memory_space=pltpu.VMEM)


def partner(index, step, count):
    if count & (count - 1) == 0:
        return index ^ step
    return (index + step) % count


def chunk_pairs(step, chunks, subs):
    return [
        (j * subs + k, partner(j, step, chunks) * subs + k) for j in range(chunks) for k in range(subs)
    ]


def sub_pairs(step, chunks, subs):
    return [
        (j * subs + k, j * subs + partner(k, step, subs)) for j in range(chunks) for k in range(subs)
    ]


def filter_kernel(
    radius, chunks, info, row_taps, col_taps, row_shift, col_shift, usable, science, inv_var, above, below, *rest
):
    sends, (pixels, colpass, maps, edges, params) = rest[:chunks], rest[chunks:]
    exposures, rows, columns = science.shape
    taps = 2 * radius + 1
    halo = above.shape[2]
    reach = rows + SHIFT
    third = reach // 2
    tiles = columns // LANES
    lead = SUBLANES
    span = pixels.shape[1]
    lane = lax.broadcasted_iota(jnp.int32, (SUBLANES, LANES), 1)
    has_above = info[0] > 0
    has_below = info[1] > 0
    own = info[2]
    zero = jnp.zeros((SUBLANES, LANES), jnp.float32)

    params[...] = jnp.zeros_like(params)
    vels = row_shift.shape[1]
    params[:, 0:vels] = row_shift[...].astype(jnp.float32)
    params[:, vels : 2 * vels] = col_shift[...].astype(jnp.float32)
    params[:, 2 * vels : 2 * vels + 1] = usable[...].astype(jnp.float32)

    def one_exposure(e, carry):
        for kind, cells in ((0, science), (1, inv_var)):
            pixels[kind, lead : lead + rows] = cells[e].astype(jnp.float32)
            top = above[kind, e, halo - lead : halo].astype(jnp.float32)
            pixels[kind, 0:lead] = jnp.where(has_above, top, 0.0)
            low = below[kind, e].astype(jnp.float32)
            pixels[kind, lead + rows : lead + rows + halo] = jnp.where(has_below, low, 0.0)
        for g in range(span // SUBLANES):
            at = pl.ds(g * SUBLANES, SUBLANES)
            inverse = pixels[1, at]
            product = pixels[0, at] * inverse
            for m, picture in ((0, product), (1, inverse)):
                cut = [picture[:, t * LANES : (t + 1) * LANES] for t in range(tiles)]
                totals = [None] * tiles
                for b in range(taps):
                    step = b - radius
                    tap = col_taps[e, b]
                    if m == 1:
                        tap = tap * tap
                    if step == 0:
                        moved = cut
                    else:
                        turned = [pltpu.roll(c, (-step) % LANES, 1) for c in cut]
                        if step > 0:
                            turned = turned + [zero]
                            moved = [
                                jnp.where(lane < LANES - step, turned[t], turned[t + 1]) for t in range(tiles)
                            ]
                        else:
                            turned = [zero] + turned
                            moved = [
                                jnp.where(lane >= -step, turned[t + 1], turned[t]) for t in range(tiles)
                            ]
                    for t in range(tiles):
                        term = tap * moved[t]
                        totals[t] = term if totals[t] is None else totals[t] + term
                for t in range(tiles):
                    colpass[m, t, at] = totals[t]

        def padded_group(m, g):
            out = []
            for t in range(tiles):
                total = None
                for a in range(taps):
                    tap = row_taps[e, a]
                    if m == 1:
                        tap = tap * tap
                    term = tap * colpass[m, t, pl.ds(g * SUBLANES + lead - radius + a, SUBLANES)]
                    total = term if total is None else total + term
                if g * SUBLANES >= rows:
                    total = jnp.where(has_below, total, 0.0)
                out.append(pltpu.roll(total, SHIFT, 1))
            out = [zero] + out + [zero]
            return [jnp.where(lane < SHIFT, out[t], out[t + 1]) for t in range(tiles + 1)]

        for g in range(third // SUBLANES):
            parts = [padded_group(m, g + h * (third // SUBLANES)) for m in (0, 1) for h in (0, 1)]
            for t in range(tiles):
                for q, part in enumerate(parts):
                    at = (q // 2) * exposures * reach + e * reach + (q % 2) * third + g * SUBLANES
                    maps[t, pl.ds(pl.multiple_of(at, SUBLANES), SUBLANES)] = part[t]
                packed = parts[0][t + 1]
                for q in range(1, 4):
                    packed = jnp.where(lane < 2 * SHIFT * q, packed, pltpu.roll(parts[q][t + 1], 2 * SHIFT * q, 1))
                at = e * third + g * SUBLANES
                edges[t, pl.ds(pl.multiple_of(at, SUBLANES), SUBLANES)] = packed
        return carry

    lax.fori_loop(0, exposures, one_exposure, 0)
    main = 2 * exposures * reach
    edge = exposures * third
    for step in range(chunks):
        to = partner(own, step, chunks)
        sends[step][0:main] = maps[to].astype(jnp.bfloat16)
        sends[step][main : main + edge] = edges[to].astype(jnp.bfloat16)
        sends[step][main + edge : main + edge + exposures] = params[...].astype(jnp.bfloat16)


def stack_kernel(groups, chunks, exposures, rows, vels, share, info, *rest):
    blocks = rest[:groups]
    outs = rest[groups : groups + chunks]
    main, side, windows, edge, whole_params, scalars, order, result, sem = rest[groups + chunks :]
    reach = rows + SHIFT
    third = reach // 2
    own = info[0]
    first_vel = info[1]
    main_rows = 2 * exposures * reach
    edge_rows = exposures * third
    for g in range(groups):
        whole_params[g * exposures : (g + 1) * exposures] = (
            blocks[g][main_rows + edge_rows : main_rows + edge_rows + exposures].astype(jnp.float32).astype(jnp.int32)
        )
    fetch = pltpu.make_async_copy(whole_params, scalars, sem)
    fetch.start()
    for g in range(groups):
        edge[g] = blocks[g][main_rows : main_rows + edge_rows].astype(jnp.float32)
    fetch.wait()
    filled = jnp.int32(0)
    for g in range(groups):

        def unpack(e, at, g=g):
            order[at] = g * exposures + e
            for m in (0, 1):
                start = pl.multiple_of(m * exposures * reach + e * reach, reach)
                main[at, m] = blocks[g][pl.ds(start, reach)].astype(jnp.float32)
            packed = edge[g, pl.ds(pl.multiple_of(e * third, SUBLANES), third)]
            for q in range(4):
                piece = packed if q == 0 else pltpu.roll(packed, LANES - 2 * SHIFT * q, 1)
                side[at, q // 2, (q % 2) * third : (q % 2 + 1) * third] = piece
            return at + scalars[g * exposures + e, 2 * vels]

        filled = lax.fori_loop(0, exposures, unpack, filled, unroll=4)
    for i in range(UNROLL):
        order[filled + i] = 0
        main[filled + i] = jnp.zeros(main.shape[1:], jnp.float32)
        side[filled + i] = jnp.zeros(side.shape[1:], jnp.float32)
    trips = (filled + UNROLL - 1) // UNROLL

    lane = lax.broadcasted_iota(jnp.int32, (rows, LANES), 1)
    zeros = jnp.zeros((rows, LANES), jnp.float32)

    def one_velocity(v, carry):
        def gather(trip, sums):
            for i in range(UNROLL):
                e = trip * UNROLL + i
                source = order[e]
                row_at = scalars[source, first_vel + v]
                col_at = scalars[source, vels + first_vel + v] + SHIFT
                turn = lax.rem(LANES - col_at, LANES)
                from_side = lane < col_at
                cells = jnp.concatenate(
                    [
                        jnp.where(from_side, side[e, m, pl.ds(row_at, rows)], main[e, m, pl.ds(row_at, rows)])
                        for m in (0, 1)
                    ]
                ).astype(jnp.bfloat16)
                cells = pltpu.roll(cells, turn, 1).astype(jnp.float32)
                out = []
                for m in (0, 1):
                    windows[e, m] = cells[m * rows : (m + 1) * rows]
                    out.append(sums[m] + cells[m * rows : (m + 1) * rows])
                sums = tuple(out)
            return sums

        signal_sum, depth_sum = lax.fori_loop(0, trips, gather, (zeros, zeros))
        flux = signal_sum / (depth_sum + 1.0)

        def reweigh(trip, sums):
            for i in range(UNROLL):
                e = trip * UNROLL + i
                signal = windows[e, 0]
                depth = windows[e, 1]
                residual = signal - flux * depth
                base = depth + 1.0
                weight = base / (base + residual * residual)
                sums = sums[0] + weight * signal, sums[1] + weight * depth
            return sums

        robust = lax.fori_loop(0, trips, reweigh, (zeros, zeros))
        result[v] = robust[0] / jnp.sqrt(robust[1] + 1.0)
        return carry

    lax.fori_loop(0, share, one_velocity, 0)
    block = rows // chunks
    for step in range(chunks):
        to = partner(own, step, chunks)
        outs[step][...] = result[:, pl.ds(pl.multiple_of(to * block, block), block)]


def columns_kernel(chunks, subs, info, *rest):
    pieces = rest[:chunks]
    outs = rest[chunks : chunks + subs]
    held, wide = rest[chunks + subs :]
    own_chunk, own_sub = info[0], info[1]
    for step in range(chunks):
        held[step] = pieces[step][...]
    rows = wide.shape[2]
    for c in range(chunks):
        piece = held[partner(own_chunk, c, chunks)]
        for k in range(subs):
            wide[k, :, :, c * LANES : (c + 1) * LANES] = piece[:, k * rows : (k + 1) * rows]
    for step in range(subs):
        outs[step][...] = wide[partner(own_sub, step, subs)]


def velocities_kernel(subs, info, *rest):
    pieces = rest[:subs]
    out, held = rest[subs:]
    own_sub = info[1]
    for step in range(subs):
        held[step] = pieces[step][...]
    share = held.shape[1]
    for k in range(subs):
        out[k * share : (k + 1) * share] = held[partner(own_sub, k, subs)]


def per_device(science, inv_var, psf_rows, psf_cols, row_shift, col_shift, exposure_ok):
    exposures, rows, columns = science.shape
    vels = row_shift.shape[1]
    radius = psf_rows.shape[1] // 2
    strips = lax.axis_size("strip")
    members = lax.axis_size("expo")
    chunks = columns // LANES
    subs = members // chunks
    share = vels // subs
    reach = rows + SHIFT
    halo = -(-(radius + SHIFT) // SUBLANES) * SUBLANES
    strip = lax.axis_index("strip")
    me = lax.axis_index("expo")
    own_chunk = me // subs
    own_sub = me % subs

    head = jnp.stack([science[:, :halo], inv_var[:, :halo]])
    tail = jnp.stack([science[:, rows - halo :], inv_var[:, rows - halo :]])
    if strips == 2:
        met = lax.ppermute(jnp.where(strip == 0, tail, head), "strip", [(0, 1), (1, 0)])
        above = below = met
    else:
        above = lax.ppermute(tail, "strip", [(i, i + 1) for i in range(strips - 1)])
        below = lax.ppermute(head, "strip", [(i + 1, i) for i in range(strips - 1)])
    info = jnp.stack([strip > 0, strip < strips - 1, own_chunk]).astype(jnp.int32)

    main_rows = 2 * exposures * reach
    edge_rows = exposures * reach // 2
    sent_rows = main_rows + edge_rows + exposures
    span = rows + halo + SUBLANES
    sent = jax.ShapeDtypeStruct((sent_rows, LANES), jnp.bfloat16)
    sends = pl.pallas_call(
        functools.partial(filter_kernel, radius, chunks),
        out_shape=[sent] * chunks,
        in_specs=[SMEM] * 3 + [VMEM] * 7,
        out_specs=[VMEM] * chunks,
        scratch_shapes=[
            pltpu.VMEM((2, span, columns), jnp.float32),
            pltpu.VMEM((2, chunks, span, LANES), jnp.float32),
            pltpu.VMEM((chunks, main_rows, LANES), jnp.float32),
            pltpu.VMEM((chunks, edge_rows, LANES), jnp.float32),
            pltpu.VMEM((exposures, LANES), jnp.float32),
        ],
        compiler_params=pltpu.CompilerParams(vmem_limit_bytes=16 << 20),
        name="filter_maps",
    )(info, psf_rows, psf_cols, row_shift, col_shift, exposure_ok[:, None], science, inv_var, above, below)

    blocks = [sends[0]]
    for step in range(1, chunks):
        blocks.append(lax.ppermute(sends[step], "expo", chunk_pairs(step, chunks, subs)))
    for step in range(1, subs):
        pairs = sub_pairs(step, chunks, subs)
        blocks += [lax.ppermute(block, "expo", pairs) for block in blocks[:chunks]]

    groups = len(blocks)
    block_rows = rows // chunks
    piece = jax.ShapeDtypeStruct((share, block_rows, LANES), jnp.float32)
    where = jnp.stack([own_chunk, own_sub * share]).astype(jnp.int32)
    total = groups * exposures
    pieces = pl.pallas_call(
        functools.partial(stack_kernel, groups, chunks, exposures, rows, vels, share),
        out_shape=[piece] * chunks,
        in_specs=[SMEM] + [VMEM] * groups,
        out_specs=[VMEM] * chunks,
        scratch_shapes=[
            pltpu.VMEM((total + UNROLL, 2, reach, LANES), jnp.float32),
            pltpu.VMEM((total + UNROLL, 2, reach, LANES), jnp.float32),
            pltpu.VMEM((total + UNROLL, 2, rows, LANES), jnp.float32),
            pltpu.VMEM((groups, edge_rows, LANES), jnp.float32),
            pltpu.VMEM((total, LANES), jnp.int32),
            pltpu.SMEM((total, LANES), jnp.int32),
            pltpu.SMEM((total + UNROLL,), jnp.int32),
            pltpu.VMEM((share, rows, LANES), jnp.float32),
            pltpu.SemaphoreType.DMA(()),
        ],
        compiler_params=pltpu.CompilerParams(vmem_limit_bytes=24 << 20),
        name="stack_twice",
    )(where, *blocks)

    held = [pieces[0]]
    for step in range(1, chunks):
        held.append(lax.ppermute(pieces[step], "expo", chunk_pairs(step, chunks, subs)))
    place = jnp.stack([own_chunk, own_sub]).astype(jnp.int32)
    out_rows = block_rows // subs
    wide = jax.ShapeDtypeStruct((share, out_rows, columns), jnp.float32)
    parts = pl.pallas_call(
        functools.partial(columns_kernel, chunks, subs),
        out_shape=[wide] * subs,
        in_specs=[SMEM] + [VMEM] * chunks,
        out_specs=[VMEM] * subs,
        scratch_shapes=[
            pltpu.VMEM((chunks, share, block_rows, LANES), jnp.float32),
            pltpu.VMEM((subs, share, out_rows, columns), jnp.float32),
        ],
        compiler_params=pltpu.CompilerParams(vmem_limit_bytes=1 << 20),
        name="join_columns",
    )(place, *held)
    met = [parts[0]]
    for step in range(1, subs):
        met.append(lax.ppermute(parts[step], "expo", sub_pairs(step, chunks, subs)))
    likelihood = pl.pallas_call(
        functools.partial(velocities_kernel, subs),
        out_shape=jax.ShapeDtypeStruct((vels, out_rows, columns), jnp.float32),
        in_specs=[SMEM] + [VMEM] * subs,
        out_specs=VMEM,
        scratch_shapes=[pltpu.VMEM((subs, share, out_rows, columns), jnp.float32)],
        compiler_params=pltpu.CompilerParams(vmem_limit_bytes=1 << 20),
        name="join_velocities",
    )(place, *met)
    return likelihood[None]


def solution(mesh):
    in_specs = (
        P(("field", "expo"), "strip", None),
        P(("field", "expo"), "strip", None),
        P(("field", "expo"), None),
        P(("field", "expo"), None),
        P(("field", "expo"), None),
        P(("field", "expo"), None),
        P(("field", "expo")),
    )
    out_specs = P("strip", "field", "expo", None)
    return jax.shard_map(
        per_device, mesh=mesh, in_specs=in_specs, out_specs=out_specs, check_vma=False
    )
```

```python
import functools

import jax
import jax.numpy as jnp
from jax import lax
from jax.experimental import pallas as pl
from jax.experimental.pallas import tpu as pltpu
from jax.sharding import PartitionSpec as P

SHIFT = 16
LANES = 128
SUBLANES = 8
UNROLL = 8

SMEM = pl.BlockSpec(memory_space=pltpu.SMEM)
VMEM = pl.BlockSpec(memory_space=pltpu.VMEM)


def partner(index, step, count):
    if count & (count - 1) == 0:
        return index ^ step
    return (index + step) % count


def chunk_pairs(step, chunks, subs):
    return [
        (j * subs + k, partner(j, step, chunks) * subs + k) for j in range(chunks) for k in range(subs)
    ]


def sub_pairs(step, chunks, subs):
    return [
        (j * subs + k, j * subs + partner(k, step, subs)) for j in range(chunks) for k in range(subs)
    ]


def column_pass(picture, col_taps, e, square):
    tiles = picture.shape[1] // LANES
    taps = col_taps.shape[1]
    lane = lax.broadcasted_iota(jnp.int32, (SUBLANES, LANES), 1)
    zero = jnp.zeros((SUBLANES, LANES), jnp.float32)
    cut = [picture[:, t * LANES : (t + 1) * LANES] for t in range(tiles)]
    totals = None
    for b in range(taps):
        step = b - taps // 2
        tap = col_taps[e, b]
        if square:
            tap = tap * tap
        moved = cut
        if step:
            turned = [pltpu.roll(c, (-step) % LANES, 1) for c in cut]
            if step > 0:
                turned = turned + [zero]
                moved = [jnp.where(lane < LANES - step, turned[t], turned[t + 1]) for t in range(tiles)]
            else:
                turned = [zero] + turned
                moved = [jnp.where(lane >= -step, turned[t + 1], turned[t]) for t in range(tiles)]
        terms = [tap * m for m in moved]
        totals = terms if totals is None else [x + y for x, y in zip(totals, terms)]
    return totals


def row_pass(colpass, row_taps, e, m, first, taps):
    tiles = colpass.shape[1]
    lane = lax.broadcasted_iota(jnp.int32, (SUBLANES, LANES), 1)
    zero = jnp.zeros((SUBLANES, LANES), jnp.float32)
    out = []
    for t in range(tiles):
        total = None
        for a in taps:
            tap = row_taps[e, a]
            if m == 1:
                tap = tap * tap
            term = tap * colpass[m, t, pl.ds(first + a, SUBLANES)]
            total = term if total is None else total + term
        out.append(pltpu.roll(total, SHIFT, 1))
    out = [zero] + out + [zero]
    return [jnp.where(lane < SHIFT, out[t], out[t + 1]) for t in range(tiles + 1)]


def pack_edges(quarters, t):
    lane = lax.broadcasted_iota(jnp.int32, (SUBLANES, LANES), 1)
    packed = jnp.zeros((SUBLANES, LANES), jnp.float32)
    for q, quarter in enumerate(quarters):
        if quarter is None:
            continue
        piece = quarter[t + 1] if q == 0 else pltpu.roll(quarter[t + 1], 2 * SHIFT * q, 1)
        inside = (lane >= 2 * SHIFT * q) & (lane < 2 * SHIFT * (q + 1))
        packed = jnp.where(inside, piece, packed)
    return packed


def inner_kernel(radius, row_taps, col_taps, science, inv_var, maps, edges, colpass):
    exposures, rows, columns = science.shape
    tiles = columns // LANES
    taps = 2 * radius + 1
    pad = SUBLANES
    colpass[:, :, 0:pad] = jnp.zeros((2, tiles, pad, LANES), jnp.float32)
    colpass[:, :, pad + rows : 2 * pad + rows] = jnp.zeros((2, tiles, pad, LANES), jnp.float32)
    parts = rows // SHIFT

    def one_exposure(e, carry):
        inverse_all = inv_var[e].astype(jnp.float32)
        product_all = science[e].astype(jnp.float32) * inverse_all
        for g in range(rows // SUBLANES):
            at = slice(g * SUBLANES, (g + 1) * SUBLANES)
            for m, picture in ((0, product_all[at]), (1, inverse_all[at])):
                for t, total in enumerate(column_pass(picture, col_taps, e, m == 1)):
                    colpass[m, t, pad + g * SUBLANES : pad + (g + 1) * SUBLANES] = total
        for p in range(parts):
            quarters = [
                row_pass(colpass, row_taps, e, m, pad + p * SHIFT + h * SUBLANES - radius, range(taps))
                for m in (0, 1)
                for h in (0, 1)
            ]
            for t in range(tiles):
                for q in range(4):
                    at = p * exposures * 2 * SHIFT + e * 2 * SHIFT + q * SUBLANES
                    maps[t, pl.ds(pl.multiple_of(at, SUBLANES), SUBLANES)] = quarters[q][t]
                at = p * exposures * SUBLANES + e * SUBLANES
                edges[t, pl.ds(pl.multiple_of(at, SUBLANES), SUBLANES)] = pack_edges(quarters, t)
        return carry

    lax.fori_loop(0, exposures, one_exposure, 0)


def outer_kernel(
    radius, chunks, info, row_taps, col_taps, usable, row_shift, col_shift, maps, edges, above, below, *rest
):
    sends, (pixels, colpass, more, more_edges, params) = rest[:chunks], rest[chunks:]
    exposures, vels = row_shift.shape
    tiles = maps.shape[0]
    parts = edges.shape[1] // (exposures * SUBLANES)
    taps = 2 * radius + 1
    pad = SUBLANES
    has_above, has_below, own = info[0] > 0, info[1] > 0, info[2]

    row = lax.broadcasted_iota(jnp.int32, (exposures, 1), 0)
    kept = jnp.zeros((exposures, 1), jnp.int32)
    for e in range(exposures):
        kept = jnp.where(row == e, usable[e], kept)
    params[...] = jnp.zeros_like(params)
    params[:, 0:vels] = row_shift[...].astype(jnp.float32)
    params[:, vels : 2 * vels] = col_shift[...].astype(jnp.float32)
    params[:, 2 * vels : 2 * vels + 1] = kept.astype(jnp.float32)
    colpass[...] = jnp.zeros_like(colpass)

    def one_exposure(e, carry):
        for kind in (0, 1):
            pixels[kind, 0:radius] = jnp.where(has_below, below[kind, e].astype(jnp.float32), 0.0)
            pixels[kind, radius : 2 * radius] = jnp.where(has_above, above[kind, e].astype(jnp.float32), 0.0)
        inverse = pixels[1]
        product = pixels[0] * inverse
        for m, picture in ((0, product), (1, inverse)):
            for t, total in enumerate(column_pass(picture, col_taps, e, m == 1)):
                colpass[m, t, pad : pad + SUBLANES] = total
        upper = [row_pass(colpass, row_taps, e, m, pad + radius, range(radius)) for m in (0, 1)]
        lower = [row_pass(colpass, row_taps, e, m, -radius, range(radius + 1, taps)) for m in (0, 1)]
        for t in range(tiles):
            for m in (0, 1):
                more[0, t, 2 * e + m] = upper[m][t]
                more[1, t, 2 * e + m] = lower[m][t]
            more_edges[0, t, e] = pack_edges([upper[0], None, upper[1], None], t)
            more_edges[1, t, e] = pack_edges([None, lower[0], None, lower[1]], t)
        return carry

    lax.fori_loop(0, exposures, one_exposure, 0)
    main = exposures * 2 * SHIFT
    size = main + exposures * SUBLANES
    for step in range(chunks):
        to = partner(own, step, chunks)
        for p in range(parts):
            for k in range(2 * exposures):
                first = maps[to, p * main + k * SHIFT : p * main + k * SHIFT + SUBLANES]
                second = maps[to, p * main + k * SHIFT + SUBLANES : p * main + (k + 1) * SHIFT]
                if p == 0:
                    first = first + more[0, to, k]
                if p == parts - 1:
                    second = second + more[1, to, k]
                at = p * size + k * SHIFT
                sends[step][at : at + SHIFT] = jnp.concatenate([first, second]).astype(jnp.bfloat16)
            packed = edges[to, p * exposures * SUBLANES : (p + 1) * exposures * SUBLANES]
            if p == 0:
                packed = packed + more_edges[0, to].reshape(packed.shape)
            if p == parts - 1:
                packed = packed + more_edges[1, to].reshape(packed.shape)
            sends[step][p * size + main : (p + 1) * size] = packed.astype(jnp.bfloat16)
        sends[step][parts * size : parts * size + exposures] = params[...].astype(jnp.bfloat16)


def stack_kernel(groups, chunks, exposures, rows, vels, info, *rest):
    bodies = rest[:groups]
    tops = rest[groups : 2 * groups]
    outs = rest[2 * groups : 2 * groups + chunks]
    main, side, windows, edge, whole_params, scalars, order, result, sem = rest[2 * groups + chunks :]
    own = info[2]
    first_vel = info[4]
    share = result.shape[0]
    parts = rows // SHIFT
    main_rows = exposures * 2 * SHIFT
    edge_rows = exposures * SUBLANES
    size = main_rows + edge_rows
    for g in range(groups):
        whole_params[g * exposures : (g + 1) * exposures] = (
            bodies[g][parts * size : parts * size + exposures].astype(jnp.float32).astype(jnp.int32)
        )
    fetch = pltpu.make_async_copy(whole_params, scalars, sem)
    fetch.start()
    for g in range(groups):
        for p in range(parts):
            edge[g, p] = bodies[g][p * size + main_rows : (p + 1) * size].astype(jnp.float32)
        edge[g, parts] = tops[g][main_rows:size].astype(jnp.float32)
    fetch.wait()
    filled = jnp.int32(0)
    for g in range(groups):

        def unpack(e, at, g=g):
            order[at] = g * exposures + e
            for p in range(parts + 1):
                source, offset = (bodies[g], p * size) if p < parts else (tops[g], 0)
                start = pl.multiple_of(offset + e * 2 * SHIFT, 2 * SUBLANES)
                both = source[pl.ds(start, 2 * SHIFT)].astype(jnp.float32)
                packed = edge[g, p, pl.ds(pl.multiple_of(e * SUBLANES, SUBLANES), SUBLANES)]
                for m in (0, 1):
                    main[at, m, p * SHIFT : (p + 1) * SHIFT] = both[m * SHIFT : (m + 1) * SHIFT]
                    for h in (0, 1):
                        q = 2 * m + h
                        piece = packed if q == 0 else pltpu.roll(packed, LANES - 2 * SHIFT * q, 1)
                        side[at, m, p * SHIFT + h * SUBLANES : p * SHIFT + (h + 1) * SUBLANES] = piece
            return at + scalars[g * exposures + e, 2 * vels]

        filled = lax.fori_loop(0, exposures, unpack, filled, unroll=4)
    for i in range(UNROLL):
        order[filled + i] = 0
        main[filled + i] = jnp.zeros(main.shape[1:], jnp.float32)
        side[filled + i] = jnp.zeros(side.shape[1:], jnp.float32)
    trips = (filled + UNROLL - 1) // UNROLL

    lane = lax.broadcasted_iota(jnp.int32, (rows, LANES), 1)
    zeros = jnp.zeros((rows, LANES), jnp.float32)

    def one_velocity(v, carry):
        def gather(trip, sums):
            for i in range(UNROLL):
                e = trip * UNROLL + i
                source = order[e]
                row_at = scalars[source, first_vel + v]
                col_at = scalars[source, vels + first_vel + v] + SHIFT
                turn = lax.rem(LANES - col_at, LANES)
                from_side = lane < col_at
                cells = jnp.concatenate(
                    [
                        jnp.where(from_side, side[e, m, pl.ds(row_at, rows)], main[e, m, pl.ds(row_at, rows)])
                        for m in (0, 1)
                    ]
                ).astype(jnp.bfloat16)
                cells = pltpu.roll(cells, turn, 1).astype(jnp.float32)
                out = []
                for m in (0, 1):
                    windows[e, m] = cells[m * rows : (m + 1) * rows]
                    out.append(sums[m] + cells[m * rows : (m + 1) * rows])
                sums = tuple(out)
            return sums

        signal_sum, depth_sum = lax.fori_loop(0, trips, gather, (zeros, zeros))
        flux = signal_sum / (depth_sum + 1.0)

        def reweigh(trip, sums):
            for i in range(UNROLL):
                e = trip * UNROLL + i
                signal = windows[e, 0]
                depth = windows[e, 1]
                residual = signal - flux * depth
                base = depth + 1.0
                weight = base / (base + residual * residual)
                sums = sums[0] + weight * signal, sums[1] + weight * depth
            return sums

        robust = lax.fori_loop(0, trips, reweigh, (zeros, zeros))
        result[v] = robust[0] / jnp.sqrt(robust[1] + 1.0)
        return carry

    lax.fori_loop(0, share, one_velocity, 0)
    block = rows // chunks
    for step in range(chunks):
        to = partner(own, step, chunks)
        outs[step][...] = result[:, pl.ds(pl.multiple_of(to * block, block), block)]


def columns_kernel(chunks, subs, info, *rest):
    pieces = rest[:chunks]
    outs = rest[chunks : chunks + subs]
    held, wide = rest[chunks + subs :]
    own_chunk, own_sub = info[2], info[3]
    for step in range(chunks):
        held[step] = pieces[step][...]
    rows = wide.shape[2]
    for c in range(chunks):
        piece = held[partner(own_chunk, c, chunks)]
        for k in range(subs):
            wide[k, :, :, c * LANES : (c + 1) * LANES] = piece[:, k * rows : (k + 1) * rows]
    for step in range(subs):
        outs[step][...] = wide[partner(own_sub, step, subs)]


def velocities_kernel(subs, info, *rest):
    pieces = rest[:subs]
    out, held = rest[subs:]
    own_sub = info[3]
    for step in range(subs):
        held[step] = pieces[step][...]
    share = held.shape[1]
    for k in range(subs):
        out[k * share : (k + 1) * share] = held[partner(own_sub, k, subs)]


def per_device(science, inv_var, psf_rows, psf_cols, row_shift, col_shift, exposure_ok):
    exposures, rows, columns = science.shape
    vels = row_shift.shape[1]
    radius = psf_rows.shape[1] // 2
    strips = lax.axis_size("strip")
    members = lax.axis_size("expo")
    chunks = columns // LANES
    subs = members // chunks
    share = vels // subs
    parts = rows // SHIFT
    strip = lax.axis_index("strip")
    me = lax.axis_index("expo")
    own_chunk = me // subs
    own_sub = me % subs
    info = jnp.stack([strip > 0, strip < strips - 1, own_chunk, own_sub, own_sub * share]).astype(jnp.int32)

    def rows_from(start):
        return jnp.stack([lax.dynamic_slice_in_dim(x, start, radius, 1) for x in (science, inv_var)])

    if strips == 2:
        met = rows_from(jnp.where(strip == 0, rows - radius, 0))
        above = below = lax.ppermute(met, "strip", [(0, 1), (1, 0)])
    else:
        above = lax.ppermute(rows_from(rows - radius), "strip", [(i, i + 1) for i in range(strips - 1)])
        below = lax.ppermute(rows_from(0), "strip", [(i + 1, i) for i in range(strips - 1)])

    map_rows = parts * exposures * 2 * SHIFT
    edge_rows = parts * exposures * SUBLANES
    maps, edges = pl.pallas_call(
        functools.partial(inner_kernel, radius),
        out_shape=[
            jax.ShapeDtypeStruct((chunks, map_rows, LANES), jnp.float32),
            jax.ShapeDtypeStruct((chunks, edge_rows, LANES), jnp.float32),
        ],
        in_specs=[SMEM] * 2 + [VMEM] * 2,
        out_specs=[VMEM] * 2,
        scratch_shapes=[pltpu.VMEM((2, chunks, rows + 2 * SUBLANES, LANES), jnp.float32)],
        compiler_params=pltpu.CompilerParams(vmem_limit_bytes=8 << 20),
        cost_estimate=pl.CostEstimate(flops=100_000_000, bytes_accessed=4_000_000, transcendentals=0),
        name="filter_inner",
    )(psf_rows, psf_cols, science, inv_var)
    sent = jax.ShapeDtypeStruct((map_rows + edge_rows + exposures, LANES), jnp.bfloat16)
    sends = pl.pallas_call(
        functools.partial(outer_kernel, radius, chunks),
        out_shape=[sent] * chunks,
        in_specs=[SMEM] * 4 + [VMEM] * 6,
        out_specs=[VMEM] * chunks,
        scratch_shapes=[
            pltpu.VMEM((2, 2 * radius, columns), jnp.float32),
            pltpu.VMEM((2, chunks, 3 * SUBLANES, LANES), jnp.float32),
            pltpu.VMEM((2, chunks, 2 * exposures, SUBLANES, LANES), jnp.float32),
            pltpu.VMEM((2, chunks, exposures, SUBLANES, LANES), jnp.float32),
            pltpu.VMEM((exposures, LANES), jnp.float32),
        ],
        compiler_params=pltpu.CompilerParams(vmem_limit_bytes=8 << 20),
        name="filter_outer",
    )(info, psf_rows, psf_cols, exposure_ok, row_shift, col_shift, maps, edges, above, below)

    top_rows = (map_rows + edge_rows) // parts
    bodies, tops = [], []
    for step in range(chunks):
        body = sends[step]
        if step:
            body = lax.ppermute(body, "expo", chunk_pairs(step, chunks, subs))
        bodies.append(body)
        tops.append(lax.ppermute(body[:top_rows], "strip", [(i + 1, i) for i in range(strips - 1)]))
    for step in range(1, subs):
        pairs = sub_pairs(step, chunks, subs)
        bodies += [lax.ppermute(block, "expo", pairs) for block in bodies[:chunks]]
        tops += [lax.ppermute(block, "expo", pairs) for block in tops[:chunks]]

    groups = len(bodies)
    block_rows = rows // chunks
    reach = rows + SHIFT
    piece = jax.ShapeDtypeStruct((share, block_rows, LANES), jnp.float32)
    total = groups * exposures
    pieces = pl.pallas_call(
        functools.partial(stack_kernel, groups, chunks, exposures, rows, vels),
        out_shape=[piece] * chunks,
        in_specs=[SMEM] + [VMEM] * (2 * groups),
        out_specs=[VMEM] * chunks,
        scratch_shapes=[
            pltpu.VMEM((total + UNROLL, 2, reach, LANES), jnp.float32),
            pltpu.VMEM((total + UNROLL, 2, reach, LANES), jnp.float32),
            pltpu.VMEM((total + UNROLL, 2, rows, LANES), jnp.float32),
            pltpu.VMEM((groups, parts + 1, exposures * SUBLANES, LANES), jnp.float32),
            pltpu.VMEM((total, LANES), jnp.int32),
            pltpu.SMEM((total, LANES), jnp.int32),
            pltpu.SMEM((total + UNROLL,), jnp.int32),
            pltpu.VMEM((share, rows, LANES), jnp.float32),
            pltpu.SemaphoreType.DMA(()),
        ],
        compiler_params=pltpu.CompilerParams(vmem_limit_bytes=24 << 20),
        name="stack_twice",
    )(info, *bodies, *tops)

    held = [pieces[0]]
    for step in range(1, chunks):
        held.append(lax.ppermute(pieces[step], "expo", chunk_pairs(step, chunks, subs)))
    out_rows = block_rows // subs
    wide = jax.ShapeDtypeStruct((share, out_rows, columns), jnp.float32)
    parts = pl.pallas_call(
        functools.partial(columns_kernel, chunks, subs),
        out_shape=[wide] * subs,
        in_specs=[SMEM] + [VMEM] * chunks,
        out_specs=[VMEM] * subs,
        scratch_shapes=[
            pltpu.VMEM((chunks, share, block_rows, LANES), jnp.float32),
            pltpu.VMEM((subs, share, out_rows, columns), jnp.float32),
        ],
        compiler_params=pltpu.CompilerParams(vmem_limit_bytes=1 << 20),
        name="join_columns",
    )(info, *held)
    met = [parts[0]]
    for step in range(1, subs):
        met.append(lax.ppermute(parts[step], "expo", sub_pairs(step, chunks, subs)))
    likelihood = pl.pallas_call(
        functools.partial(velocities_kernel, subs),
        out_shape=jax.ShapeDtypeStruct((vels, out_rows, columns), jnp.float32),
        in_specs=[SMEM] + [VMEM] * subs,
        out_specs=VMEM,
        scratch_shapes=[pltpu.VMEM((subs, share, out_rows, columns), jnp.float32)],
        compiler_params=pltpu.CompilerParams(vmem_limit_bytes=1 << 20),
        name="join_velocities",
    )(info, *met)
    return likelihood[None]


def solution(mesh):
    in_specs = (
        P(("field", "expo"), "strip", None),
        P(("field", "expo"), "strip", None),
        P(("field", "expo"), None),
        P(("field", "expo"), None),
        P(("field", "expo"), None),
        P(("field", "expo"), None),
        P(("field", "expo")),
    )
    out_specs = P("strip", "field", "expo", None)
    return jax.shard_map(
        per_device, mesh=mesh, in_specs=in_specs, out_specs=out_specs, check_vma=False
    )
```

```python
import functools

import jax
import jax.numpy as jnp
from jax import lax
from jax.experimental import pallas as pl
from jax.experimental.pallas import tpu as pltpu
from jax.sharding import PartitionSpec as P

SHIFT = 16
LANES = 128
SUBLANES = 8
UNROLL = 8

SMEM = pl.BlockSpec(memory_space=pltpu.SMEM)
VMEM = pl.BlockSpec(memory_space=pltpu.VMEM)


def partner(index, step, count):
    if count & (count - 1) == 0:
        return index ^ step
    return (index + step) % count


def chunk_pairs(step, chunks, subs):
    return [
        (j * subs + k, partner(j, step, chunks) * subs + k) for j in range(chunks) for k in range(subs)
    ]


def sub_pairs(step, chunks, subs):
    return [
        (j * subs + k, j * subs + partner(k, step, subs)) for j in range(chunks) for k in range(subs)
    ]


def column_pass(picture, col_taps, e, square):
    tiles = picture.shape[1] // LANES
    taps = col_taps.shape[1]
    lane = lax.broadcasted_iota(jnp.int32, (SUBLANES, LANES), 1)
    zero = jnp.zeros((SUBLANES, LANES), jnp.float32)
    cut = [picture[:, t * LANES : (t + 1) * LANES] for t in range(tiles)]
    totals = None
    for b in range(taps):
        step = b - taps // 2
        tap = col_taps[e, b]
        if square:
            tap = tap * tap
        moved = cut
        if step:
            turned = [pltpu.roll(c, (-step) % LANES, 1) for c in cut]
            if step > 0:
                turned = turned + [zero]
                moved = [jnp.where(lane < LANES - step, turned[t], turned[t + 1]) for t in range(tiles)]
            else:
                turned = [zero] + turned
                moved = [jnp.where(lane >= -step, turned[t + 1], turned[t]) for t in range(tiles)]
        terms = [tap * m for m in moved]
        totals = terms if totals is None else [x + y for x, y in zip(totals, terms)]
    return totals


def row_pass(colpass, row_taps, e, m, first, taps):
    tiles = colpass.shape[1]
    lane = lax.broadcasted_iota(jnp.int32, (SUBLANES, LANES), 1)
    zero = jnp.zeros((SUBLANES, LANES), jnp.float32)
    out = []
    for t in range(tiles):
        total = None
        for a in taps:
            tap = row_taps[e, a]
            if m == 1:
                tap = tap * tap
            term = tap * colpass[m, t, pl.ds(first + a, SUBLANES)]
            total = term if total is None else total + term
        out.append(pltpu.roll(total, SHIFT, 1))
    out = [zero] + out + [zero]
    return [jnp.where(lane < SHIFT, out[t], out[t + 1]) for t in range(tiles + 1)]


def pack_edges(quarters, t):
    lane = lax.broadcasted_iota(jnp.int32, (SUBLANES, LANES), 1)
    packed = jnp.zeros((SUBLANES, LANES), jnp.float32)
    for q, quarter in enumerate(quarters):
        if quarter is None:
            continue
        piece = quarter[t + 1] if q == 0 else pltpu.roll(quarter[t + 1], 2 * SHIFT * q, 1)
        inside = (lane >= 2 * SHIFT * q) & (lane < 2 * SHIFT * (q + 1))
        packed = jnp.where(inside, piece, packed)
    return packed


def inner_kernel(radius, row_taps, col_taps, science, inv_var, maps, edges, colpass):
    exposures, rows, columns = science.shape
    tiles = columns // LANES
    taps = 2 * radius + 1
    pad = SUBLANES
    colpass[:, :, 0:pad] = jnp.zeros((2, tiles, pad, LANES), jnp.float32)
    colpass[:, :, pad + rows : 2 * pad + rows] = jnp.zeros((2, tiles, pad, LANES), jnp.float32)
    parts = rows // SHIFT

    def one_exposure(e, carry):
        inverse_all = inv_var[e].astype(jnp.float32)
        product_all = science[e].astype(jnp.float32) * inverse_all
        for g in range(rows // SUBLANES):
            at = slice(g * SUBLANES, (g + 1) * SUBLANES)
            for m, picture in ((0, product_all[at]), (1, inverse_all[at])):
                for t, total in enumerate(column_pass(picture, col_taps, e, m == 1)):
                    colpass[m, t, pad + g * SUBLANES : pad + (g + 1) * SUBLANES] = total
        for p in range(parts):
            quarters = [
                row_pass(colpass, row_taps, e, m, pad + p * SHIFT + h * SUBLANES - radius, range(taps))
                for m in (0, 1)
                for h in (0, 1)
            ]
            for t in range(tiles):
                for q in range(4):
                    at = p * exposures * 2 * SHIFT + e * 2 * SHIFT + q * SUBLANES
                    maps[t, pl.ds(pl.multiple_of(at, SUBLANES), SUBLANES)] = quarters[q][t]
                at = p * exposures * SUBLANES + e * SUBLANES
                edges[t, pl.ds(pl.multiple_of(at, SUBLANES), SUBLANES)] = pack_edges(quarters, t)
        return carry

    lax.fori_loop(0, exposures, one_exposure, 0, unroll=2)


def outer_kernel(
    radius, chunks, info, row_taps, col_taps, usable, row_shift, col_shift, maps, edges, above, below, *rest
):
    exposures, vels = row_shift.shape
    tiles = maps.shape[0]
    parts = edges.shape[1] // (exposures * SUBLANES)
    sends, (pixels, colpass, more, more_edges, params) = rest[: chunks * parts], rest[chunks * parts :]
    taps = 2 * radius + 1
    pad = SUBLANES
    has_above, has_below, own = info[0] > 0, info[1] > 0, info[2]

    row = lax.broadcasted_iota(jnp.int32, (exposures, 1), 0)
    kept = jnp.zeros((exposures, 1), jnp.int32)
    for e in range(exposures):
        kept = jnp.where(row == e, usable[e], kept)
    params[...] = jnp.zeros_like(params)
    params[:, 0:vels] = row_shift[...].astype(jnp.float32)
    params[:, vels : 2 * vels] = col_shift[...].astype(jnp.float32)
    params[:, 2 * vels : 2 * vels + 1] = kept.astype(jnp.float32)
    colpass[...] = jnp.zeros_like(colpass)

    def one_exposure(e, carry):
        for kind in (0, 1):
            pixels[kind, 0:radius] = jnp.where(has_below, below[kind, e].astype(jnp.float32), 0.0)
            pixels[kind, radius : 2 * radius] = jnp.where(has_above, above[kind, e].astype(jnp.float32), 0.0)
        inverse = pixels[1]
        product = pixels[0] * inverse
        for m, picture in ((0, product), (1, inverse)):
            for t, total in enumerate(column_pass(picture, col_taps, e, m == 1)):
                colpass[m, t, pad : pad + SUBLANES] = total
        upper = [row_pass(colpass, row_taps, e, m, pad + radius, range(radius)) for m in (0, 1)]
        lower = [row_pass(colpass, row_taps, e, m, -radius, range(radius + 1, taps)) for m in (0, 1)]
        for t in range(tiles):
            for m in (0, 1):
                more[0, t, 2 * e + m] = upper[m][t]
                more[1, t, 2 * e + m] = lower[m][t]
            more_edges[0, t, e] = pack_edges([upper[0], None, upper[1], None], t)
            more_edges[1, t, e] = pack_edges([None, lower[0], None, lower[1]], t)
        return carry

    lax.fori_loop(0, exposures, one_exposure, 0, unroll=4)
    main = exposures * 2 * SHIFT
    for step in range(chunks):
        to = partner(own, step, chunks)
        for p in range(parts):
            out = sends[step * parts + p]
            for k in range(2 * exposures):
                first = maps[to, p * main + k * SHIFT : p * main + k * SHIFT + SUBLANES]
                second = maps[to, p * main + k * SHIFT + SUBLANES : p * main + (k + 1) * SHIFT]
                if p == 0:
                    first = first + more[0, to, k]
                if p == parts - 1:
                    second = second + more[1, to, k]
                out[k * SHIFT : (k + 1) * SHIFT] = jnp.concatenate([first, second]).astype(jnp.bfloat16)
            packed = edges[to, p * exposures * SUBLANES : (p + 1) * exposures * SUBLANES]
            if p == 0:
                packed = packed + more_edges[0, to].reshape(packed.shape)
            if p == parts - 1:
                packed = packed + more_edges[1, to].reshape(packed.shape)
            out[main : main + exposures * SUBLANES] = packed.astype(jnp.bfloat16)
            if p == parts - 1:
                tail = main + exposures * SUBLANES
                out[tail : tail + exposures] = params[...].astype(jnp.bfloat16)


def stack_kernel(groups, chunks, exposures, rows, vels, info, *rest):
    parts = rows // SHIFT
    blocks = [rest[p * groups : (p + 1) * groups] for p in range(parts + 1)]
    rest = rest[(parts + 1) * groups :]
    outs = rest[:chunks]
    main, side, windows, edge, whole_params, scalars, order, result, sem = rest[chunks:]
    own = info[2]
    first_vel = info[4]
    share = result.shape[0]
    main_rows = exposures * 2 * SHIFT
    size = main_rows + exposures * SUBLANES
    for g in range(groups):
        whole_params[g * exposures : (g + 1) * exposures] = (
            blocks[parts - 1][g][size : size + exposures].astype(jnp.float32).astype(jnp.int32)
        )
    fetch = pltpu.make_async_copy(whole_params, scalars, sem)
    fetch.start()
    for g in range(groups):
        for p in range(parts + 1):
            edge[g, p] = blocks[p][g][main_rows:size].astype(jnp.float32)
    fetch.wait()
    filled = jnp.int32(0)
    for g in range(groups):

        def unpack(e, at, g=g):
            order[at] = g * exposures + e
            for p in range(parts + 1):
                start = pl.multiple_of(e * 2 * SHIFT, 2 * SHIFT)
                both = blocks[p][g][pl.ds(start, 2 * SHIFT)].astype(jnp.float32)
                packed = edge[g, p, pl.ds(pl.multiple_of(e * SUBLANES, SUBLANES), SUBLANES)]
                for m in (0, 1):
                    main[at, m, p * SHIFT : (p + 1) * SHIFT] = both[m * SHIFT : (m + 1) * SHIFT]
                    for h in (0, 1):
                        q = 2 * m + h
                        piece = packed if q == 0 else pltpu.roll(packed, LANES - 2 * SHIFT * q, 1)
                        side[at, m, p * SHIFT + h * SUBLANES : p * SHIFT + (h + 1) * SUBLANES] = piece
            return at + scalars[g * exposures + e, 2 * vels]

        filled = lax.fori_loop(0, exposures, unpack, filled, unroll=4)
    for i in range(UNROLL):
        order[filled + i] = 0
        main[filled + i] = jnp.zeros(main.shape[1:], jnp.float32)
        side[filled + i] = jnp.zeros(side.shape[1:], jnp.float32)
    trips = (filled + UNROLL - 1) // UNROLL

    lane = lax.broadcasted_iota(jnp.int32, (rows, LANES), 1)
    zeros = jnp.zeros((rows, LANES), jnp.float32)

    def one_velocity(v, carry):
        def gather(trip, sums):
            for i in range(UNROLL):
                e = trip * UNROLL + i
                source = order[e]
                row_at = scalars[source, first_vel + v]
                col_at = scalars[source, vels + first_vel + v] + SHIFT
                turn = lax.rem(LANES - col_at, LANES)
                from_side = lane < col_at
                cells = jnp.concatenate(
                    [
                        jnp.where(from_side, side[e, m, pl.ds(row_at, rows)], main[e, m, pl.ds(row_at, rows)])
                        for m in (0, 1)
                    ]
                ).astype(jnp.bfloat16)
                cells = pltpu.roll(cells, turn, 1).astype(jnp.float32)
                out = []
                for m in (0, 1):
                    windows[e, m] = cells[m * rows : (m + 1) * rows]
                    out.append(sums[m] + cells[m * rows : (m + 1) * rows])
                sums = tuple(out)
            return sums

        signal_sum, depth_sum = lax.fori_loop(0, trips, gather, (zeros, zeros))
        flux = signal_sum / (depth_sum + 1.0)

        def reweigh(trip, sums):
            for i in range(UNROLL):
                e = trip * UNROLL + i
                signal = windows[e, 0]
                depth = windows[e, 1]
                residual = signal - flux * depth
                base = depth + 1.0
                weight = base / (base + residual * residual)
                sums = sums[0] + weight * signal, sums[1] + weight * depth
            return sums

        robust = lax.fori_loop(0, trips, reweigh, (zeros, zeros))
        result[v] = robust[0] / jnp.sqrt(robust[1] + 1.0)
        return carry

    lax.fori_loop(0, share, one_velocity, 0)
    block = rows // chunks
    for step in range(chunks):
        to = partner(own, step, chunks)
        outs[step][...] = result[:, pl.ds(pl.multiple_of(to * block, block), block)]


def columns_kernel(chunks, subs, info, *rest):
    pieces = rest[:chunks]
    outs = rest[chunks : chunks + subs]
    held, wide = rest[chunks + subs :]
    own_chunk, own_sub = info[2], info[3]
    for step in range(chunks):
        held[step] = pieces[step][...]
    rows = wide.shape[2]
    for c in range(chunks):
        piece = held[partner(own_chunk, c, chunks)]
        for k in range(subs):
            wide[k, :, :, c * LANES : (c + 1) * LANES] = piece[:, k * rows : (k + 1) * rows]
    for step in range(subs):
        outs[step][...] = wide[partner(own_sub, step, subs)]


def velocities_kernel(subs, info, *rest):
    pieces = rest[:subs]
    out, held = rest[subs:]
    own_sub = info[3]
    for step in range(subs):
        held[step] = pieces[step][...]
    share = held.shape[1]
    for k in range(subs):
        out[k * share : (k + 1) * share] = held[partner(own_sub, k, subs)]


def per_device(science, inv_var, psf_rows, psf_cols, row_shift, col_shift, exposure_ok):
    exposures, rows, columns = science.shape
    vels = row_shift.shape[1]
    radius = psf_rows.shape[1] // 2
    strips = lax.axis_size("strip")
    members = lax.axis_size("expo")
    chunks = columns // LANES
    subs = members // chunks
    share = vels // subs
    parts = rows // SHIFT
    strip = lax.axis_index("strip")
    me = lax.axis_index("expo")
    own_chunk = me // subs
    own_sub = me % subs
    info = jnp.stack([strip > 0, strip < strips - 1, own_chunk, own_sub, own_sub * share]).astype(jnp.int32)

    def rows_from(start):
        return jnp.stack([lax.dynamic_slice_in_dim(x, start, radius, 1) for x in (science, inv_var)])

    if strips == 2:
        met = rows_from(jnp.where(strip == 0, rows - radius, 0))
        above = below = lax.ppermute(met, "strip", [(0, 1), (1, 0)])
    else:
        above = lax.ppermute(rows_from(rows - radius), "strip", [(i, i + 1) for i in range(strips - 1)])
        below = lax.ppermute(rows_from(0), "strip", [(i + 1, i) for i in range(strips - 1)])

    map_rows = parts * exposures * 2 * SHIFT
    edge_rows = parts * exposures * SUBLANES
    maps, edges = pl.pallas_call(
        functools.partial(inner_kernel, radius),
        out_shape=[
            jax.ShapeDtypeStruct((chunks, map_rows, LANES), jnp.float32),
            jax.ShapeDtypeStruct((chunks, edge_rows, LANES), jnp.float32),
        ],
        in_specs=[SMEM] * 2 + [VMEM] * 2,
        out_specs=[VMEM] * 2,
        scratch_shapes=[pltpu.VMEM((2, chunks, rows + 2 * SUBLANES, LANES), jnp.float32)],
        compiler_params=pltpu.CompilerParams(vmem_limit_bytes=8 << 20),
        cost_estimate=pl.CostEstimate(flops=100_000_000, bytes_accessed=4_000_000, transcendentals=0),
        name="filter_inner",
    )(psf_rows, psf_cols, science, inv_var)
    block = exposures * (2 * SHIFT + SUBLANES)
    sent = [
        jax.ShapeDtypeStruct((block + (exposures if p == parts - 1 else 0), LANES), jnp.bfloat16)
        for p in range(parts)
    ]
    sends = pl.pallas_call(
        functools.partial(outer_kernel, radius, chunks),
        out_shape=sent * chunks,
        in_specs=[SMEM] * 4 + [VMEM] * 6,
        out_specs=[VMEM] * (chunks * parts),
        scratch_shapes=[
            pltpu.VMEM((2, 2 * radius, columns), jnp.float32),
            pltpu.VMEM((2, chunks, 3 * SUBLANES, LANES), jnp.float32),
            pltpu.VMEM((2, chunks, 2 * exposures, SUBLANES, LANES), jnp.float32),
            pltpu.VMEM((2, chunks, exposures, SUBLANES, LANES), jnp.float32),
            pltpu.VMEM((exposures, LANES), jnp.float32),
        ],
        compiler_params=pltpu.CompilerParams(vmem_limit_bytes=8 << 20),
        name="filter_outer",
    )(info, psf_rows, psf_cols, exposure_ok, row_shift, col_shift, maps, edges, above, below)

    blocks = [[[None] * chunks for _ in range(subs)] for _ in range(parts + 1)]
    up = [(i + 1, i) for i in range(strips - 1)]
    for step in range(chunks):
        for p in range(parts):
            blocks[p][0][step] = sends[step * parts + p]
            if step:
                blocks[p][0][step] = lax.ppermute(sends[step * parts + p], "expo", chunk_pairs(step, chunks, subs))
        blocks[parts][0][step] = lax.ppermute(blocks[0][0][step], "strip", up)
    for p in range(parts + 1):
        for u in range(1, subs):
            for step in range(chunks):
                blocks[p][u][step] = lax.ppermute(blocks[p][0][step], "expo", sub_pairs(u, chunks, subs))
    blocks = [[block for sub in part for block in sub] for part in blocks]

    groups = len(blocks[0])
    block_rows = rows // chunks
    reach = rows + SHIFT
    piece = jax.ShapeDtypeStruct((share, block_rows, LANES), jnp.float32)
    total = groups * exposures
    pieces = pl.pallas_call(
        functools.partial(stack_kernel, groups, chunks, exposures, rows, vels),
        out_shape=[piece] * chunks,
        in_specs=[SMEM] + [VMEM] * ((parts + 1) * groups),
        out_specs=[VMEM] * chunks,
        scratch_shapes=[
            pltpu.VMEM((total + UNROLL, 2, reach, LANES), jnp.float32),
            pltpu.VMEM((total + UNROLL, 2, reach, LANES), jnp.float32),
            pltpu.VMEM((total + UNROLL, 2, rows, LANES), jnp.float32),
            pltpu.VMEM((groups, parts + 1, exposures * SUBLANES, LANES), jnp.float32),
            pltpu.VMEM((total, LANES), jnp.int32),
            pltpu.SMEM((total, LANES), jnp.int32),
            pltpu.SMEM((total + UNROLL,), jnp.int32),
            pltpu.VMEM((share, rows, LANES), jnp.float32),
            pltpu.SemaphoreType.DMA(()),
        ],
        compiler_params=pltpu.CompilerParams(vmem_limit_bytes=24 << 20),
        name="stack_twice",
    )(info, *[block for part in blocks for block in part])

    held = [pieces[0]]
    for step in range(1, chunks):
        held.append(lax.ppermute(pieces[step], "expo", chunk_pairs(step, chunks, subs)))
    out_rows = block_rows // subs
    wide = jax.ShapeDtypeStruct((share, out_rows, columns), jnp.float32)
    parts = pl.pallas_call(
        functools.partial(columns_kernel, chunks, subs),
        out_shape=[wide] * subs,
        in_specs=[SMEM] + [VMEM] * chunks,
        out_specs=[VMEM] * subs,
        scratch_shapes=[
            pltpu.VMEM((chunks, share, block_rows, LANES), jnp.float32),
            pltpu.VMEM((subs, share, out_rows, columns), jnp.float32),
        ],
        compiler_params=pltpu.CompilerParams(vmem_limit_bytes=1 << 20),
        name="join_columns",
    )(info, *held)
    met = [parts[0]]
    for step in range(1, subs):
        met.append(lax.ppermute(parts[step], "expo", sub_pairs(step, chunks, subs)))
    likelihood = pl.pallas_call(
        functools.partial(velocities_kernel, subs),
        out_shape=jax.ShapeDtypeStruct((vels, out_rows, columns), jnp.float32),
        in_specs=[SMEM] + [VMEM] * subs,
        out_specs=VMEM,
        scratch_shapes=[pltpu.VMEM((subs, share, out_rows, columns), jnp.float32)],
        compiler_params=pltpu.CompilerParams(vmem_limit_bytes=1 << 20),
        name="join_velocities",
    )(info, *met)
    return likelihood[None]


def solution(mesh):
    in_specs = (
        P(("field", "expo"), "strip", None),
        P(("field", "expo"), "strip", None),
        P(("field", "expo"), None),
        P(("field", "expo"), None),
        P(("field", "expo"), None),
        P(("field", "expo"), None),
        P(("field", "expo")),
    )
    out_specs = P("strip", "field", "expo", None)

    return jax.shard_map(per_device, mesh=mesh, in_specs=in_specs, out_specs=out_specs, check_vma=False)
```

```python
import functools

import jax
import jax.numpy as jnp
from jax import lax
from jax.experimental import pallas as pl
from jax.experimental.pallas import tpu as pltpu
from jax.sharding import PartitionSpec as P

SHIFT = 16
LANES = 128
SUBLANES = 8
UNROLL = 4

SMEM = pl.BlockSpec(memory_space=pltpu.SMEM)
VMEM = pl.BlockSpec(memory_space=pltpu.VMEM)


def partner(index, step, count):
    if count & (count - 1) == 0:
        return index ^ step
    return (index + step) % count


def chunk_pairs(step, chunks, subs):
    return [
        (j * subs + k, partner(j, step, chunks) * subs + k) for j in range(chunks) for k in range(subs)
    ]


def sub_pairs(step, chunks, subs):
    return [
        (j * subs + k, j * subs + partner(k, step, subs)) for j in range(chunks) for k in range(subs)
    ]


def column_pass(picture, col_taps, e, square):
    tiles = picture.shape[1] // LANES
    taps = col_taps.shape[1]
    lane = lax.broadcasted_iota(jnp.int32, (SUBLANES, LANES), 1)
    zero = jnp.zeros((SUBLANES, LANES), jnp.float32)
    cut = [picture[:, t * LANES : (t + 1) * LANES] for t in range(tiles)]
    totals = None
    for b in range(taps):
        step = b - taps // 2
        tap = col_taps[e, b]
        if square:
            tap = tap * tap
        moved = cut
        if step:
            turned = [pltpu.roll(c, (-step) % LANES, 1) for c in cut]
            if step > 0:
                turned = turned + [zero]
                moved = [jnp.where(lane < LANES - step, turned[t], turned[t + 1]) for t in range(tiles)]
            else:
                turned = [zero] + turned
                moved = [jnp.where(lane >= -step, turned[t + 1], turned[t]) for t in range(tiles)]
        terms = [tap * m for m in moved]
        totals = terms if totals is None else [x + y for x, y in zip(totals, terms)]
    return totals


def row_pass(colpass, row_taps, e, m, first, taps):
    tiles = colpass.shape[1]
    lane = lax.broadcasted_iota(jnp.int32, (SUBLANES, LANES), 1)
    zero = jnp.zeros((SUBLANES, LANES), jnp.float32)
    out = []
    for t in range(tiles):
        total = None
        for a in taps:
            tap = row_taps[e, a]
            if m == 1:
                tap = tap * tap
            term = tap * colpass[m, t, pl.ds(first + a, SUBLANES)]
            total = term if total is None else total + term
        out.append(pltpu.roll(total, SHIFT, 1))
    out = [zero] + out + [zero]
    return [jnp.where(lane < SHIFT, out[t], out[t + 1]) for t in range(tiles + 1)]


def pack_edges(quarters, t):
    lane = lax.broadcasted_iota(jnp.int32, (SUBLANES, LANES), 1)
    packed = jnp.zeros((SUBLANES, LANES), jnp.float32)
    for q, quarter in enumerate(quarters):
        if quarter is None:
            continue
        piece = quarter[t + 1] if q == 0 else pltpu.roll(quarter[t + 1], 2 * SHIFT * q, 1)
        inside = (lane >= 2 * SHIFT * q) & (lane < 2 * SHIFT * (q + 1))
        packed = jnp.where(inside, piece, packed)
    return packed


def inner_kernel(radius, row_taps, col_taps, science, inv_var, maps, edges, colpass):
    exposures, rows, columns = science.shape
    tiles = columns // LANES
    taps = 2 * radius + 1
    pad = SUBLANES
    colpass[:, :, 0:pad] = jnp.zeros((2, tiles, pad, LANES), jnp.float32)
    colpass[:, :, pad + rows : 2 * pad + rows] = jnp.zeros((2, tiles, pad, LANES), jnp.float32)
    parts = rows // SHIFT

    def one_exposure(e, carry):
        inverse_all = inv_var[e].astype(jnp.float32)
        product_all = science[e].astype(jnp.float32) * inverse_all
        for g in range(rows // SUBLANES):
            at = slice(g * SUBLANES, (g + 1) * SUBLANES)
            for m, picture in ((0, product_all[at]), (1, inverse_all[at])):
                for t, total in enumerate(column_pass(picture, col_taps, e, m == 1)):
                    colpass[m, t, pad + g * SUBLANES : pad + (g + 1) * SUBLANES] = total
        for p in range(parts):
            quarters = [
                row_pass(colpass, row_taps, e, m, pad + p * SHIFT + h * SUBLANES - radius, range(taps))
                for m in (0, 1)
                for h in (0, 1)
            ]
            for t in range(tiles):
                for q in range(4):
                    at = p * exposures * 2 * SHIFT + e * 2 * SHIFT + q * SUBLANES
                    maps[t, pl.ds(pl.multiple_of(at, SUBLANES), SUBLANES)] = quarters[q][t]
                at = p * exposures * SUBLANES + e * SUBLANES
                edges[t, pl.ds(pl.multiple_of(at, SUBLANES), SUBLANES)] = pack_edges(quarters, t)
        return carry

    lax.fori_loop(0, exposures, one_exposure, 0, unroll=2)


def outer_kernel(
    radius, chunks, info, row_taps, col_taps, usable, row_shift, col_shift, maps, edges, above, below, *rest
):
    exposures, vels = row_shift.shape
    tiles = maps.shape[0]
    parts = edges.shape[1] // (exposures * SUBLANES)
    sends, (pixels, colpass, more, more_edges, params) = rest[: chunks * parts], rest[chunks * parts :]
    taps = 2 * radius + 1
    pad = SUBLANES
    has_above, has_below, own = info[0] > 0, info[1] > 0, info[2]

    row = lax.broadcasted_iota(jnp.int32, (exposures, 1), 0)
    kept = jnp.zeros((exposures, 1), jnp.int32)
    for e in range(exposures):
        kept = jnp.where(row == e, usable[e], kept)
    params[...] = jnp.zeros_like(params)
    params[:, 0:vels] = row_shift[...].astype(jnp.float32)
    params[:, vels : 2 * vels] = col_shift[...].astype(jnp.float32)
    params[:, 2 * vels : 2 * vels + 1] = kept.astype(jnp.float32)
    colpass[...] = jnp.zeros_like(colpass)

    def one_exposure(e, carry):
        for kind in (0, 1):
            pixels[kind, 0:radius] = jnp.where(has_below, below[kind, e].astype(jnp.float32), 0.0)
            pixels[kind, radius : 2 * radius] = jnp.where(has_above, above[kind, e].astype(jnp.float32), 0.0)
        inverse = pixels[1]
        product = pixels[0] * inverse
        for m, picture in ((0, product), (1, inverse)):
            for t, total in enumerate(column_pass(picture, col_taps, e, m == 1)):
                colpass[m, t, pad : pad + SUBLANES] = total
        upper = [row_pass(colpass, row_taps, e, m, pad + radius, range(radius)) for m in (0, 1)]
        lower = [row_pass(colpass, row_taps, e, m, -radius, range(radius + 1, taps)) for m in (0, 1)]
        for t in range(tiles):
            for m in (0, 1):
                more[0, t, 2 * e + m] = upper[m][t]
                more[1, t, 2 * e + m] = lower[m][t]
            more_edges[0, t, e] = pack_edges([upper[0], None, upper[1], None], t)
            more_edges[1, t, e] = pack_edges([None, lower[0], None, lower[1]], t)
        return carry

    lax.fori_loop(0, exposures, one_exposure, 0, unroll=4)
    main = exposures * 2 * SHIFT
    for step in range(chunks):
        to = partner(own, step, chunks)
        for p in range(parts):
            out = sends[step * parts + p]
            for k in range(2 * exposures):
                first = maps[to, p * main + k * SHIFT : p * main + k * SHIFT + SUBLANES]
                second = maps[to, p * main + k * SHIFT + SUBLANES : p * main + (k + 1) * SHIFT]
                if p == 0:
                    first = first + more[0, to, k]
                if p == parts - 1:
                    second = second + more[1, to, k]
                out[k * SHIFT : (k + 1) * SHIFT] = jnp.concatenate([first, second]).astype(jnp.bfloat16)
            packed = edges[to, p * exposures * SUBLANES : (p + 1) * exposures * SUBLANES]
            if p == 0:
                packed = packed + more_edges[0, to].reshape(packed.shape)
            if p == parts - 1:
                packed = packed + more_edges[1, to].reshape(packed.shape)
            out[main : main + exposures * SUBLANES] = packed.astype(jnp.bfloat16)
            if p == parts - 1:
                tail = main + exposures * SUBLANES
                out[tail : tail + exposures] = params[...].astype(jnp.bfloat16)


def stack_kernel(groups, chunks, exposures, rows, vels, info, *rest):
    parts = rows // SHIFT
    blocks = [rest[p * groups : (p + 1) * groups] for p in range(parts + 1)]
    rest = rest[(parts + 1) * groups :]
    outs = rest[:chunks]
    main, side, even, odd, edge, whole_params, scalars, order, result, sem = rest[chunks:]
    windows = (even, odd)
    own = info[2]
    first_vel = info[4]
    share = result.shape[0]
    main_rows = exposures * 2 * SHIFT
    size = main_rows + exposures * SUBLANES
    for g in range(groups):
        whole_params[g * exposures : (g + 1) * exposures] = (
            blocks[parts - 1][g][size : size + exposures].astype(jnp.float32).astype(jnp.int32)
        )
    fetch = pltpu.make_async_copy(whole_params, scalars, sem)
    fetch.start()
    for g in range(groups):
        for p in range(parts + 1):
            edge[g, p] = blocks[p][g][main_rows:size].astype(jnp.float32)
    fetch.wait()
    has_below = info[1].astype(jnp.float32)
    filled = jnp.int32(0)
    for g in range(groups):

        def unpack(e, at, g=g):
            source = g * exposures + e
            order[at] = source
            for p in range(parts + 1):
                start = pl.multiple_of(e * 2 * SHIFT, 2 * SHIFT)
                both = blocks[p][g][pl.ds(start, 2 * SHIFT)].astype(jnp.float32)
                packed = edge[g, p, pl.ds(pl.multiple_of(e * SUBLANES, SUBLANES), SUBLANES)]
                if p == parts:
                    both = both * has_below
                    packed = packed * has_below
                for m in (0, 1):
                    main[at, m, p * SHIFT : (p + 1) * SHIFT] = both[m * SHIFT : (m + 1) * SHIFT]
                    for h in (0, 1):
                        q = 2 * m + h
                        piece = packed if q == 0 else pltpu.roll(packed, LANES - 2 * SHIFT * q, 1)
                        side[at, m, p * SHIFT + h * SUBLANES : p * SHIFT + (h + 1) * SUBLANES] = piece
            return at + scalars[source, 2 * vels]

        filled = lax.fori_loop(0, exposures, unpack, filled, unroll=4)
    for i in range(UNROLL):
        order[filled + i] = 0
        main[filled + i] = jnp.zeros(main.shape[1:], jnp.float32)
        side[filled + i] = jnp.zeros(side.shape[1:], jnp.float32)
    trips = (filled + UNROLL - 1) // UNROLL

    lane = lax.broadcasted_iota(jnp.int32, (rows, LANES), 1)

    def gather(v, e, sums):
        source = order[e]
        row_at = scalars[source, first_vel + v]
        col_at = scalars[source, vels + first_vel + v] + SHIFT
        from_side = lane < col_at
        cells = jnp.concatenate(
            [
                jnp.where(from_side, side[e, m, pl.ds(row_at, rows)], main[e, m, pl.ds(row_at, rows)])
                for m in (0, 1)
            ]
        ).astype(jnp.bfloat16)
        cells = pltpu.roll(cells, (LANES - col_at) & (LANES - 1), 1).astype(jnp.float32)
        windows[v % 2][e, 0] = cells[:rows]
        windows[v % 2][e, 1] = cells[rows:]
        return sums[0] + cells[:rows], sums[1] + cells[rows:]

    def reweigh(v, e, flux, sums):
        signal = windows[v % 2][e, 0]
        depth = windows[v % 2][e, 1]
        residual = signal - flux * depth
        base = depth + 1.0
        weight = base / (base + residual * residual)
        return sums[0] + weight * signal, sums[1] + weight * depth

    def over_exposures(step, start):
        def trip(t, sums):
            for i in range(UNROLL):
                sums = step(t * UNROLL + i, sums)
            return sums

        return lax.fori_loop(0, trips, trip, start)

    zeros = main[filled, 0, 0:rows]
    none = (zeros, zeros)

    sums = over_exposures(functools.partial(gather, 0), none)
    for v in range(share):
        flux = sums[0] / (sums[1] + 1.0)

        def weigh(e, sums, v=v, flux=flux):
            return reweigh(v, e, flux, sums)

        def both(e, sums, v=v, weigh=weigh):
            return gather(v + 1, e, sums[:2]) + weigh(e, sums[2:])

        if v + 1 < share:
            sums = over_exposures(both, none + none)
        else:
            sums = none + over_exposures(weigh, none)
        result[v] = sums[2] / jnp.sqrt(sums[3] + 1.0)
    block = rows // chunks
    for step in range(chunks):
        to = partner(own, step, chunks)
        outs[step][...] = result[:, pl.ds(pl.multiple_of(to * block, block), block)]


def columns_kernel(chunks, subs, info, *rest):
    pieces = rest[:chunks]
    outs = rest[chunks : chunks + subs]
    held, wide = rest[chunks + subs :]
    own_chunk, own_sub = info[2], info[3]
    for step in range(chunks):
        held[step] = pieces[step][...]
    rows = wide.shape[2]
    for c in range(chunks):
        piece = held[partner(own_chunk, c, chunks)]
        for k in range(subs):
            wide[k, :, :, c * LANES : (c + 1) * LANES] = piece[:, k * rows : (k + 1) * rows]
    for step in range(subs):
        outs[step][...] = wide[partner(own_sub, step, subs)]


def velocities_kernel(subs, info, *rest):
    pieces = rest[:subs]
    out, held = rest[subs:]
    own_sub = info[3]
    for step in range(subs):
        held[step] = pieces[step][...]
    share = held.shape[1]
    for k in range(subs):
        out[k * share : (k + 1) * share] = held[partner(own_sub, k, subs)]


def per_device(science, inv_var, psf_rows, psf_cols, row_shift, col_shift, exposure_ok):
    exposures, rows, columns = science.shape
    vels = row_shift.shape[1]
    radius = psf_rows.shape[1] // 2
    strips = lax.axis_size("strip")
    members = lax.axis_size("expo")
    chunks = columns // LANES
    subs = members // chunks
    share = vels // subs
    parts = rows // SHIFT
    strip = lax.axis_index("strip")
    me = lax.axis_index("expo")
    own_chunk = me // subs
    own_sub = me % subs
    info = jnp.stack([strip > 0, strip < strips - 1, own_chunk, own_sub, own_sub * share]).astype(jnp.int32)

    def rows_from(start):
        return jnp.stack([lax.dynamic_slice_in_dim(x, start, radius, 1) for x in (science, inv_var)])

    if strips == 2:
        met = rows_from(jnp.where(strip == 0, rows - radius, 0))
        above = below = lax.ppermute(met, "strip", [(0, 1), (1, 0)])
    else:
        above = lax.ppermute(rows_from(rows - radius), "strip", [(i, i + 1) for i in range(strips - 1)])
        below = lax.ppermute(rows_from(0), "strip", [(i + 1, i) for i in range(strips - 1)])

    map_rows = parts * exposures * 2 * SHIFT
    edge_rows = parts * exposures * SUBLANES
    maps, edges = pl.pallas_call(
        functools.partial(inner_kernel, radius),
        out_shape=[
            jax.ShapeDtypeStruct((chunks, map_rows, LANES), jnp.float32),
            jax.ShapeDtypeStruct((chunks, edge_rows, LANES), jnp.float32),
        ],
        in_specs=[SMEM] * 2 + [VMEM] * 2,
        out_specs=[VMEM] * 2,
        scratch_shapes=[pltpu.VMEM((2, chunks, rows + 2 * SUBLANES, LANES), jnp.float32)],
        compiler_params=pltpu.CompilerParams(vmem_limit_bytes=8 << 20),
        cost_estimate=pl.CostEstimate(flops=100_000_000, bytes_accessed=4_000_000, transcendentals=0),
        name="filter_inner",
    )(psf_rows, psf_cols, science, inv_var)
    block = exposures * (2 * SHIFT + SUBLANES)
    sent = [
        jax.ShapeDtypeStruct((block + (exposures if p == parts - 1 else 0), LANES), jnp.bfloat16)
        for p in range(parts)
    ]
    sends = pl.pallas_call(
        functools.partial(outer_kernel, radius, chunks),
        out_shape=sent * chunks,
        in_specs=[SMEM] * 4 + [VMEM] * 6,
        out_specs=[VMEM] * (chunks * parts),
        scratch_shapes=[
            pltpu.VMEM((2, 2 * radius, columns), jnp.float32),
            pltpu.VMEM((2, chunks, 3 * SUBLANES, LANES), jnp.float32),
            pltpu.VMEM((2, chunks, 2 * exposures, SUBLANES, LANES), jnp.float32),
            pltpu.VMEM((2, chunks, exposures, SUBLANES, LANES), jnp.float32),
            pltpu.VMEM((exposures, LANES), jnp.float32),
        ],
        compiler_params=pltpu.CompilerParams(vmem_limit_bytes=8 << 20),
        name="filter_outer",
    )(info, psf_rows, psf_cols, exposure_ok, row_shift, col_shift, maps, edges, above, below)

    blocks = [[[None] * chunks for _ in range(subs)] for _ in range(parts + 1)]
    up = [((i + 1) % strips, i) for i in range(strips)]
    for step in range(chunks):
        for p in range(parts):
            blocks[p][0][step] = sends[step * parts + p]
            if step:
                blocks[p][0][step] = lax.ppermute(sends[step * parts + p], "expo", chunk_pairs(step, chunks, subs))
        blocks[parts][0][step] = lax.ppermute(blocks[0][0][step], "strip", up)
    for p in range(parts + 1):
        for u in range(1, subs):
            for step in range(chunks):
                blocks[p][u][step] = lax.ppermute(blocks[p][0][step], "expo", sub_pairs(u, chunks, subs))
    blocks = [[block for sub in part for block in sub] for part in blocks]

    groups = len(blocks[0])
    block_rows = rows // chunks
    reach = rows + SHIFT
    piece = jax.ShapeDtypeStruct((share, block_rows, LANES), jnp.float32)
    total = groups * exposures
    pieces = pl.pallas_call(
        functools.partial(stack_kernel, groups, chunks, exposures, rows, vels),
        out_shape=[piece] * chunks,
        in_specs=[SMEM] + [VMEM] * ((parts + 1) * groups),
        out_specs=[VMEM] * chunks,
        scratch_shapes=[
            pltpu.VMEM((total + UNROLL, 2, reach, LANES), jnp.float32),
            pltpu.VMEM((total + UNROLL, 2, reach, LANES), jnp.float32),
            pltpu.VMEM((total + UNROLL, 2, rows, LANES), jnp.float32),
            pltpu.VMEM((total + UNROLL, 2, rows, LANES), jnp.float32),
            pltpu.VMEM((groups, parts + 1, exposures * SUBLANES, LANES), jnp.float32),
            pltpu.VMEM((total, LANES), jnp.int32),
            pltpu.SMEM((total, LANES), jnp.int32),
            pltpu.SMEM((total + UNROLL,), jnp.int32),
            pltpu.VMEM((share, rows, LANES), jnp.float32),
            pltpu.SemaphoreType.DMA(()),
        ],
        compiler_params=pltpu.CompilerParams(vmem_limit_bytes=24 << 20),
        name="stack_twice",
    )(info, *[block for part in blocks for block in part])

    held = [pieces[0]]
    for step in range(1, chunks):
        held.append(lax.ppermute(pieces[step], "expo", chunk_pairs(step, chunks, subs)))
    out_rows = block_rows // subs
    wide = jax.ShapeDtypeStruct((share, out_rows, columns), jnp.float32)
    parts = pl.pallas_call(
        functools.partial(columns_kernel, chunks, subs),
        out_shape=[wide] * subs,
        in_specs=[SMEM] + [VMEM] * chunks,
        out_specs=[VMEM] * subs,
        scratch_shapes=[
            pltpu.VMEM((chunks, share, block_rows, LANES), jnp.float32),
            pltpu.VMEM((subs, share, out_rows, columns), jnp.float32),
        ],
        compiler_params=pltpu.CompilerParams(vmem_limit_bytes=1 << 20),
        name="join_columns",
    )(info, *held)
    met = [parts[0]]
    for step in range(1, subs):
        met.append(lax.ppermute(parts[step], "expo", sub_pairs(step, chunks, subs)))
    likelihood = pl.pallas_call(
        functools.partial(velocities_kernel, subs),
        out_shape=jax.ShapeDtypeStruct((vels, out_rows, columns), jnp.float32),
        in_specs=[SMEM] + [VMEM] * subs,
        out_specs=VMEM,
        scratch_shapes=[pltpu.VMEM((subs, share, out_rows, columns), jnp.float32)],
        compiler_params=pltpu.CompilerParams(vmem_limit_bytes=1 << 20),
        name="join_velocities",
    )(info, *met)
    return likelihood[None]


def solution(mesh):
    in_specs = (
        P(("field", "expo"), "strip", None),
        P(("field", "expo"), "strip", None),
        P(("field", "expo"), None),
        P(("field", "expo"), None),
        P(("field", "expo"), None),
        P(("field", "expo"), None),
        P(("field", "expo")),
    )
    out_specs = P("strip", "field", "expo", None)

    return jax.shard_map(per_device, mesh=mesh, in_specs=in_specs, out_specs=out_specs, check_vma=False)
```

```python
import functools

import jax
import jax.numpy as jnp
from jax import lax
from jax.experimental import pallas as pl
from jax.experimental.pallas import tpu as pltpu
from jax.sharding import PartitionSpec as P

SHIFT = 16
LANES = 128
SUBLANES = 8
UNROLL = 16

SMEM = pl.BlockSpec(memory_space=pltpu.SMEM)
VMEM = pl.BlockSpec(memory_space=pltpu.VMEM)


def partner(index, step, count):
    if count & (count - 1) == 0:
        return index ^ step
    return (index + step) % count


def chunk_pairs(step, chunks, subs):
    return [
        (j * subs + k, partner(j, step, chunks) * subs + k) for j in range(chunks) for k in range(subs)
    ]


def sub_pairs(step, chunks, subs):
    return [
        (j * subs + k, j * subs + partner(k, step, subs)) for j in range(chunks) for k in range(subs)
    ]


def column_pass(picture, col_taps, e, square):
    tiles = picture.shape[1] // LANES
    taps = col_taps.shape[1]
    lane = lax.broadcasted_iota(jnp.int32, (SUBLANES, LANES), 1)
    zero = jnp.zeros((SUBLANES, LANES), jnp.float32)
    cut = [picture[:, t * LANES : (t + 1) * LANES] for t in range(tiles)]
    totals = None
    for b in range(taps):
        step = b - taps // 2
        tap = col_taps[e, b]
        if square:
            tap = tap * tap
        moved = cut
        if step:
            turned = [pltpu.roll(c, (-step) % LANES, 1) for c in cut]
            if step > 0:
                turned = turned + [zero]
                moved = [jnp.where(lane < LANES - step, turned[t], turned[t + 1]) for t in range(tiles)]
            else:
                turned = [zero] + turned
                moved = [jnp.where(lane >= -step, turned[t + 1], turned[t]) for t in range(tiles)]
        terms = [tap * m for m in moved]
        totals = terms if totals is None else [x + y for x, y in zip(totals, terms)]
    return totals


def row_pass(colpass, row_taps, e, m, first, taps):
    tiles = colpass.shape[1]
    lane = lax.broadcasted_iota(jnp.int32, (SUBLANES, LANES), 1)
    zero = jnp.zeros((SUBLANES, LANES), jnp.float32)
    out = []
    for t in range(tiles):
        total = None
        for a in taps:
            tap = row_taps[e, a]
            if m == 1:
                tap = tap * tap
            term = tap * colpass[m, t, pl.ds(first + a, SUBLANES)]
            total = term if total is None else total + term
        out.append(pltpu.roll(total, SHIFT, 1))
    out = [zero] + out + [zero]
    return [jnp.where(lane < SHIFT, out[t], out[t + 1]) for t in range(tiles + 1)]


def pack_edges(quarters, t):
    lane = lax.broadcasted_iota(jnp.int32, (SUBLANES, LANES), 1)
    packed = jnp.zeros((SUBLANES, LANES), jnp.float32)
    for q, quarter in enumerate(quarters):
        if quarter is None:
            continue
        piece = quarter[t + 1] if q == 0 else pltpu.roll(quarter[t + 1], 2 * SHIFT * q, 1)
        inside = (lane >= 2 * SHIFT * q) & (lane < 2 * SHIFT * (q + 1))
        packed = jnp.where(inside, piece, packed)
    return packed


def inner_kernel(radius, row_taps, col_taps, science, inv_var, maps, edges, colpass):
    exposures, rows, columns = science.shape
    tiles = columns // LANES
    taps = 2 * radius + 1
    pad = SUBLANES
    colpass[:, :, 0:pad] = jnp.zeros((2, tiles, pad, LANES), jnp.float32)
    colpass[:, :, pad + rows : 2 * pad + rows] = jnp.zeros((2, tiles, pad, LANES), jnp.float32)
    parts = rows // SHIFT

    def one_exposure(e, carry):
        inverse_all = inv_var[e].astype(jnp.float32)
        product_all = science[e].astype(jnp.float32) * inverse_all
        for g in range(rows // SUBLANES):
            at = slice(g * SUBLANES, (g + 1) * SUBLANES)
            for m, picture in ((0, product_all[at]), (1, inverse_all[at])):
                for t, total in enumerate(column_pass(picture, col_taps, e, m == 1)):
                    colpass[m, t, pad + g * SUBLANES : pad + (g + 1) * SUBLANES] = total
        for p in range(parts):
            quarters = [
                row_pass(colpass, row_taps, e, m, pad + p * SHIFT + h * SUBLANES - radius, range(taps))
                for m in (0, 1)
                for h in (0, 1)
            ]
            for t in range(tiles):
                for q in range(4):
                    at = p * exposures * 2 * SHIFT + e * 2 * SHIFT + q * SUBLANES
                    maps[t, pl.ds(pl.multiple_of(at, SUBLANES), SUBLANES)] = quarters[q][t]
                at = p * exposures * SUBLANES + e * SUBLANES
                edges[t, pl.ds(pl.multiple_of(at, SUBLANES), SUBLANES)] = pack_edges(quarters, t)
        return carry

    lax.fori_loop(0, exposures, one_exposure, 0, unroll=2)


def outer_kernel(
    radius, chunks, info, row_taps, col_taps, usable, row_shift, col_shift, maps, edges, above, below, *rest
):
    exposures, vels = row_shift.shape
    tiles = maps.shape[0]
    parts = edges.shape[1] // (exposures * SUBLANES)
    sends, (pixels, colpass, more, more_edges, params) = rest[: chunks * parts], rest[chunks * parts :]
    taps = 2 * radius + 1
    pad = SUBLANES
    has_above, has_below, own = info[0] > 0, info[1] > 0, info[2]

    row = lax.broadcasted_iota(jnp.int32, (exposures, 1), 0)
    kept = jnp.zeros((exposures, 1), jnp.int32)
    for e in range(exposures):
        kept = jnp.where(row == e, usable[e], kept)
    params[...] = jnp.zeros_like(params)
    params[:, 0:vels] = row_shift[...].astype(jnp.float32)
    params[:, vels : 2 * vels] = col_shift[...].astype(jnp.float32)
    params[:, 2 * vels : 2 * vels + 1] = kept.astype(jnp.float32)
    colpass[...] = jnp.zeros_like(colpass)

    def one_exposure(e, carry):
        for kind in (0, 1):
            pixels[kind, 0:radius] = jnp.where(has_below, below[kind, e].astype(jnp.float32), 0.0)
            pixels[kind, radius : 2 * radius] = jnp.where(has_above, above[kind, e].astype(jnp.float32), 0.0)
        inverse = pixels[1]
        product = pixels[0] * inverse
        for m, picture in ((0, product), (1, inverse)):
            for t, total in enumerate(column_pass(picture, col_taps, e, m == 1)):
                colpass[m, t, pad : pad + SUBLANES] = total
        upper = [row_pass(colpass, row_taps, e, m, pad + radius, range(radius)) for m in (0, 1)]
        lower = [row_pass(colpass, row_taps, e, m, -radius, range(radius + 1, taps)) for m in (0, 1)]
        for t in range(tiles):
            for m in (0, 1):
                more[0, t, 2 * e + m] = upper[m][t]
                more[1, t, 2 * e + m] = lower[m][t]
            more_edges[0, t, e] = pack_edges([upper[0], None, upper[1], None], t)
            more_edges[1, t, e] = pack_edges([None, lower[0], None, lower[1]], t)
        return carry

    lax.fori_loop(0, exposures, one_exposure, 0, unroll=4)
    main = exposures * 2 * SHIFT
    for step in range(chunks):
        to = partner(own, step, chunks)
        for p in range(parts):
            out = sends[step * parts + p]
            for k in range(2 * exposures):
                first = maps[to, p * main + k * SHIFT : p * main + k * SHIFT + SUBLANES]
                second = maps[to, p * main + k * SHIFT + SUBLANES : p * main + (k + 1) * SHIFT]
                if p == 0:
                    first = first + more[0, to, k]
                if p == parts - 1:
                    second = second + more[1, to, k]
                out[k * SHIFT : (k + 1) * SHIFT] = jnp.concatenate([first, second]).astype(jnp.bfloat16)
            packed = edges[to, p * exposures * SUBLANES : (p + 1) * exposures * SUBLANES]
            if p == 0:
                packed = packed + more_edges[0, to].reshape(packed.shape)
            if p == parts - 1:
                packed = packed + more_edges[1, to].reshape(packed.shape)
            out[main : main + exposures * SUBLANES] = packed.astype(jnp.bfloat16)
            if p == parts - 1:
                tail = main + exposures * SUBLANES
                out[tail : tail + exposures] = params[...].astype(jnp.bfloat16)


def stack_kernel(groups, chunks, exposures, rows, vels, info, *rest):
    parts = rows // SHIFT
    blocks = [rest[p * groups : (p + 1) * groups] for p in range(parts + 1)]
    rest = rest[(parts + 1) * groups :]
    outs = rest[:chunks]
    main, side, even, odd, whole_params, scalars, order, result, sem = rest[chunks:]
    windows = (even, odd)
    own = info[2]
    first_vel = info[4]
    share = result.shape[0]
    main_rows = exposures * 2 * SHIFT
    size = main_rows + exposures * SUBLANES
    total = groups * exposures
    whole_params[total:] = jnp.zeros((exposures, LANES), jnp.int32)
    for g in range(groups):
        whole_params[g * exposures : (g + 1) * exposures] = (
            blocks[parts - 1][g][size : size + exposures].astype(jnp.float32).astype(jnp.int32)
        )
    fetch = pltpu.make_async_copy(whole_params, scalars, sem)
    fetch.start()
    has_below = info[1].astype(jnp.float32)
    for g in range(groups):
        for p in range(parts + 1):
            packed = blocks[p][g][main_rows:size]
            for q in range(4):
                piece = packed if q == 0 else pltpu.roll(packed, LANES - 2 * SHIFT * q, 1)
                piece = piece.astype(jnp.float32)
                if p == parts:
                    piece = piece * has_below
                at = p * SHIFT + (q % 2) * SUBLANES
                for e in range(exposures):
                    side[g * exposures + e, q // 2, at : at + SUBLANES] = piece[e * SUBLANES : (e + 1) * SUBLANES]
            for k in range(2 * exposures):
                cells = blocks[p][g][k * SHIFT : (k + 1) * SHIFT].astype(jnp.float32)
                if p == parts:
                    cells = cells * has_below
                main[g * exposures + k // 2, k % 2, p * SHIFT : (p + 1) * SHIFT] = cells
    main[total] = jnp.zeros(main.shape[1:], jnp.float32)
    side[total] = jnp.zeros(side.shape[1:], jnp.float32)
    fetch.wait()
    filled = jnp.int32(0)
    for source in range(total):
        order[filled] = source
        filled = filled + scalars[source, 2 * vels]
    for i in range(UNROLL):
        order[filled + i] = total
    trips = (filled + UNROLL - 1) // UNROLL

    lane = lax.broadcasted_iota(jnp.int32, (rows, LANES), 1)

    def gather(v, e, sums):
        source = order[e]
        row_at = scalars[source, first_vel + v]
        col_at = scalars[source, vels + first_vel + v] + SHIFT
        from_side = lane < col_at
        cells = jnp.concatenate(
            [
                jnp.where(from_side, side[source, m, pl.ds(row_at, rows)], main[source, m, pl.ds(row_at, rows)])
                for m in (0, 1)
            ]
        ).astype(jnp.bfloat16)
        cells = pltpu.roll(cells, (LANES - col_at) & (LANES - 1), 1).astype(jnp.float32)
        windows[v % 2][e, 0] = cells[:rows]
        windows[v % 2][e, 1] = cells[rows:]
        return sums[0] + cells[:rows], sums[1] + cells[rows:]

    def reweigh(v, e, flux, sums):
        signal = windows[v % 2][e, 0]
        depth = windows[v % 2][e, 1]
        residual = signal - flux * depth
        base = depth + 1.0
        weight = base / (base + residual * residual)
        return sums[0] + weight * signal, sums[1] + weight * depth

    def over_exposures(step, start):
        def trip(t, sums):
            for i in range(UNROLL):
                sums = step(t * UNROLL + i, sums)
            return sums

        return lax.fori_loop(0, trips, trip, start)

    zeros = main[total, 0, 0:rows]
    none = (zeros, zeros)

    sums = over_exposures(functools.partial(gather, 0), none)
    for v in range(share):
        flux = sums[0] / (sums[1] + 1.0)

        def weigh(e, sums, v=v, flux=flux):
            return reweigh(v, e, flux, sums)

        def both(e, sums, v=v, weigh=weigh):
            return gather(v + 1, e, sums[:2]) + weigh(e, sums[2:])

        if v + 1 < share:
            sums = over_exposures(both, none + none)
        else:
            sums = none + over_exposures(weigh, none)
        result[v] = sums[2] / jnp.sqrt(sums[3] + 1.0)
    block = rows // chunks
    for step in range(chunks):
        to = partner(own, step, chunks)
        outs[step][...] = result[:, pl.ds(pl.multiple_of(to * block, block), block)]


def columns_kernel(chunks, subs, info, *rest):
    pieces = rest[:chunks]
    outs = rest[chunks : chunks + subs]
    held, wide = rest[chunks + subs :]
    own_chunk, own_sub = info[2], info[3]
    for step in range(chunks):
        held[step] = pieces[step][...]
    rows = wide.shape[2]
    for c in range(chunks):
        piece = held[partner(own_chunk, c, chunks)]
        for k in range(subs):
            wide[k, :, :, c * LANES : (c + 1) * LANES] = piece[:, k * rows : (k + 1) * rows]
    for step in range(subs):
        outs[step][...] = wide[partner(own_sub, step, subs)]


def velocities_kernel(subs, info, *rest):
    pieces = rest[:subs]
    out, held = rest[subs:]
    own_sub = info[3]
    for step in range(subs):
        held[step] = pieces[step][...]
    share = held.shape[1]
    for k in range(subs):
        out[k * share : (k + 1) * share] = held[partner(own_sub, k, subs)]


def per_device(science, inv_var, psf_rows, psf_cols, row_shift, col_shift, exposure_ok):
    exposures, rows, columns = science.shape
    vels = row_shift.shape[1]
    radius = psf_rows.shape[1] // 2
    strips = lax.axis_size("strip")
    members = lax.axis_size("expo")
    chunks = columns // LANES
    subs = members // chunks
    share = vels // subs
    parts = rows // SHIFT
    strip = lax.axis_index("strip")
    me = lax.axis_index("expo")
    own_chunk = me // subs
    own_sub = me % subs
    info = jnp.stack([strip > 0, strip < strips - 1, own_chunk, own_sub, own_sub * share]).astype(jnp.int32)

    def rows_from(start):
        return jnp.stack([lax.dynamic_slice_in_dim(x, start, radius, 1) for x in (science, inv_var)])

    if strips == 2:
        met = rows_from(jnp.where(strip == 0, rows - radius, 0))
        above = below = lax.ppermute(met, "strip", [(0, 1), (1, 0)])
    else:
        above = lax.ppermute(rows_from(rows - radius), "strip", [(i, i + 1) for i in range(strips - 1)])
        below = lax.ppermute(rows_from(0), "strip", [(i + 1, i) for i in range(strips - 1)])

    map_rows = parts * exposures * 2 * SHIFT
    edge_rows = parts * exposures * SUBLANES
    maps, edges = pl.pallas_call(
        functools.partial(inner_kernel, radius),
        out_shape=[
            jax.ShapeDtypeStruct((chunks, map_rows, LANES), jnp.float32),
            jax.ShapeDtypeStruct((chunks, edge_rows, LANES), jnp.float32),
        ],
        in_specs=[SMEM] * 2 + [VMEM] * 2,
        out_specs=[VMEM] * 2,
        scratch_shapes=[pltpu.VMEM((2, chunks, rows + 2 * SUBLANES, LANES), jnp.float32)],
        compiler_params=pltpu.CompilerParams(vmem_limit_bytes=8 << 20),
        cost_estimate=pl.CostEstimate(flops=100_000_000, bytes_accessed=4_000_000, transcendentals=0),
        name="filter_inner",
    )(psf_rows, psf_cols, science, inv_var)
    block = exposures * (2 * SHIFT + SUBLANES)
    sent = [
        jax.ShapeDtypeStruct((block + (exposures if p == parts - 1 else 0), LANES), jnp.bfloat16)
        for p in range(parts)
    ]
    sends = pl.pallas_call(
        functools.partial(outer_kernel, radius, chunks),
        out_shape=sent * chunks,
        in_specs=[SMEM] * 4 + [VMEM] * 6,
        out_specs=[VMEM] * (chunks * parts),
        scratch_shapes=[
            pltpu.VMEM((2, 2 * radius, columns), jnp.float32),
            pltpu.VMEM((2, chunks, 3 * SUBLANES, LANES), jnp.float32),
            pltpu.VMEM((2, chunks, 2 * exposures, SUBLANES, LANES), jnp.float32),
            pltpu.VMEM((2, chunks, exposures, SUBLANES, LANES), jnp.float32),
            pltpu.VMEM((exposures, LANES), jnp.float32),
        ],
        compiler_params=pltpu.CompilerParams(vmem_limit_bytes=8 << 20),
        name="filter_outer",
    )(info, psf_rows, psf_cols, exposure_ok, row_shift, col_shift, maps, edges, above, below)

    blocks = [[[None] * chunks for _ in range(subs)] for _ in range(parts + 1)]
    up = [((i + 1) % strips, i) for i in range(strips)]
    for step in range(chunks):
        for p in range(parts):
            blocks[p][0][step] = sends[step * parts + p]
            if step:
                blocks[p][0][step] = lax.ppermute(sends[step * parts + p], "expo", chunk_pairs(step, chunks, subs))
        blocks[parts][0][step] = lax.ppermute(blocks[0][0][step], "strip", up)
    for p in range(parts + 1):
        for u in range(1, subs):
            for step in range(chunks):
                blocks[p][u][step] = lax.ppermute(blocks[p][0][step], "expo", sub_pairs(u, chunks, subs))
    blocks = [[block for sub in part for block in sub] for part in blocks]

    groups = len(blocks[0])
    block_rows = rows // chunks
    reach = rows + SHIFT
    piece = jax.ShapeDtypeStruct((share, block_rows, LANES), jnp.float32)
    total = groups * exposures
    pieces = pl.pallas_call(
        functools.partial(stack_kernel, groups, chunks, exposures, rows, vels),
        out_shape=[piece] * chunks,
        in_specs=[SMEM] + [VMEM] * ((parts + 1) * groups),
        out_specs=[VMEM] * chunks,
        scratch_shapes=[
            pltpu.VMEM((total + 1, 2, reach, LANES), jnp.float32),
            pltpu.VMEM((total + 1, 2, reach, LANES), jnp.float32),
            pltpu.VMEM((total + UNROLL, 2, rows, LANES), jnp.float32),
            pltpu.VMEM((total + UNROLL, 2, rows, LANES), jnp.float32),
            pltpu.VMEM((total + exposures, LANES), jnp.int32),
            pltpu.SMEM((total + exposures, LANES), jnp.int32),
            pltpu.SMEM((total + UNROLL,), jnp.int32),
            pltpu.VMEM((share, rows, LANES), jnp.float32),
            pltpu.SemaphoreType.DMA(()),
        ],
        compiler_params=pltpu.CompilerParams(vmem_limit_bytes=24 << 20),
        name="stack_twice",
    )(info, *[block for part in blocks for block in part])

    held = [pieces[0]]
    for step in range(1, chunks):
        held.append(lax.ppermute(pieces[step], "expo", chunk_pairs(step, chunks, subs)))
    out_rows = block_rows // subs
    wide = jax.ShapeDtypeStruct((share, out_rows, columns), jnp.float32)
    parts = pl.pallas_call(
        functools.partial(columns_kernel, chunks, subs),
        out_shape=[wide] * subs,
        in_specs=[SMEM] + [VMEM] * chunks,
        out_specs=[VMEM] * subs,
        scratch_shapes=[
            pltpu.VMEM((chunks, share, block_rows, LANES), jnp.float32),
            pltpu.VMEM((subs, share, out_rows, columns), jnp.float32),
        ],
        compiler_params=pltpu.CompilerParams(vmem_limit_bytes=1 << 20),
        name="join_columns",
    )(info, *held)
    met = [parts[0]]
    for step in range(1, subs):
        met.append(lax.ppermute(parts[step], "expo", sub_pairs(step, chunks, subs)))
    likelihood = pl.pallas_call(
        functools.partial(velocities_kernel, subs),
        out_shape=jax.ShapeDtypeStruct((vels, out_rows, columns), jnp.float32),
        in_specs=[SMEM] + [VMEM] * subs,
        out_specs=VMEM,
        scratch_shapes=[pltpu.VMEM((subs, share, out_rows, columns), jnp.float32)],
        compiler_params=pltpu.CompilerParams(vmem_limit_bytes=1 << 20),
        name="join_velocities",
    )(info, *met)
    return likelihood[None]


def solution(mesh):
    in_specs = (
        P(("field", "expo"), "strip", None),
        P(("field", "expo"), "strip", None),
        P(("field", "expo"), None),
        P(("field", "expo"), None),
        P(("field", "expo"), None),
        P(("field", "expo"), None),
        P(("field", "expo")),
    )
    out_specs = P("strip", "field", "expo", None)

    return jax.shard_map(per_device, mesh=mesh, in_specs=in_specs, out_specs=out_specs, check_vma=False)
```

```python
import functools

import jax
import jax.numpy as jnp
from jax import lax
from jax.experimental import pallas as pl
from jax.experimental.pallas import tpu as pltpu
from jax.sharding import PartitionSpec as P

SHIFT = 16
LANES = 128
SUBLANES = 8
UNROLL = 16

SMEM = pl.BlockSpec(memory_space=pltpu.SMEM)
VMEM = pl.BlockSpec(memory_space=pltpu.VMEM)
HBM = pl.BlockSpec(memory_space=pltpu.HBM)


def partner(index, step, count):
    if count & (count - 1) == 0:
        return index ^ step
    return (index + step) % count


def chunk_pairs(step, chunks, subs):
    return [
        (j * subs + k, partner(j, step, chunks) * subs + k) for j in range(chunks) for k in range(subs)
    ]


def sub_pairs(step, chunks, subs):
    return [
        (j * subs + k, j * subs + partner(k, step, subs)) for j in range(chunks) for k in range(subs)
    ]


def column_pass(picture, col_taps, e, square):
    tiles = picture.shape[1] // LANES
    taps = col_taps.shape[1]
    lane = lax.broadcasted_iota(jnp.int32, (SUBLANES, LANES), 1)
    zero = jnp.zeros((SUBLANES, LANES), jnp.float32)
    cut = [picture[:, t * LANES : (t + 1) * LANES] for t in range(tiles)]
    totals = None
    for b in range(taps):
        step = b - taps // 2
        tap = col_taps[e, b]
        if square:
            tap = tap * tap
        moved = cut
        if step:
            turned = [pltpu.roll(c, (-step) % LANES, 1) for c in cut]
            if step > 0:
                turned = turned + [zero]
                moved = [jnp.where(lane < LANES - step, turned[t], turned[t + 1]) for t in range(tiles)]
            else:
                turned = [zero] + turned
                moved = [jnp.where(lane >= -step, turned[t + 1], turned[t]) for t in range(tiles)]
        terms = [tap * m for m in moved]
        totals = terms if totals is None else [x + y for x, y in zip(totals, terms)]
    return totals


def row_pass(colpass, row_taps, e, m, first, taps):
    tiles = colpass.shape[1]
    lane = lax.broadcasted_iota(jnp.int32, (SUBLANES, LANES), 1)
    zero = jnp.zeros((SUBLANES, LANES), jnp.float32)
    out = []
    for t in range(tiles):
        total = None
        for a in taps:
            tap = row_taps[e, a]
            if m == 1:
                tap = tap * tap
            term = tap * colpass[m, t, pl.ds(first + a, SUBLANES)]
            total = term if total is None else total + term
        out.append(pltpu.roll(total, SHIFT, 1))
    out = [zero] + out + [zero]
    return [jnp.where(lane < SHIFT, out[t], out[t + 1]) for t in range(tiles + 1)]


def pack_edges(quarters, t):
    lane = lax.broadcasted_iota(jnp.int32, (SUBLANES, LANES), 1)
    packed = jnp.zeros((SUBLANES, LANES), jnp.float32)
    for q, quarter in enumerate(quarters):
        if quarter is None:
            continue
        piece = quarter[t + 1] if q == 0 else pltpu.roll(quarter[t + 1], 2 * SHIFT * q, 1)
        inside = (lane >= 2 * SHIFT * q) & (lane < 2 * SHIFT * (q + 1))
        packed = jnp.where(inside, piece, packed)
    return packed


def inner_kernel(
    radius,
    science_hbm,
    inv_var_hbm,
    row_taps_hbm,
    col_taps_hbm,
    row_shift_hbm,
    col_shift_hbm,
    usable_hbm,
    maps,
    edges,
    params,
    science,
    inv_var,
    row_taps,
    col_taps,
    row_shift,
    col_shift,
    usable,
    colpass,
    sems,
):
    exposures, rows, columns = science.shape
    tiles = columns // LANES
    taps = 2 * radius + 1
    vels = row_shift.shape[1]
    pad = SUBLANES
    pairs = (
        (row_taps_hbm, row_taps),
        (col_taps_hbm, col_taps),
        (science_hbm, science),
        (inv_var_hbm, inv_var),
        (row_shift_hbm, row_shift),
        (col_shift_hbm, col_shift),
        (usable_hbm, usable),
    )
    copies = [pltpu.make_async_copy(source, target, sems.at[i]) for i, (source, target) in enumerate(pairs)]
    for copy in copies:
        copy.start()
    colpass[:, :, 0:pad] = jnp.zeros((2, tiles, pad, LANES), jnp.float32)
    colpass[:, :, pad + rows : 2 * pad + rows] = jnp.zeros((2, tiles, pad, LANES), jnp.float32)
    params[...] = jnp.zeros_like(params)
    for copy in copies:
        copy.wait()
    row = lax.broadcasted_iota(jnp.int32, (exposures, 1), 0)
    kept = jnp.zeros((exposures, 1), jnp.int32)
    for e in range(exposures):
        kept = jnp.where(row == e, usable[e], kept)
    params[:, 0:vels] = row_shift[...].astype(jnp.float32)
    params[:, vels : 2 * vels] = col_shift[...].astype(jnp.float32)
    params[:, 2 * vels : 2 * vels + 1] = kept.astype(jnp.float32)
    parts = rows // SHIFT

    def one_exposure(e, carry):
        inverse_all = inv_var[e].astype(jnp.float32)
        product_all = science[e].astype(jnp.float32) * inverse_all
        for g in range(rows // SUBLANES):
            at = slice(g * SUBLANES, (g + 1) * SUBLANES)
            for m, picture in ((0, product_all[at]), (1, inverse_all[at])):
                for t, total in enumerate(column_pass(picture, col_taps, e, m == 1)):
                    colpass[m, t, pad + g * SUBLANES : pad + (g + 1) * SUBLANES] = total
        for p in range(parts):
            quarters = [
                row_pass(colpass, row_taps, e, m, pad + p * SHIFT + h * SUBLANES - radius, range(taps))
                for m in (0, 1)
                for h in (0, 1)
            ]
            for t in range(tiles):
                for q in range(4):
                    at = p * exposures * 2 * SHIFT + e * 2 * SHIFT + q * SUBLANES
                    maps[t, pl.ds(pl.multiple_of(at, SUBLANES), SUBLANES)] = quarters[q][t]
                at = p * exposures * SUBLANES + e * SUBLANES
                edges[t, pl.ds(pl.multiple_of(at, SUBLANES), SUBLANES)] = pack_edges(quarters, t)
        return carry

    lax.fori_loop(0, exposures, one_exposure, 0, unroll=2)


def outer_kernel(
    radius, chunks, info, row_taps, col_taps, maps, edges, params, above, below, *rest
):
    exposures = params.shape[0]
    tiles = maps.shape[0]
    parts = edges.shape[1] // (exposures * SUBLANES)
    sends, (pixels, colpass, more, more_edges) = rest[: chunks * parts], rest[chunks * parts :]
    taps = 2 * radius + 1
    pad = SUBLANES
    has_above, has_below, own = info[0] > 0, info[1] > 0, info[2]

    colpass[...] = jnp.zeros_like(colpass)

    def one_exposure(e, carry):
        for kind in (0, 1):
            pixels[kind, 0:radius] = jnp.where(has_below, below[kind, e].astype(jnp.float32), 0.0)
            pixels[kind, radius : 2 * radius] = jnp.where(has_above, above[kind, e].astype(jnp.float32), 0.0)
        inverse = pixels[1]
        product = pixels[0] * inverse
        for m, picture in ((0, product), (1, inverse)):
            for t, total in enumerate(column_pass(picture, col_taps, e, m == 1)):
                colpass[m, t, pad : pad + SUBLANES] = total
        upper = [row_pass(colpass, row_taps, e, m, pad + radius, range(radius)) for m in (0, 1)]
        lower = [row_pass(colpass, row_taps, e, m, -radius, range(radius + 1, taps)) for m in (0, 1)]
        for t in range(tiles):
            for m in (0, 1):
                more[0, t, 2 * e + m] = upper[m][t]
                more[1, t, 2 * e + m] = lower[m][t]
            more_edges[0, t, e] = pack_edges([upper[0], None, upper[1], None], t)
            more_edges[1, t, e] = pack_edges([None, lower[0], None, lower[1]], t)
        return carry

    lax.fori_loop(0, exposures, one_exposure, 0, unroll=4)
    main = exposures * 2 * SHIFT
    for step in range(chunks):
        to = partner(own, step, chunks)
        for p in range(parts):
            out = sends[step * parts + p]
            for k in range(2 * exposures):
                first = maps[to, p * main + k * SHIFT : p * main + k * SHIFT + SUBLANES]
                second = maps[to, p * main + k * SHIFT + SUBLANES : p * main + (k + 1) * SHIFT]
                if p == 0:
                    first = first + more[0, to, k]
                if p == parts - 1:
                    second = second + more[1, to, k]
                out[k * SHIFT : (k + 1) * SHIFT] = jnp.concatenate([first, second]).astype(jnp.bfloat16)
            packed = edges[to, p * exposures * SUBLANES : (p + 1) * exposures * SUBLANES]
            if p == 0:
                packed = packed + more_edges[0, to].reshape(packed.shape)
            if p == parts - 1:
                packed = packed + more_edges[1, to].reshape(packed.shape)
            out[main : main + exposures * SUBLANES] = packed.astype(jnp.bfloat16)
            if p == parts - 1:
                tail = main + exposures * SUBLANES
                out[tail : tail + exposures] = params[...].astype(jnp.bfloat16)


def stack_kernel(groups, chunks, exposures, rows, vels, info, *rest):
    parts = rows // SHIFT
    blocks = [rest[p * groups : (p + 1) * groups] for p in range(parts + 1)]
    rest = rest[(parts + 1) * groups :]
    outs = rest[:chunks]
    main, side, even, odd, whole_params, scalars, order, result, sem = rest[chunks:]
    windows = (even, odd)
    own = info[2]
    first_vel = info[4]
    share = result.shape[0]
    main_rows = exposures * 2 * SHIFT
    size = main_rows + exposures * SUBLANES
    total = groups * exposures
    whole_params[total:] = jnp.zeros((exposures, LANES), jnp.int32)
    for g in range(groups):
        whole_params[g * exposures : (g + 1) * exposures] = (
            blocks[parts - 1][g][size : size + exposures].astype(jnp.float32).astype(jnp.int32)
        )
    fetch = pltpu.make_async_copy(whole_params, scalars, sem)
    fetch.start()
    has_below = info[1].astype(jnp.float32)
    for g in range(groups):
        for p in range(parts + 1):
            packed = blocks[p][g][main_rows:size]
            for q in range(4):
                piece = packed if q == 0 else pltpu.roll(packed, LANES - 2 * SHIFT * q, 1)
                piece = piece.astype(jnp.float32)
                if p == parts:
                    piece = piece * has_below
                at = p * SHIFT + (q % 2) * SUBLANES
                for e in range(exposures):
                    side[g * exposures + e, q // 2, at : at + SUBLANES] = piece[e * SUBLANES : (e + 1) * SUBLANES]
            for k in range(2 * exposures):
                cells = blocks[p][g][k * SHIFT : (k + 1) * SHIFT].astype(jnp.float32)
                if p == parts:
                    cells = cells * has_below
                main[g * exposures + k // 2, k % 2, p * SHIFT : (p + 1) * SHIFT] = cells
    main[total] = jnp.zeros(main.shape[1:], jnp.float32)
    side[total] = jnp.zeros(side.shape[1:], jnp.float32)
    fetch.wait()
    filled = jnp.int32(0)
    for source in range(total):
        order[filled] = source
        filled = filled + scalars[source, 2 * vels]
    for i in range(UNROLL):
        order[filled + i] = total
    trips = (filled + UNROLL - 1) // UNROLL

    lane = lax.broadcasted_iota(jnp.int32, (rows, LANES), 1)

    def gather(v, e, sums):
        source = order[e]
        row_at = scalars[source, first_vel + v]
        col_at = scalars[source, vels + first_vel + v] + SHIFT
        from_side = lane < col_at
        cells = jnp.concatenate(
            [
                jnp.where(from_side, side[source, m, pl.ds(row_at, rows)], main[source, m, pl.ds(row_at, rows)])
                for m in (0, 1)
            ]
        ).astype(jnp.bfloat16)
        cells = pltpu.roll(cells, (LANES - col_at) & (LANES - 1), 1).astype(jnp.float32)
        windows[v % 2][e, 0] = cells[:rows]
        windows[v % 2][e, 1] = cells[rows:]
        return sums[0] + cells[:rows], sums[1] + cells[rows:]

    def reweigh(v, e, flux, sums):
        signal = windows[v % 2][e, 0]
        depth = windows[v % 2][e, 1]
        residual = signal - flux * depth
        base = depth + 1.0
        weight = base / (base + residual * residual)
        return sums[0] + weight * signal, sums[1] + weight * depth

    def over_exposures(step, start):
        def trip(t, sums):
            for i in range(UNROLL):
                sums = step(t * UNROLL + i, sums)
            return sums

        return lax.fori_loop(0, trips, trip, start)

    zeros = main[total, 0, 0:rows]
    none = (zeros, zeros)

    sums = over_exposures(functools.partial(gather, 0), none)
    for v in range(share):
        flux = sums[0] / (sums[1] + 1.0)

        def weigh(e, sums, v=v, flux=flux):
            return reweigh(v, e, flux, sums)

        def both(e, sums, v=v, weigh=weigh):
            return gather(v + 1, e, sums[:2]) + weigh(e, sums[2:])

        if v + 1 < share:
            sums = over_exposures(both, none + none)
        else:
            sums = none + over_exposures(weigh, none)
        result[v] = sums[2] / jnp.sqrt(sums[3] + 1.0)
    block = rows // chunks
    for step in range(chunks):
        to = partner(own, step, chunks)
        outs[step][...] = result[:, pl.ds(pl.multiple_of(to * block, block), block)]


def columns_kernel(chunks, subs, info, *rest):
    pieces = rest[:chunks]
    outs = rest[chunks : chunks + subs]
    held, wide = rest[chunks + subs :]
    own_chunk, own_sub = info[2], info[3]
    for step in range(chunks):
        held[step] = pieces[step][...]
    rows = wide.shape[2]
    for c in range(chunks):
        piece = held[partner(own_chunk, c, chunks)]
        for k in range(subs):
            wide[k, :, :, c * LANES : (c + 1) * LANES] = piece[:, k * rows : (k + 1) * rows]
    for step in range(subs):
        outs[step][...] = wide[partner(own_sub, step, subs)]


def velocities_kernel(subs, info, *rest):
    pieces = rest[:subs]
    out, held = rest[subs:]
    own_sub = info[3]
    for step in range(subs):
        held[step] = pieces[step][...]
    share = held.shape[1]
    for k in range(subs):
        out[k * share : (k + 1) * share] = held[partner(own_sub, k, subs)]


def per_device(science, inv_var, psf_rows, psf_cols, row_shift, col_shift, exposure_ok):
    exposures, rows, columns = science.shape
    vels = row_shift.shape[1]
    radius = psf_rows.shape[1] // 2
    strips = lax.axis_size("strip")
    members = lax.axis_size("expo")
    chunks = columns // LANES
    subs = members // chunks
    share = vels // subs
    parts = rows // SHIFT
    strip = lax.axis_index("strip")
    me = lax.axis_index("expo")
    own_chunk = me // subs
    own_sub = me % subs
    info = jnp.stack([strip > 0, strip < strips - 1, own_chunk, own_sub, own_sub * share]).astype(jnp.int32)

    def rows_from(start):
        return jnp.stack([lax.dynamic_slice_in_dim(x, start, radius, 1) for x in (science, inv_var)])

    if strips == 2:
        met = rows_from(jnp.where(strip == 0, rows - radius, 0))
        above = below = lax.ppermute(met, "strip", [(0, 1), (1, 0)])
    else:
        above = lax.ppermute(rows_from(rows - radius), "strip", [(i, i + 1) for i in range(strips - 1)])
        below = lax.ppermute(rows_from(0), "strip", [(i + 1, i) for i in range(strips - 1)])

    map_rows = parts * exposures * 2 * SHIFT
    edge_rows = parts * exposures * SUBLANES
    maps, edges, params = pl.pallas_call(
        functools.partial(inner_kernel, radius),
        out_shape=[
            jax.ShapeDtypeStruct((chunks, map_rows, LANES), jnp.float32),
            jax.ShapeDtypeStruct((chunks, edge_rows, LANES), jnp.float32),
            jax.ShapeDtypeStruct((exposures, LANES), jnp.float32),
        ],
        in_specs=[HBM] * 7,
        out_specs=[VMEM] * 3,
        scratch_shapes=[
            pltpu.VMEM(science.shape, science.dtype),
            pltpu.VMEM(inv_var.shape, inv_var.dtype),
            pltpu.SMEM(psf_rows.shape, jnp.float32),
            pltpu.SMEM(psf_cols.shape, jnp.float32),
            pltpu.VMEM(row_shift.shape, jnp.int32),
            pltpu.VMEM(col_shift.shape, jnp.int32),
            pltpu.SMEM(exposure_ok.shape, jnp.int32),
            pltpu.VMEM((2, chunks, rows + 2 * SUBLANES, LANES), jnp.float32),
            pltpu.SemaphoreType.DMA((7,)),
        ],
        compiler_params=pltpu.CompilerParams(vmem_limit_bytes=8 << 20),
        cost_estimate=pl.CostEstimate(flops=100_000_000, bytes_accessed=4_000_000, transcendentals=0),
        name="filter_inner",
    )(*[pltpu.with_memory_space_constraint(x, pltpu.HBM) for x in (science, inv_var, psf_rows, psf_cols, row_shift, col_shift, exposure_ok)])
    block = exposures * (2 * SHIFT + SUBLANES)
    sent = [
        jax.ShapeDtypeStruct((block + (exposures if p == parts - 1 else 0), LANES), jnp.bfloat16)
        for p in range(parts)
    ]
    sends = pl.pallas_call(
        functools.partial(outer_kernel, radius, chunks),
        out_shape=sent * chunks,
        in_specs=[SMEM] * 3 + [VMEM] * 5,
        out_specs=[VMEM] * (chunks * parts),
        scratch_shapes=[
            pltpu.VMEM((2, 2 * radius, columns), jnp.float32),
            pltpu.VMEM((2, chunks, 3 * SUBLANES, LANES), jnp.float32),
            pltpu.VMEM((2, chunks, 2 * exposures, SUBLANES, LANES), jnp.float32),
            pltpu.VMEM((2, chunks, exposures, SUBLANES, LANES), jnp.float32),
        ],
        compiler_params=pltpu.CompilerParams(vmem_limit_bytes=8 << 20),
        name="filter_outer",
    )(info, psf_rows, psf_cols, maps, edges, params, above, below)

    blocks = [[[None] * chunks for _ in range(subs)] for _ in range(parts + 1)]
    up = [((i + 1) % strips, i) for i in range(strips)]
    for step in range(chunks):
        for p in range(parts):
            blocks[p][0][step] = sends[step * parts + p]
            if step:
                blocks[p][0][step] = lax.ppermute(sends[step * parts + p], "expo", chunk_pairs(step, chunks, subs))
        blocks[parts][0][step] = lax.ppermute(blocks[0][0][step], "strip", up)
    for p in range(parts + 1):
        for u in range(1, subs):
            for step in range(chunks):
                blocks[p][u][step] = lax.ppermute(blocks[p][0][step], "expo", sub_pairs(u, chunks, subs))
    blocks = [[block for sub in part for block in sub] for part in blocks]

    groups = len(blocks[0])
    block_rows = rows // chunks
    reach = rows + SHIFT
    piece = jax.ShapeDtypeStruct((share, block_rows, LANES), jnp.float32)
    total = groups * exposures
    pieces = pl.pallas_call(
        functools.partial(stack_kernel, groups, chunks, exposures, rows, vels),
        out_shape=[piece] * chunks,
        in_specs=[SMEM] + [VMEM] * ((parts + 1) * groups),
        out_specs=[VMEM] * chunks,
        scratch_shapes=[
            pltpu.VMEM((total + 1, 2, reach, LANES), jnp.float32),
            pltpu.VMEM((total + 1, 2, reach, LANES), jnp.float32),
            pltpu.VMEM((total + UNROLL, 2, rows, LANES), jnp.float32),
            pltpu.VMEM((total + UNROLL, 2, rows, LANES), jnp.float32),
            pltpu.VMEM((total + exposures, LANES), jnp.int32),
            pltpu.SMEM((total + exposures, LANES), jnp.int32),
            pltpu.SMEM((total + UNROLL,), jnp.int32),
            pltpu.VMEM((share, rows, LANES), jnp.float32),
            pltpu.SemaphoreType.DMA(()),
        ],
        compiler_params=pltpu.CompilerParams(vmem_limit_bytes=24 << 20),
        name="stack_twice",
    )(info, *[block for part in blocks for block in part])

    held = [pieces[0]]
    for step in range(1, chunks):
        held.append(lax.ppermute(pieces[step], "expo", chunk_pairs(step, chunks, subs)))
    out_rows = block_rows // subs
    wide = jax.ShapeDtypeStruct((share, out_rows, columns), jnp.float32)
    parts = pl.pallas_call(
        functools.partial(columns_kernel, chunks, subs),
        out_shape=[wide] * subs,
        in_specs=[SMEM] + [VMEM] * chunks,
        out_specs=[VMEM] * subs,
        scratch_shapes=[
            pltpu.VMEM((chunks, share, block_rows, LANES), jnp.float32),
            pltpu.VMEM((subs, share, out_rows, columns), jnp.float32),
        ],
        compiler_params=pltpu.CompilerParams(vmem_limit_bytes=1 << 20),
        name="join_columns",
    )(info, *held)
    met = [parts[0]]
    for step in range(1, subs):
        met.append(lax.ppermute(parts[step], "expo", sub_pairs(step, chunks, subs)))
    likelihood = pl.pallas_call(
        functools.partial(velocities_kernel, subs),
        out_shape=jax.ShapeDtypeStruct((vels, out_rows, columns), jnp.float32),
        in_specs=[SMEM] + [VMEM] * subs,
        out_specs=VMEM,
        scratch_shapes=[pltpu.VMEM((subs, share, out_rows, columns), jnp.float32)],
        compiler_params=pltpu.CompilerParams(vmem_limit_bytes=1 << 20),
        name="join_velocities",
    )(info, *met)
    return likelihood[None]


def solution(mesh):
    in_specs = (
        P(("field", "expo"), "strip", None),
        P(("field", "expo"), "strip", None),
        P(("field", "expo"), None),
        P(("field", "expo"), None),
        P(("field", "expo"), None),
        P(("field", "expo"), None),
        P(("field", "expo")),
    )
    out_specs = P("strip", "field", "expo", None)

    return jax.shard_map(per_device, mesh=mesh, in_specs=in_specs, out_specs=out_specs, check_vma=False)
```

```python
import functools

import jax
import jax.numpy as jnp
from jax import lax
from jax.experimental import pallas as pl
from jax.experimental.pallas import tpu as pltpu
from jax.sharding import PartitionSpec as P

SHIFT = 16
LANES = 128
SUBLANES = 8
UNROLL = 16

SMEM = pl.BlockSpec(memory_space=pltpu.SMEM)
VMEM = pl.BlockSpec(memory_space=pltpu.VMEM)
HBM = pl.BlockSpec(memory_space=pltpu.HBM)


def partner(index, step, count):
    if count & (count - 1) == 0:
        return index ^ step
    return (index + step) % count


def chunk_pairs(step, chunks, subs):
    return [
        (j * subs + k, partner(j, step, chunks) * subs + k) for j in range(chunks) for k in range(subs)
    ]


def sub_pairs(step, chunks, subs):
    return [
        (j * subs + k, j * subs + partner(k, step, subs)) for j in range(chunks) for k in range(subs)
    ]


def split_rows(subs, parts):
    return subs == 2 and parts == 2


def strip_pairs(strips, chunks):
    same, cross = [], []
    for x in range(strips):
        after = (x + 1) % strips
        for j in range(chunks):
            first, second = 2 * j * strips, (2 * j + 1) * strips
            same += [(first + x, first + x), (second + after, second + x)]
            cross += [(second + x, first + x), (first + after, second + x)]
    return same, cross


def row_pairs(step, chunks):
    return [(2 * j + h, chunks * h + partner(j, step, chunks)) for j in range(chunks) for h in (0, 1)]


def column_pass(picture, col_tap, taps, e, square):
    tiles = picture.shape[1] // LANES
    lane = lax.broadcasted_iota(jnp.int32, (SUBLANES, LANES), 1)
    zero = jnp.zeros((SUBLANES, LANES), jnp.float32)
    cut = [picture[:, t * LANES : (t + 1) * LANES] for t in range(tiles)]
    totals = None
    for b in range(taps):
        step = b - taps // 2
        tap = col_tap(e, b)
        if square:
            tap = tap * tap
        moved = cut
        if step:
            turned = [pltpu.roll(c, (-step) % LANES, 1) for c in cut]
            if step > 0:
                turned = turned + [zero]
                moved = [jnp.where(lane < LANES - step, turned[t], turned[t + 1]) for t in range(tiles)]
            else:
                turned = [zero] + turned
                moved = [jnp.where(lane >= -step, turned[t + 1], turned[t]) for t in range(tiles)]
        terms = [tap * m for m in moved]
        totals = terms if totals is None else [x + y for x, y in zip(totals, terms)]
    return totals


def row_pass(colpass, row_tap, e, m, first, taps):
    tiles = colpass.shape[1]
    lane = lax.broadcasted_iota(jnp.int32, (SUBLANES, LANES), 1)
    zero = jnp.zeros((SUBLANES, LANES), jnp.float32)
    out = []
    for t in range(tiles):
        total = None
        for a in taps:
            tap = row_tap(e, a)
            if m == 1:
                tap = tap * tap
            term = tap * colpass[m, t, pl.ds(first + a, SUBLANES)]
            total = term if total is None else total + term
        out.append(pltpu.roll(total, SHIFT, 1))
    out = [zero] + out + [zero]
    return [jnp.where(lane < SHIFT, out[t], out[t + 1]) for t in range(tiles + 1)]


def pack_edges(quarters, t):
    lane = lax.broadcasted_iota(jnp.int32, (SUBLANES, LANES), 1)
    packed = jnp.zeros((SUBLANES, LANES), jnp.float32)
    for q, quarter in enumerate(quarters):
        if quarter is None:
            continue
        piece = quarter[t + 1] if q == 0 else pltpu.roll(quarter[t + 1], 2 * SHIFT * q, 1)
        inside = (lane >= 2 * SHIFT * q) & (lane < 2 * SHIFT * (q + 1))
        packed = jnp.where(inside, piece, packed)
    return packed


def inner_kernel(
    radius,
    science_hbm,
    inv_var_hbm,
    row_taps_hbm,
    col_taps_hbm,
    row_shift_hbm,
    col_shift_hbm,
    usable_hbm,
    maps,
    edges,
    params,
    tap_rows,
    science,
    inv_var,
    row_taps,
    col_taps,
    row_shift,
    col_shift,
    usable,
    colpass,
    sems,
):
    exposures, rows, columns = science.shape
    tiles = columns // LANES
    taps = 2 * radius + 1
    vels = row_shift.shape[1]
    pad = SUBLANES
    pairs = (
        (row_taps_hbm, row_taps),
        (col_taps_hbm, col_taps),
        (science_hbm, science),
        (inv_var_hbm, inv_var),
        (row_shift_hbm, row_shift),
        (col_shift_hbm, col_shift),
        (usable_hbm, usable),
    )
    copies = [pltpu.make_async_copy(source, target, sems.at[i]) for i, (source, target) in enumerate(pairs)]
    for copy in copies:
        copy.start()
    colpass[:, :, 0:pad] = jnp.zeros((2, tiles, pad, LANES), jnp.float32)
    colpass[:, :, pad + rows : 2 * pad + rows] = jnp.zeros((2, tiles, pad, LANES), jnp.float32)
    params[...] = jnp.zeros_like(params)
    for copy in copies:
        copy.wait()
    row = lax.broadcasted_iota(jnp.int32, (exposures, 1), 0)
    kept = jnp.zeros((exposures, 1), jnp.int32)
    for e in range(exposures):
        kept = jnp.where(row == e, usable[e], kept)
    params[:, 0:vels] = row_shift[...].astype(jnp.float32)
    params[:, vels : 2 * vels] = col_shift[...].astype(jnp.float32)
    params[:, 2 * vels : 2 * vels + 1] = kept.astype(jnp.float32)
    parts = rows // SHIFT

    def row_tap(e, a):
        return row_taps[e, a]

    def col_tap(e, b):
        return col_taps[e, b]

    def one_exposure(e, carry):
        for a in range(taps):
            tap_rows[e, a : a + 1] = jnp.full((1, LANES), row_taps[e, a])
            tap_rows[e, taps + a : taps + a + 1] = jnp.full((1, LANES), col_taps[e, a])
        inverse_all = inv_var[e].astype(jnp.float32)
        product_all = science[e].astype(jnp.float32) * inverse_all
        for g in range(rows // SUBLANES):
            at = slice(g * SUBLANES, (g + 1) * SUBLANES)
            for m, picture in ((0, product_all[at]), (1, inverse_all[at])):
                for t, total in enumerate(column_pass(picture, col_tap, taps, e, m == 1)):
                    colpass[m, t, pad + g * SUBLANES : pad + (g + 1) * SUBLANES] = total
        for p in range(parts):
            quarters = [
                row_pass(colpass, row_tap, e, m, pad + p * SHIFT + h * SUBLANES - radius, range(taps))
                for m in (0, 1)
                for h in (0, 1)
            ]
            for t in range(tiles):
                for q in range(4):
                    at = p * exposures * 2 * SHIFT + e * 2 * SHIFT + q * SUBLANES
                    maps[t, pl.ds(pl.multiple_of(at, SUBLANES), SUBLANES)] = quarters[q][t]
                at = p * exposures * SUBLANES + e * SUBLANES
                edges[t, pl.ds(pl.multiple_of(at, SUBLANES), SUBLANES)] = pack_edges(quarters, t)
        return carry

    lax.fori_loop(0, exposures, one_exposure, 0, unroll=2)


def outer_kernel(
    radius, chunks, info, maps, edges, params, tap_rows, above, below, *rest
):
    exposures = params.shape[0]
    tiles = maps.shape[0]
    parts = edges.shape[1] // (exposures * SUBLANES)
    sends, (pixels, colpass, more, more_edges) = rest[: chunks * parts], rest[chunks * parts :]
    taps = 2 * radius + 1
    pad = SUBLANES
    has_above, has_below, own = info[0] > 0, info[1] > 0, info[2]

    colpass[...] = jnp.zeros_like(colpass)

    def row_tap(e, a):
        return tap_rows[e, a : a + 1]

    def col_tap(e, b):
        return tap_rows[e, taps + b : taps + b + 1]

    def one_exposure(e, carry):
        for kind in (0, 1):
            pixels[kind, 0:radius] = jnp.where(has_below, below[kind, e].astype(jnp.float32), 0.0)
            pixels[kind, radius : 2 * radius] = jnp.where(has_above, above[kind, e].astype(jnp.float32), 0.0)
        inverse = pixels[1]
        product = pixels[0] * inverse
        for m, picture in ((0, product), (1, inverse)):
            for t, total in enumerate(column_pass(picture, col_tap, taps, e, m == 1)):
                colpass[m, t, pad : pad + SUBLANES] = total
        upper = [row_pass(colpass, row_tap, e, m, pad + radius, range(radius)) for m in (0, 1)]
        lower = [row_pass(colpass, row_tap, e, m, -radius, range(radius + 1, taps)) for m in (0, 1)]
        for t in range(tiles):
            for m in (0, 1):
                more[0, t, 2 * e + m] = upper[m][t]
                more[1, t, 2 * e + m] = lower[m][t]
            more_edges[0, t, e] = pack_edges([upper[0], None, upper[1], None], t)
            more_edges[1, t, e] = pack_edges([None, lower[0], None, lower[1]], t)
        return carry

    lax.fori_loop(0, exposures, one_exposure, 0, unroll=4)
    main = exposures * 2 * SHIFT
    for step in range(chunks):
        to = partner(own, step, chunks)
        for p in range(parts):
            out = sends[step * parts + p]
            for k in range(2 * exposures):
                first = maps[to, p * main + k * SHIFT : p * main + k * SHIFT + SUBLANES]
                second = maps[to, p * main + k * SHIFT + SUBLANES : p * main + (k + 1) * SHIFT]
                if p == 0:
                    first = first + more[0, to, k]
                if p == parts - 1:
                    second = second + more[1, to, k]
                out[k * SHIFT : (k + 1) * SHIFT] = jnp.concatenate([first, second]).astype(jnp.bfloat16)
            packed = edges[to, p * exposures * SUBLANES : (p + 1) * exposures * SUBLANES]
            if p == 0:
                packed = packed + more_edges[0, to].reshape(packed.shape)
            if p == parts - 1:
                packed = packed + more_edges[1, to].reshape(packed.shape)
            out[main : main + exposures * SUBLANES] = packed.astype(jnp.bfloat16)
            if p == parts - 1:
                tail = main + exposures * SUBLANES
                out[tail : tail + exposures] = params[...].astype(jnp.bfloat16)


def unpack_all(blocks, kept_as, main, side, exposures):
    main_rows = exposures * 2 * SHIFT
    size = main_rows + exposures * SUBLANES
    for g, group in enumerate(blocks):
        for q in range(4):
            turned = []
            for block in group:
                packed = block[main_rows:size]
                piece = packed if q == 0 else pltpu.roll(packed, LANES - 2 * SHIFT * q, 1)
                turned.append(piece.astype(jnp.float32))
            for p, piece in enumerate(kept_as(turned)):
                at = p * SHIFT + (q % 2) * SUBLANES
                for e in range(exposures):
                    side[g * exposures + e, q // 2, at : at + SUBLANES] = piece[e * SUBLANES : (e + 1) * SUBLANES]
        for k in range(2 * exposures):
            cells = [block[k * SHIFT : (k + 1) * SHIFT].astype(jnp.float32) for block in group]
            for p, piece in enumerate(kept_as(cells)):
                main[g * exposures + k // 2, k % 2, p * SHIFT : (p + 1) * SHIFT] = piece


def stack_kernel(groups, per_group, exposures, vels, halves, info, *rest):
    blocks = [[rest[p * groups + g] for p in range(per_group)] for g in range(groups)]
    rest = rest[per_group * groups :]
    main, side, even, odd, whole_params, scalars, order, result, sem = rest[-9:]
    outs = rest[:-9]
    windows = (even, odd)
    own_sub, first_vel = info[3], info[4]
    share, rows = result.shape[0], result.shape[1]
    size = exposures * (2 * SHIFT + SUBLANES)
    total = groups * exposures
    whole_params[total:] = jnp.zeros((exposures, LANES), jnp.int32)
    for g in range(groups):
        whole_params[g * exposures : (g + 1) * exposures] = (
            blocks[g][1][size : size + exposures].astype(jnp.float32).astype(jnp.int32)
        )
    fetch = pltpu.make_async_copy(whole_params, scalars, sem)
    fetch.start()
    has_below = info[1] > 0
    if halves:
        second = own_sub > 0
        valid = has_below | (own_sub == 0)

        def kept_as(cells):
            outer, inner = jnp.where(valid, cells[0], 0.0), cells[1]
            return jnp.where(second, inner, outer), jnp.where(second, outer, inner)

    else:

        def kept_as(cells):
            return *cells[:-1], jnp.where(has_below, cells[-1], 0.0)

    unpack_all(blocks, kept_as, main, side, exposures)
    main[total] = jnp.zeros(main.shape[1:], jnp.float32)
    side[total] = jnp.zeros(side.shape[1:], jnp.float32)
    fetch.wait()
    filled = jnp.int32(0)
    for source in range(total):
        order[filled] = source
        filled = filled + scalars[source, 2 * vels]
    for i in range(UNROLL):
        order[filled + i] = total
    trips = (filled + UNROLL - 1) // UNROLL

    lane = lax.broadcasted_iota(jnp.int32, (rows, LANES), 1)

    def gather(v, e, sums):
        source = order[e]
        row_at = scalars[source, first_vel + v]
        col_at = scalars[source, vels + first_vel + v] + SHIFT
        from_side = lane < col_at
        cells = jnp.concatenate(
            [
                jnp.where(from_side, side[source, m, pl.ds(row_at, rows)], main[source, m, pl.ds(row_at, rows)])
                for m in (0, 1)
            ]
        ).astype(jnp.bfloat16)
        cells = pltpu.roll(cells, (LANES - col_at) & (LANES - 1), 1).astype(jnp.float32)
        windows[v % 2][e, 0] = cells[:rows]
        windows[v % 2][e, 1] = cells[rows:]
        return sums[0] + cells[:rows], sums[1] + cells[rows:]

    def reweigh(v, e, flux, sums):
        signal = windows[v % 2][e, 0]
        depth = windows[v % 2][e, 1]
        residual = signal - flux * depth
        base = depth + 1.0
        weight = base / (base + residual * residual)
        return sums[0] + weight * signal, sums[1] + weight * depth

    def over_exposures(step, start):
        def trip(t, sums):
            for i in range(UNROLL):
                sums = step(t * UNROLL + i, sums)
            return sums

        return lax.fori_loop(0, trips, trip, start)

    zeros = main[total, 0, 0:rows]
    none = (zeros, zeros)

    sums = over_exposures(functools.partial(gather, 0), none)
    for v in range(share):
        flux = sums[0] / (sums[1] + 1.0)

        def weigh(e, sums, v=v, flux=flux):
            return reweigh(v, e, flux, sums)

        def both(e, sums, v=v, weigh=weigh):
            return gather(v + 1, e, sums[:2]) + weigh(e, sums[2:])

        if v + 1 < share:
            sums = over_exposures(both, none + none)
        else:
            sums = none + over_exposures(weigh, none)
        result[v] = sums[2] / jnp.sqrt(sums[3] + 1.0)
    block = rows // len(outs)
    for step, out in enumerate(outs):
        to = partner(info[2], step, len(outs))
        out[...] = result[:, pl.ds(pl.multiple_of(to * block, block), block)]


def rows_kernel(chunks, info, *rest):
    pieces = rest[:chunks]
    out, held = rest[chunks:]
    for step in range(chunks):
        held[step] = pieces[step][...]
    own = (info[2] * 2 + info[3]) % chunks
    for c in range(chunks):
        out[:, :, c * LANES : (c + 1) * LANES] = held[partner(own, c, chunks)]


def columns_kernel(chunks, subs, info, *rest):
    pieces = rest[:chunks]
    outs = rest[chunks : chunks + subs]
    held, wide = rest[chunks + subs :]
    own_chunk, own_sub = info[2], info[3]
    for step in range(chunks):
        held[step] = pieces[step][...]
    rows = wide.shape[2]
    for c in range(chunks):
        piece = held[partner(own_chunk, c, chunks)]
        for k in range(subs):
            wide[k, :, :, c * LANES : (c + 1) * LANES] = piece[:, k * rows : (k + 1) * rows]
    for step in range(subs):
        outs[step][...] = wide[partner(own_sub, step, subs)]


def velocities_kernel(subs, info, *rest):
    pieces = rest[:subs]
    out, held = rest[subs:]
    own_sub = info[3]
    for step in range(subs):
        held[step] = pieces[step][...]
    share = held.shape[1]
    for k in range(subs):
        out[k * share : (k + 1) * share] = held[partner(own_sub, k, subs)]


def per_device(*arguments):
    science, inv_var, psf_rows, psf_cols, row_shift, col_shift, exposure_ok = arguments
    exposures, rows, columns = science.shape
    vels = row_shift.shape[1]
    radius = psf_rows.shape[1] // 2
    strips = lax.axis_size("strip")
    members = lax.axis_size("expo")
    chunks = columns // LANES
    subs = members // chunks
    share = vels // subs
    parts = rows // SHIFT
    strip = lax.axis_index("strip")
    me = lax.axis_index("expo")
    own_chunk = me // subs
    own_sub = me % subs
    first_vel = 0 if split_rows(subs, parts) else own_sub * share
    info = jnp.stack([strip > 0, strip < strips - 1, own_chunk, own_sub, first_vel]).astype(jnp.int32)

    def rows_from(start):
        return jnp.stack([lax.dynamic_slice_in_dim(x, start, radius, 1) for x in (science, inv_var)])

    if strips == 2:
        met = rows_from(jnp.where(strip == 0, rows - radius, 0))
        above = below = lax.ppermute(met, "strip", [(0, 1), (1, 0)])
    else:
        above = lax.ppermute(rows_from(rows - radius), "strip", [(i, i + 1) for i in range(strips - 1)])
        below = lax.ppermute(rows_from(0), "strip", [(i + 1, i) for i in range(strips - 1)])

    map_rows = parts * exposures * 2 * SHIFT
    tap_room = -(-2 * psf_rows.shape[1] // SUBLANES) * SUBLANES
    edge_rows = parts * exposures * SUBLANES
    maps, edges, params, tap_rows = pl.pallas_call(
        functools.partial(inner_kernel, radius),
        out_shape=[
            jax.ShapeDtypeStruct((chunks, map_rows, LANES), jnp.float32),
            jax.ShapeDtypeStruct((chunks, edge_rows, LANES), jnp.float32),
            jax.ShapeDtypeStruct((exposures, LANES), jnp.float32),
            jax.ShapeDtypeStruct((exposures, tap_room, LANES), jnp.float32),
        ],
        in_specs=[HBM] * 7,
        out_specs=[VMEM] * 4,
        scratch_shapes=[
            pltpu.VMEM(science.shape, science.dtype),
            pltpu.VMEM(inv_var.shape, inv_var.dtype),
            pltpu.SMEM(psf_rows.shape, jnp.float32),
            pltpu.SMEM(psf_cols.shape, jnp.float32),
            pltpu.VMEM(row_shift.shape, jnp.int32),
            pltpu.VMEM(col_shift.shape, jnp.int32),
            pltpu.SMEM(exposure_ok.shape, jnp.int32),
            pltpu.VMEM((2, chunks, rows + 2 * SUBLANES, LANES), jnp.float32),
            pltpu.SemaphoreType.DMA((7,)),
        ],
        compiler_params=pltpu.CompilerParams(vmem_limit_bytes=8 << 20),
        cost_estimate=pl.CostEstimate(flops=100_000_000, bytes_accessed=4_000_000, transcendentals=0),
        name="filter_inner",
    )(*[pltpu.with_memory_space_constraint(x, pltpu.HBM) for x in arguments])
    block = exposures * (2 * SHIFT + SUBLANES)
    sent = [
        jax.ShapeDtypeStruct((block + (exposures if p == parts - 1 else 0), LANES), jnp.bfloat16)
        for p in range(parts)
    ]
    sends = pl.pallas_call(
        functools.partial(outer_kernel, radius, chunks),
        out_shape=sent * chunks,
        in_specs=[SMEM] + [VMEM] * 6,
        out_specs=[VMEM] * (chunks * parts),
        scratch_shapes=[
            pltpu.VMEM((2, 2 * radius, columns), jnp.float32),
            pltpu.VMEM((2, chunks, 3 * SUBLANES, LANES), jnp.float32),
            pltpu.VMEM((2, chunks, 2 * exposures, SUBLANES, LANES), jnp.float32),
            pltpu.VMEM((2, chunks, exposures, SUBLANES, LANES), jnp.float32),
        ],
        compiler_params=pltpu.CompilerParams(vmem_limit_bytes=8 << 20),
        name="filter_outer",
    )(info, maps, edges, params, tap_rows, above, below)

    halves = split_rows(subs, parts)
    arrived = []
    for step in range(chunks):
        arrived.append(
            [
                lax.ppermute(sends[step * parts + p], "expo", chunk_pairs(step, chunks, subs))
                if step
                else sends[p]
                for p in range(parts)
            ]
        )
    if halves:
        both = ("expo", "strip")
        same, cross = strip_pairs(strips, chunks)
        swap = sub_pairs(1, chunks, subs)
        outer = [lax.ppermute(arrived[s][0], both, same) for s in range(chunks)]
        outer += [lax.ppermute(arrived[s][0], both, cross) for s in range(chunks)]
        inner = [arrived[s][1] for s in range(chunks)]
        inner += [lax.ppermute(arrived[s][1], "expo", swap) for s in range(chunks)]
        blocks = [outer, inner]
        stacked_rows, share = rows // subs, vels
    else:
        up = [((i + 1) % strips, i) for i in range(strips)]
        blocks = [[block[p] for block in arrived] for p in range(parts)]
        blocks.append([lax.ppermute(arrived[step][0], "strip", up) for step in range(chunks)])
        for part in blocks:
            for u in range(1, subs):
                pairs = sub_pairs(u, chunks, subs)
                part += [lax.ppermute(part[step], "expo", pairs) for step in range(chunks)]
        stacked_rows = rows

    groups = len(blocks[0])
    block_rows = stacked_rows // chunks
    reach = stacked_rows + SHIFT
    piece = jax.ShapeDtypeStruct((share, block_rows, LANES), jnp.float32)
    total = groups * exposures
    pieces = pl.pallas_call(
        functools.partial(stack_kernel, groups, len(blocks), exposures, vels, halves),
        out_shape=[piece] * chunks,
        in_specs=[SMEM] + [VMEM] * (len(blocks) * groups),
        out_specs=[VMEM] * chunks,
        scratch_shapes=[
            pltpu.VMEM((total + 1, 2, reach, LANES), jnp.float32),
            pltpu.VMEM((total + 1, 2, reach, LANES), jnp.float32),
            pltpu.VMEM((total + UNROLL, 2, stacked_rows, LANES), jnp.float32),
            pltpu.VMEM((total + UNROLL, 2, stacked_rows, LANES), jnp.float32),
            pltpu.VMEM((total + exposures, LANES), jnp.int32),
            pltpu.SMEM((total + exposures, LANES), jnp.int32),
            pltpu.SMEM((total + UNROLL,), jnp.int32),
            pltpu.VMEM((share, stacked_rows, LANES), jnp.float32),
            pltpu.SemaphoreType.DMA(()),
        ],
        compiler_params=pltpu.CompilerParams(vmem_limit_bytes=24 << 20),
        name="stack_twice",
    )(info, *[block for part in blocks for block in part])

    if halves:
        held = [lax.ppermute(pieces[t], "expo", row_pairs(t, chunks)) for t in range(chunks)]
        likelihood = pl.pallas_call(
            functools.partial(rows_kernel, chunks),
            out_shape=jax.ShapeDtypeStruct((vels, block_rows, columns), jnp.float32),
            in_specs=[SMEM] + [VMEM] * chunks,
            out_specs=VMEM,
            scratch_shapes=[pltpu.VMEM((chunks, vels, block_rows, LANES), jnp.float32)],
            compiler_params=pltpu.CompilerParams(vmem_limit_bytes=1 << 20),
            name="join_rows",
        )(info, *held)
        return likelihood[None]

    held = [pieces[0]]
    for step in range(1, chunks):
        held.append(lax.ppermute(pieces[step], "expo", chunk_pairs(step, chunks, subs)))
    out_rows = block_rows // subs
    wide = jax.ShapeDtypeStruct((share, out_rows, columns), jnp.float32)
    parts = pl.pallas_call(
        functools.partial(columns_kernel, chunks, subs),
        out_shape=[wide] * subs,
        in_specs=[SMEM] + [VMEM] * chunks,
        out_specs=[VMEM] * subs,
        scratch_shapes=[
            pltpu.VMEM((chunks, share, block_rows, LANES), jnp.float32),
            pltpu.VMEM((subs, share, out_rows, columns), jnp.float32),
        ],
        compiler_params=pltpu.CompilerParams(vmem_limit_bytes=1 << 20),
        name="join_columns",
    )(info, *held)
    met = [parts[0]]
    for step in range(1, subs):
        met.append(lax.ppermute(parts[step], "expo", sub_pairs(step, chunks, subs)))
    likelihood = pl.pallas_call(
        functools.partial(velocities_kernel, subs),
        out_shape=jax.ShapeDtypeStruct((vels, out_rows, columns), jnp.float32),
        in_specs=[SMEM] + [VMEM] * subs,
        out_specs=VMEM,
        scratch_shapes=[pltpu.VMEM((subs, share, out_rows, columns), jnp.float32)],
        compiler_params=pltpu.CompilerParams(vmem_limit_bytes=1 << 20),
        name="join_velocities",
    )(info, *met)
    return likelihood[None]


def solution(mesh):
    in_specs = (
        P(("field", "expo"), "strip", None),
        P(("field", "expo"), "strip", None),
        P(("field", "expo"), None),
        P(("field", "expo"), None),
        P(("field", "expo"), None),
        P(("field", "expo"), None),
        P(("field", "expo")),
    )
    out_specs = P("strip", "field", "expo", None)

    return jax.shard_map(per_device, mesh=mesh, in_specs=in_specs, out_specs=out_specs, check_vma=False)
```

```python
import functools

import jax
import jax.numpy as jnp
from jax import lax
from jax.experimental import pallas as pl
from jax.experimental.pallas import tpu as pltpu
from jax.sharding import PartitionSpec as P

SHIFT = 16
LANES = 128
SUBLANES = 8
UNROLL = 16
TAIL = 4

SMEM = pl.BlockSpec(memory_space=pltpu.SMEM)
VMEM = pl.BlockSpec(memory_space=pltpu.VMEM)
HBM = pl.BlockSpec(memory_space=pltpu.HBM)


def partner(index, step, count):
    if count & (count - 1) == 0:
        return index ^ step
    return (index + step) % count


def chunk_pairs(step, chunks, subs):
    return [
        (j * subs + k, partner(j, step, chunks) * subs + k) for j in range(chunks) for k in range(subs)
    ]


def sub_pairs(step, chunks, subs):
    return [
        (j * subs + k, j * subs + partner(k, step, subs)) for j in range(chunks) for k in range(subs)
    ]


def column_pass(picture, col_tap, taps, e, square):
    tiles = picture.shape[1] // LANES
    lane = lax.broadcasted_iota(jnp.int32, (SUBLANES, LANES), 1)
    zero = jnp.zeros((SUBLANES, LANES), jnp.float32)
    cut = [picture[:, t * LANES : (t + 1) * LANES] for t in range(tiles)]
    totals = None
    for b in range(taps):
        step = b - taps // 2
        tap = col_tap(e, b)
        if square:
            tap = tap * tap
        moved = cut
        if step:
            turned = [pltpu.roll(c, (-step) % LANES, 1) for c in cut]
            if step > 0:
                turned = turned + [zero]
                moved = [jnp.where(lane < LANES - step, turned[t], turned[t + 1]) for t in range(tiles)]
            else:
                turned = [zero] + turned
                moved = [jnp.where(lane >= -step, turned[t + 1], turned[t]) for t in range(tiles)]
        terms = [tap * m for m in moved]
        totals = terms if totals is None else [x + y for x, y in zip(totals, terms)]
    return totals


def row_pass(colpass, row_tap, e, m, first, taps):
    tiles = colpass.shape[1]
    lane = lax.broadcasted_iota(jnp.int32, (SUBLANES, LANES), 1)
    zero = jnp.zeros((SUBLANES, LANES), jnp.float32)
    out = []
    for t in range(tiles):
        total = None
        for a in taps:
            tap = row_tap(e, a)
            if m == 1:
                tap = tap * tap
            term = tap * colpass[m, t, pl.ds(first + a, SUBLANES)]
            total = term if total is None else total + term
        out.append(pltpu.roll(total, SHIFT, 1))
    out = [zero] + out + [zero]
    return [jnp.where(lane < SHIFT, out[t], out[t + 1]) for t in range(tiles + 1)]


def pack_edges(quarters, t):
    lane = lax.broadcasted_iota(jnp.int32, (SUBLANES, LANES), 1)
    packed = jnp.zeros((SUBLANES, LANES), jnp.float32)
    for q, quarter in enumerate(quarters):
        if quarter is None:
            continue
        piece = quarter[t + 1] if q == 0 else pltpu.roll(quarter[t + 1], 2 * SHIFT * q, 1)
        inside = (lane >= 2 * SHIFT * q) & (lane < 2 * SHIFT * (q + 1))
        packed = jnp.where(inside, piece, packed)
    return packed


def inner_kernel(
    radius,
    science_hbm,
    inv_var_hbm,
    row_taps_hbm,
    col_taps_hbm,
    row_shift_hbm,
    col_shift_hbm,
    usable_hbm,
    maps,
    edges,
    params,
    tap_rows,
    science,
    inv_var,
    row_taps,
    col_taps,
    row_shift,
    col_shift,
    usable,
    colpass,
    sems,
):
    exposures, rows, columns = science.shape
    tiles = columns // LANES
    taps = 2 * radius + 1
    vels = row_shift.shape[1]
    pad = SUBLANES
    pairs = (
        (row_taps_hbm, row_taps),
        (col_taps_hbm, col_taps),
        (science_hbm, science),
        (inv_var_hbm, inv_var),
        (row_shift_hbm, row_shift),
        (col_shift_hbm, col_shift),
        (usable_hbm, usable),
    )
    copies = [pltpu.make_async_copy(source, target, sems.at[i]) for i, (source, target) in enumerate(pairs)]
    for copy in copies:
        copy.start()
    colpass[:, :, 0:pad] = jnp.zeros((2, tiles, pad, LANES), jnp.float32)
    colpass[:, :, pad + rows : 2 * pad + rows] = jnp.zeros((2, tiles, pad, LANES), jnp.float32)
    params[...] = jnp.zeros_like(params)
    for copy in copies:
        copy.wait()
    row = lax.broadcasted_iota(jnp.int32, (exposures, 1), 0)
    kept = jnp.zeros((exposures, 1), jnp.int32)
    for e in range(exposures):
        kept = jnp.where(row == e, usable[e], kept)
    params[:, 0:vels] = row_shift[...].astype(jnp.float32)
    params[:, vels : 2 * vels] = col_shift[...].astype(jnp.float32)
    params[:, 2 * vels : 2 * vels + 1] = kept.astype(jnp.float32)
    parts = rows // SHIFT

    def row_tap(e, a):
        return row_taps[e, a]

    def col_tap(e, b):
        return col_taps[e, b]

    def one_exposure(e, carry):
        for a in range(taps):
            tap_rows[e, a : a + 1] = jnp.full((1, LANES), row_taps[e, a])
            tap_rows[e, taps + a : taps + a + 1] = jnp.full((1, LANES), col_taps[e, a])
        inverse_all = inv_var[e].astype(jnp.float32)
        product_all = science[e].astype(jnp.float32) * inverse_all
        for g in range(rows // SUBLANES):
            at = slice(g * SUBLANES, (g + 1) * SUBLANES)
            for m, picture in ((0, product_all[at]), (1, inverse_all[at])):
                for t, total in enumerate(column_pass(picture, col_tap, taps, e, m == 1)):
                    colpass[m, t, pad + g * SUBLANES : pad + (g + 1) * SUBLANES] = total
        for p in range(parts):
            quarters = [
                row_pass(colpass, row_tap, e, m, pad + p * SHIFT + h * SUBLANES - radius, range(taps))
                for m in (0, 1)
                for h in (0, 1)
            ]
            for t in range(tiles):
                for q in range(4):
                    at = p * exposures * 2 * SHIFT + e * 2 * SHIFT + q * SUBLANES
                    maps[t, pl.ds(pl.multiple_of(at, SUBLANES), SUBLANES)] = quarters[q][t]
                at = p * exposures * SUBLANES + e * SUBLANES
                edges[t, pl.ds(pl.multiple_of(at, SUBLANES), SUBLANES)] = pack_edges(quarters, t)
        return carry

    lax.fori_loop(0, exposures, one_exposure, 0, unroll=2)


def outer_kernel(
    radius, chunks, info, maps, edges, params, tap_rows, above, below, *rest
):
    exposures = params.shape[0]
    tiles = maps.shape[0]
    parts = edges.shape[1] // (exposures * SUBLANES)
    sends, (pixels, colpass, more, more_edges) = rest[: chunks * parts], rest[chunks * parts :]
    taps = 2 * radius + 1
    pad = SUBLANES
    has_above, has_below, own = info[0] > 0, info[1] > 0, info[2]

    colpass[...] = jnp.zeros_like(colpass)

    def row_tap(e, a):
        return tap_rows[e, a : a + 1]

    def col_tap(e, b):
        return tap_rows[e, taps + b : taps + b + 1]

    def one_exposure(e, carry):
        for kind in (0, 1):
            pixels[kind, 0:radius] = jnp.where(has_below, below[kind, e].astype(jnp.float32), 0.0)
            pixels[kind, radius : 2 * radius] = jnp.where(has_above, above[kind, e].astype(jnp.float32), 0.0)
        inverse = pixels[1]
        product = pixels[0] * inverse
        for m, picture in ((0, product), (1, inverse)):
            for t, total in enumerate(column_pass(picture, col_tap, taps, e, m == 1)):
                colpass[m, t, pad : pad + SUBLANES] = total
        upper = [row_pass(colpass, row_tap, e, m, pad + radius, range(radius)) for m in (0, 1)]
        lower = [row_pass(colpass, row_tap, e, m, -radius, range(radius + 1, taps)) for m in (0, 1)]
        for t in range(tiles):
            for m in (0, 1):
                more[0, t, 2 * e + m] = upper[m][t]
                more[1, t, 2 * e + m] = lower[m][t]
            more_edges[0, t, e] = pack_edges([upper[0], None, upper[1], None], t)
            more_edges[1, t, e] = pack_edges([None, lower[0], None, lower[1]], t)
        return carry

    lax.fori_loop(0, exposures, one_exposure, 0, unroll=4)
    main = exposures * 2 * SHIFT
    for step in range(chunks):
        to = partner(own, step, chunks)
        for p in range(parts):
            out = sends[step * parts + p]
            for k in range(2 * exposures):
                first = maps[to, p * main + k * SHIFT : p * main + k * SHIFT + SUBLANES]
                second = maps[to, p * main + k * SHIFT + SUBLANES : p * main + (k + 1) * SHIFT]
                if p == 0:
                    first = first + more[0, to, k]
                if p == parts - 1:
                    second = second + more[1, to, k]
                out[k * SHIFT : (k + 1) * SHIFT] = jnp.concatenate([first, second]).astype(jnp.bfloat16)
            packed = edges[to, p * exposures * SUBLANES : (p + 1) * exposures * SUBLANES]
            if p == 0:
                packed = packed + more_edges[0, to].reshape(packed.shape)
            if p == parts - 1:
                packed = packed + more_edges[1, to].reshape(packed.shape)
            out[main : main + exposures * SUBLANES] = packed.astype(jnp.bfloat16)
            if p == parts - 1:
                tail = main + exposures * SUBLANES
                out[tail : tail + exposures] = params[...].astype(jnp.bfloat16)


def stack_kernel(groups, chunks, exposures, rows, vels, info, *rest):
    parts = rows // SHIFT
    blocks = [rest[p * groups : (p + 1) * groups] for p in range(parts + 1)]
    rest = rest[(parts + 1) * groups :]
    outs = rest[:chunks]
    main, side, even, odd, whole_params, scalars, order, result, sem = rest[chunks:]
    windows = (even, odd)
    own = info[2]
    first_vel = info[4]
    share = result.shape[0]
    main_rows = exposures * 2 * SHIFT
    size = main_rows + exposures * SUBLANES
    total = groups * exposures
    whole_params[total:] = jnp.zeros((exposures, LANES), jnp.int32)
    for g in range(groups):
        whole_params[g * exposures : (g + 1) * exposures] = (
            blocks[parts - 1][g][size : size + exposures].astype(jnp.float32).astype(jnp.int32)
        )
    fetch = pltpu.make_async_copy(whole_params, scalars, sem)
    fetch.start()
    has_below = info[1].astype(jnp.float32)
    for g in range(groups):
        for p in range(parts + 1):
            packed = blocks[p][g][main_rows:size]
            for q in range(4):
                piece = packed if q == 0 else pltpu.roll(packed, LANES - 2 * SHIFT * q, 1)
                piece = piece.astype(jnp.float32)
                if p == parts:
                    piece = piece * has_below
                at = p * SHIFT + (q % 2) * SUBLANES
                for e in range(exposures):
                    side[g * exposures + e, q // 2, at : at + SUBLANES] = piece[e * SUBLANES : (e + 1) * SUBLANES]
            for k in range(2 * exposures):
                cells = blocks[p][g][k * SHIFT : (k + 1) * SHIFT].astype(jnp.float32)
                if p == parts:
                    cells = cells * has_below
                main[g * exposures + k // 2, k % 2, p * SHIFT : (p + 1) * SHIFT] = cells
    main[total] = jnp.zeros(main.shape[1:], jnp.float32)
    side[total] = jnp.zeros(side.shape[1:], jnp.float32)
    fetch.wait()
    filled = jnp.int32(0)
    for source in range(total):
        order[filled] = source
        filled = filled + scalars[source, 2 * vels]
    for i in range(TAIL):
        order[filled + i] = total
    trips = filled // UNROLL
    tail_trips = (filled - trips * UNROLL + TAIL - 1) // TAIL

    lane = lax.broadcasted_iota(jnp.int32, (rows, LANES), 1)

    def gather(v, e, sums):
        source = order[e]
        row_at = scalars[source, first_vel + v]
        col_at = scalars[source, vels + first_vel + v] + SHIFT
        from_side = lane < col_at
        cells = jnp.concatenate(
            [
                jnp.where(from_side, side[source, m, pl.ds(row_at, rows)], main[source, m, pl.ds(row_at, rows)])
                for m in (0, 1)
            ]
        ).astype(jnp.bfloat16)
        cells = pltpu.roll(cells, (LANES - col_at) & (LANES - 1), 1).astype(jnp.float32)
        windows[v % 2][e, 0] = cells[:rows]
        windows[v % 2][e, 1] = cells[rows:]
        return sums[0] + cells[:rows], sums[1] + cells[rows:]

    def reweigh(v, e, flux, sums):
        signal = windows[v % 2][e, 0]
        depth = windows[v % 2][e, 1]
        residual = signal - flux * depth
        base = depth + 1.0
        weight = base / (base + residual * residual)
        return sums[0] + weight * signal, sums[1] + weight * depth

    def over_exposures(step, start):
        def trip(t, sums):
            for i in range(UNROLL):
                sums = step(t * UNROLL + i, sums)
            return sums

        def tail_trip(t, sums):
            for i in range(TAIL):
                sums = step(trips * UNROLL + t * TAIL + i, sums)
            return sums

        return lax.fori_loop(0, tail_trips, tail_trip, lax.fori_loop(0, trips, trip, start))

    zeros = main[total, 0, 0:rows]
    none = (zeros, zeros)

    sums = over_exposures(functools.partial(gather, 0), none)
    for v in range(share):
        flux = sums[0] / (sums[1] + 1.0)

        def weigh(e, sums, v=v, flux=flux):
            return reweigh(v, e, flux, sums)

        def both(e, sums, v=v, weigh=weigh):
            return gather(v + 1, e, sums[:2]) + weigh(e, sums[2:])

        if v + 1 < share:
            sums = over_exposures(both, none + none)
        else:
            sums = none + over_exposures(weigh, none)
        result[v] = sums[2] / jnp.sqrt(sums[3] + 1.0)
    block = rows // chunks
    for step in range(chunks):
        to = partner(own, step, chunks)
        outs[step][...] = result[:, pl.ds(pl.multiple_of(to * block, block), block)]


def join_kernel(chunks, subs, info, *rest):
    pieces = rest[: chunks * subs]
    out, held = rest[chunks * subs :]
    own_chunk, own_sub = info[2], info[3]
    share, rows = held.shape[2], out.shape[1]
    for u in range(subs):
        for step in range(chunks):
            held[u, step] = pieces[u * chunks + step][...]
    for k in range(subs):
        for c in range(chunks):
            block = held.at[partner(own_sub, k, subs), partner(own_chunk, c, chunks)]
            for v in range(share):
                out[k * share + v, :, c * LANES : (c + 1) * LANES] = block[v, pl.ds(own_sub * rows, rows)]


def per_device(*arguments):
    science, inv_var, psf_rows, psf_cols, row_shift, col_shift, exposure_ok = arguments
    exposures, rows, columns = science.shape
    vels = row_shift.shape[1]
    radius = psf_rows.shape[1] // 2
    strips = lax.axis_size("strip")
    members = lax.axis_size("expo")
    chunks = columns // LANES
    subs = members // chunks
    share = vels // subs
    parts = rows // SHIFT
    strip = lax.axis_index("strip")
    me = lax.axis_index("expo")
    own_chunk = me // subs
    own_sub = me % subs
    info = jnp.stack([strip > 0, strip < strips - 1, own_chunk, own_sub, own_sub * share]).astype(jnp.int32)

    def rows_from(start):
        return jnp.stack([lax.dynamic_slice_in_dim(x, start, radius, 1) for x in (science, inv_var)])

    if strips == 2:
        met = rows_from(jnp.where(strip == 0, rows - radius, 0))
        above = below = lax.ppermute(met, "strip", [(0, 1), (1, 0)])
    else:
        above = lax.ppermute(rows_from(rows - radius), "strip", [(i, i + 1) for i in range(strips - 1)])
        below = lax.ppermute(rows_from(0), "strip", [(i + 1, i) for i in range(strips - 1)])

    map_rows = parts * exposures * 2 * SHIFT
    tap_room = -(-2 * psf_rows.shape[1] // SUBLANES) * SUBLANES
    edge_rows = parts * exposures * SUBLANES
    maps, edges, params, tap_rows = pl.pallas_call(
        functools.partial(inner_kernel, radius),
        out_shape=[
            jax.ShapeDtypeStruct((chunks, map_rows, LANES), jnp.float32),
            jax.ShapeDtypeStruct((chunks, edge_rows, LANES), jnp.float32),
            jax.ShapeDtypeStruct((exposures, LANES), jnp.float32),
            jax.ShapeDtypeStruct((exposures, tap_room, LANES), jnp.float32),
        ],
        in_specs=[HBM] * 7,
        out_specs=[VMEM] * 4,
        scratch_shapes=[
            pltpu.VMEM(science.shape, science.dtype),
            pltpu.VMEM(inv_var.shape, inv_var.dtype),
            pltpu.SMEM(psf_rows.shape, jnp.float32),
            pltpu.SMEM(psf_cols.shape, jnp.float32),
            pltpu.VMEM(row_shift.shape, jnp.int32),
            pltpu.VMEM(col_shift.shape, jnp.int32),
            pltpu.SMEM(exposure_ok.shape, jnp.int32),
            pltpu.VMEM((2, chunks, rows + 2 * SUBLANES, LANES), jnp.float32),
            pltpu.SemaphoreType.DMA((7,)),
        ],
        compiler_params=pltpu.CompilerParams(vmem_limit_bytes=8 << 20),
        cost_estimate=pl.CostEstimate(flops=100_000_000, bytes_accessed=4_000_000, transcendentals=0),
        name="filter_inner",
    )(*[pltpu.with_memory_space_constraint(x, pltpu.HBM) for x in arguments])
    block = exposures * (2 * SHIFT + SUBLANES)
    sent = [
        jax.ShapeDtypeStruct((block + (exposures if p == parts - 1 else 0), LANES), jnp.bfloat16)
        for p in range(parts)
    ]
    sends = pl.pallas_call(
        functools.partial(outer_kernel, radius, chunks),
        out_shape=sent * chunks,
        in_specs=[SMEM] + [VMEM] * 6,
        out_specs=[VMEM] * (chunks * parts),
        scratch_shapes=[
            pltpu.VMEM((2, 2 * radius, columns), jnp.float32),
            pltpu.VMEM((2, chunks, 3 * SUBLANES, LANES), jnp.float32),
            pltpu.VMEM((2, chunks, 2 * exposures, SUBLANES, LANES), jnp.float32),
            pltpu.VMEM((2, chunks, exposures, SUBLANES, LANES), jnp.float32),
        ],
        compiler_params=pltpu.CompilerParams(vmem_limit_bytes=8 << 20),
        name="filter_outer",
    )(info, maps, edges, params, tap_rows, above, below)

    blocks = [[[None] * chunks for _ in range(subs)] for _ in range(parts + 1)]
    up = [((i + 1) % strips, i) for i in range(strips)]
    for step in range(chunks):
        for p in range(parts):
            blocks[p][0][step] = sends[step * parts + p]
            if step:
                blocks[p][0][step] = lax.ppermute(sends[step * parts + p], "expo", chunk_pairs(step, chunks, subs))
        blocks[parts][0][step] = lax.ppermute(blocks[0][0][step], "strip", up)
    for p in range(parts + 1):
        for u in range(1, subs):
            for step in range(chunks):
                blocks[p][u][step] = lax.ppermute(blocks[p][0][step], "expo", sub_pairs(u, chunks, subs))
    blocks = [[block for sub in part for block in sub] for part in blocks]

    groups = len(blocks[0])
    block_rows = rows // chunks
    reach = rows + SHIFT
    piece = jax.ShapeDtypeStruct((share, block_rows, LANES), jnp.float32)
    total = groups * exposures
    pieces = pl.pallas_call(
        functools.partial(stack_kernel, groups, chunks, exposures, rows, vels),
        out_shape=[piece] * chunks,
        in_specs=[SMEM] + [VMEM] * ((parts + 1) * groups),
        out_specs=[VMEM] * chunks,
        scratch_shapes=[
            pltpu.VMEM((total + 1, 2, reach, LANES), jnp.float32),
            pltpu.VMEM((total + 1, 2, reach, LANES), jnp.float32),
            pltpu.VMEM((total + UNROLL, 2, rows, LANES), jnp.float32),
            pltpu.VMEM((total + UNROLL, 2, rows, LANES), jnp.float32),
            pltpu.VMEM((total + exposures, LANES), jnp.int32),
            pltpu.SMEM((total + exposures, LANES), jnp.int32),
            pltpu.SMEM((total + UNROLL,), jnp.int32),
            pltpu.VMEM((share, rows, LANES), jnp.float32),
            pltpu.SemaphoreType.DMA(()),
        ],
        compiler_params=pltpu.CompilerParams(vmem_limit_bytes=24 << 20),
        name="stack_twice",
    )(info, *[block for part in blocks for block in part])

    held = [pieces[0]]
    for step in range(1, chunks):
        held.append(lax.ppermute(pieces[step], "expo", chunk_pairs(step, chunks, subs)))
    groups = [held]
    for u in range(1, subs):
        pairs = sub_pairs(u, chunks, subs)
        groups.append([lax.ppermute(held[step], "expo", pairs) for step in range(chunks)])
    out_rows = block_rows // subs
    likelihood = pl.pallas_call(
        functools.partial(join_kernel, chunks, subs),
        out_shape=jax.ShapeDtypeStruct((vels, out_rows, columns), jnp.float32),
        in_specs=[SMEM] + [VMEM] * (chunks * subs),
        out_specs=VMEM,
        scratch_shapes=[pltpu.VMEM((subs, chunks, share, block_rows, LANES), jnp.float32)],
        compiler_params=pltpu.CompilerParams(vmem_limit_bytes=2 << 20),
        name="join_all",
    )(info, *[block for group in groups for block in group])
    return likelihood[None]


def solution(mesh):
    in_specs = (
        P(("field", "expo"), "strip", None),
        P(("field", "expo"), "strip", None),
        P(("field", "expo"), None),
        P(("field", "expo"), None),
        P(("field", "expo"), None),
        P(("field", "expo"), None),
        P(("field", "expo")),
    )
    out_specs = P("strip", "field", "expo", None)

    return jax.shard_map(per_device, mesh=mesh, in_specs=in_specs, out_specs=out_specs, check_vma=False)
```

```python
import functools

import jax
import jax.numpy as jnp
from jax import lax
from jax.experimental import pallas as pl
from jax.experimental.pallas import tpu as pltpu
from jax.sharding import PartitionSpec as P

SHIFT = 16
LANES = 128
SUBLANES = 8
UNROLL = 18

SMEM = pl.BlockSpec(memory_space=pltpu.SMEM)
VMEM = pl.BlockSpec(memory_space=pltpu.VMEM)
HBM = pl.BlockSpec(memory_space=pltpu.HBM)


def partner(index, step, count):
    if count & (count - 1) == 0:
        return index ^ step
    return (index + step) % count


def chunk_pairs(step, chunks, subs):
    return [
        (j * subs + k, partner(j, step, chunks) * subs + k) for j in range(chunks) for k in range(subs)
    ]


def sub_pairs(step, chunks, subs):
    return [
        (j * subs + k, j * subs + partner(k, step, subs)) for j in range(chunks) for k in range(subs)
    ]


def column_pass(picture, col_tap, taps, e, square):
    tiles = picture.shape[1] // LANES
    lane = lax.broadcasted_iota(jnp.int32, (SUBLANES, LANES), 1)
    zero = jnp.zeros((SUBLANES, LANES), jnp.float32)
    cut = [picture[:, t * LANES : (t + 1) * LANES] for t in range(tiles)]
    totals = None
    for b in range(taps):
        step = b - taps // 2
        tap = col_tap(e, b)
        if square:
            tap = tap * tap
        moved = cut
        if step:
            turned = [pltpu.roll(c, (-step) % LANES, 1) for c in cut]
            if step > 0:
                turned = turned + [zero]
                moved = [jnp.where(lane < LANES - step, turned[t], turned[t + 1]) for t in range(tiles)]
            else:
                turned = [zero] + turned
                moved = [jnp.where(lane >= -step, turned[t + 1], turned[t]) for t in range(tiles)]
        terms = [tap * m for m in moved]
        totals = terms if totals is None else [x + y for x, y in zip(totals, terms)]
    return totals


def row_pass(colpass, row_tap, e, m, first, taps):
    tiles = colpass.shape[1]
    lane = lax.broadcasted_iota(jnp.int32, (SUBLANES, LANES), 1)
    zero = jnp.zeros((SUBLANES, LANES), jnp.float32)
    out = []
    for t in range(tiles):
        total = None
        for a in taps:
            tap = row_tap(e, a)
            if m == 1:
                tap = tap * tap
            term = tap * colpass[m, t, pl.ds(first + a, SUBLANES)]
            total = term if total is None else total + term
        out.append(pltpu.roll(total, SHIFT, 1))
    out = [zero] + out + [zero]
    return [jnp.where(lane < SHIFT, out[t], out[t + 1]) for t in range(tiles + 1)]


def pack_edges(quarters, t):
    lane = lax.broadcasted_iota(jnp.int32, (SUBLANES, LANES), 1)
    packed = jnp.zeros((SUBLANES, LANES), jnp.float32)
    for q, quarter in enumerate(quarters):
        if quarter is None:
            continue
        piece = quarter[t + 1] if q == 0 else pltpu.roll(quarter[t + 1], 2 * SHIFT * q, 1)
        inside = (lane >= 2 * SHIFT * q) & (lane < 2 * SHIFT * (q + 1))
        packed = jnp.where(inside, piece, packed)
    return packed


def inner_kernel(
    radius,
    science_hbm,
    inv_var_hbm,
    row_taps_hbm,
    col_taps_hbm,
    row_shift_hbm,
    col_shift_hbm,
    usable_hbm,
    maps,
    edges,
    params,
    tap_rows,
    science,
    inv_var,
    row_taps,
    col_taps,
    row_shift,
    col_shift,
    usable,
    colpass,
    sems,
):
    exposures, rows, columns = science.shape
    tiles = columns // LANES
    taps = 2 * radius + 1
    vels = row_shift.shape[1]
    pad = SUBLANES
    pairs = (
        (row_taps_hbm, row_taps),
        (col_taps_hbm, col_taps),
        (science_hbm, science),
        (inv_var_hbm, inv_var),
        (row_shift_hbm, row_shift),
        (col_shift_hbm, col_shift),
        (usable_hbm, usable),
    )
    copies = [pltpu.make_async_copy(source, target, sems.at[i]) for i, (source, target) in enumerate(pairs)]
    for copy in copies:
        copy.start()
    colpass[:, :, 0:pad] = jnp.zeros((2, tiles, pad, LANES), jnp.float32)
    colpass[:, :, pad + rows : 2 * pad + rows] = jnp.zeros((2, tiles, pad, LANES), jnp.float32)
    params[...] = jnp.zeros_like(params)
    for copy in copies:
        copy.wait()
    row = lax.broadcasted_iota(jnp.int32, (exposures, 1), 0)
    kept = jnp.zeros((exposures, 1), jnp.int32)
    for e in range(exposures):
        kept = jnp.where(row == e, usable[e], kept)
    params[:, 0:vels] = row_shift[...].astype(jnp.float32)
    params[:, vels : 2 * vels] = col_shift[...].astype(jnp.float32)
    params[:, 2 * vels : 2 * vels + 1] = kept.astype(jnp.float32)
    parts = rows // SHIFT

    def row_tap(e, a):
        return row_taps[e, a]

    def col_tap(e, b):
        return col_taps[e, b]

    def one_exposure(e, carry):
        for a in range(taps):
            tap_rows[e, a : a + 1] = jnp.full((1, LANES), row_taps[e, a])
            tap_rows[e, taps + a : taps + a + 1] = jnp.full((1, LANES), col_taps[e, a])
        inverse_all = inv_var[e].astype(jnp.float32)
        product_all = science[e].astype(jnp.float32) * inverse_all
        for g in range(rows // SUBLANES):
            at = slice(g * SUBLANES, (g + 1) * SUBLANES)
            for m, picture in ((0, product_all[at]), (1, inverse_all[at])):
                for t, total in enumerate(column_pass(picture, col_tap, taps, e, m == 1)):
                    colpass[m, t, pad + g * SUBLANES : pad + (g + 1) * SUBLANES] = total
        for p in range(parts):
            quarters = [
                row_pass(colpass, row_tap, e, m, pad + p * SHIFT + h * SUBLANES - radius, range(taps))
                for m in (0, 1)
                for h in (0, 1)
            ]
            for t in range(tiles):
                for q in range(4):
                    at = p * exposures * 2 * SHIFT + e * 2 * SHIFT + q * SUBLANES
                    maps[t, pl.ds(pl.multiple_of(at, SUBLANES), SUBLANES)] = quarters[q][t]
                at = p * exposures * SUBLANES + e * SUBLANES
                edges[t, pl.ds(pl.multiple_of(at, SUBLANES), SUBLANES)] = pack_edges(quarters, t)
        return carry

    lax.fori_loop(0, exposures, one_exposure, 0, unroll=2)


def outer_kernel(
    radius, chunks, info, maps, edges, params, tap_rows, above, below, *rest
):
    exposures = params.shape[0]
    tiles = maps.shape[0]
    parts = edges.shape[1] // (exposures * SUBLANES)
    sends, (pixels, colpass, more, more_edges) = rest[: chunks * parts], rest[chunks * parts :]
    taps = 2 * radius + 1
    pad = SUBLANES
    has_above, has_below, own = info[0] > 0, info[1] > 0, info[2]

    colpass[...] = jnp.zeros_like(colpass)

    def row_tap(e, a):
        return tap_rows[e, a : a + 1]

    def col_tap(e, b):
        return tap_rows[e, taps + b : taps + b + 1]

    def one_exposure(e, carry):
        for kind in (0, 1):
            pixels[kind, 0:radius] = jnp.where(has_below, below[kind, e].astype(jnp.float32), 0.0)
            pixels[kind, radius : 2 * radius] = jnp.where(has_above, above[kind, e].astype(jnp.float32), 0.0)
        inverse = pixels[1]
        product = pixels[0] * inverse
        for m, picture in ((0, product), (1, inverse)):
            for t, total in enumerate(column_pass(picture, col_tap, taps, e, m == 1)):
                colpass[m, t, pad : pad + SUBLANES] = total
        upper = [row_pass(colpass, row_tap, e, m, pad + radius, range(radius)) for m in (0, 1)]
        lower = [row_pass(colpass, row_tap, e, m, -radius, range(radius + 1, taps)) for m in (0, 1)]
        for t in range(tiles):
            for m in (0, 1):
                more[0, t, 2 * e + m] = upper[m][t]
                more[1, t, 2 * e + m] = lower[m][t]
            more_edges[0, t, e] = pack_edges([upper[0], None, upper[1], None], t)
            more_edges[1, t, e] = pack_edges([None, lower[0], None, lower[1]], t)
        return carry

    lax.fori_loop(0, exposures, one_exposure, 0, unroll=4)
    main = exposures * 2 * SHIFT
    for step in range(chunks):
        to = partner(own, step, chunks)
        for p in range(parts):
            out = sends[step * parts + p]
            for k in range(2 * exposures):
                first = maps[to, p * main + k * SHIFT : p * main + k * SHIFT + SUBLANES]
                second = maps[to, p * main + k * SHIFT + SUBLANES : p * main + (k + 1) * SHIFT]
                if p == 0:
                    first = first + more[0, to, k]
                if p == parts - 1:
                    second = second + more[1, to, k]
                out[k * SHIFT : (k + 1) * SHIFT] = jnp.concatenate([first, second]).astype(jnp.bfloat16)
            packed = edges[to, p * exposures * SUBLANES : (p + 1) * exposures * SUBLANES]
            if p == 0:
                packed = packed + more_edges[0, to].reshape(packed.shape)
            if p == parts - 1:
                packed = packed + more_edges[1, to].reshape(packed.shape)
            out[main : main + exposures * SUBLANES] = packed.astype(jnp.bfloat16)
            if p == parts - 1:
                tail = main + exposures * SUBLANES
                out[tail : tail + exposures] = params[...].astype(jnp.bfloat16)


def stack_kernel(groups, chunks, exposures, rows, vels, info, *rest):
    parts = rows // SHIFT
    blocks = [rest[p * groups : (p + 1) * groups] for p in range(parts + 1)]
    rest = rest[(parts + 1) * groups :]
    outs = rest[:chunks]
    main, side, even, odd, whole_params, scalars, order, result, sem = rest[chunks:]
    windows = (even, odd)
    own = info[2]
    first_vel = info[4]
    share = result.shape[0]
    main_rows = exposures * 2 * SHIFT
    size = main_rows + exposures * SUBLANES
    total = groups * exposures
    whole_params[total:] = jnp.zeros((exposures, LANES), jnp.int32)
    for g in range(groups):
        whole_params[g * exposures : (g + 1) * exposures] = (
            blocks[parts - 1][g][size : size + exposures].astype(jnp.float32).astype(jnp.int32)
        )
    fetch = pltpu.make_async_copy(whole_params, scalars, sem)
    fetch.start()
    has_below = info[1].astype(jnp.float32)
    for g in range(groups):
        for p in range(parts + 1):
            packed = blocks[p][g][main_rows:size]
            for q in range(4):
                piece = packed if q == 0 else pltpu.roll(packed, LANES - 2 * SHIFT * q, 1)
                piece = piece.astype(jnp.float32)
                if p == parts:
                    piece = piece * has_below
                at = p * SHIFT + (q % 2) * SUBLANES
                for e in range(exposures):
                    side[g * exposures + e, q // 2, at : at + SUBLANES] = piece[e * SUBLANES : (e + 1) * SUBLANES]
            for k in range(2 * exposures):
                cells = blocks[p][g][k * SHIFT : (k + 1) * SHIFT].astype(jnp.float32)
                if p == parts:
                    cells = cells * has_below
                main[g * exposures + k // 2, k % 2, p * SHIFT : (p + 1) * SHIFT] = cells
    main[total] = jnp.zeros(main.shape[1:], jnp.float32)
    side[total] = jnp.zeros(side.shape[1:], jnp.float32)
    fetch.wait()
    filled = jnp.int32(0)
    for source in range(total):
        order[filled] = source
        filled = filled + scalars[source, 2 * vels]
    for i in range(UNROLL):
        order[filled + i] = total
    trips = (filled + UNROLL - 1) // UNROLL

    lane = lax.broadcasted_iota(jnp.int32, (rows, LANES), 1)

    def gather(v, e, sums):
        source = order[e]
        row_at = scalars[source, first_vel + v]
        col_at = scalars[source, vels + first_vel + v] + SHIFT
        from_side = lane < col_at
        cells = jnp.concatenate(
            [
                jnp.where(from_side, side[source, m, pl.ds(row_at, rows)], main[source, m, pl.ds(row_at, rows)])
                for m in (0, 1)
            ]
        ).astype(jnp.bfloat16)
        cells = pltpu.roll(cells, (LANES - col_at) & (LANES - 1), 1).astype(jnp.float32)
        windows[v % 2][e, 0] = cells[:rows]
        windows[v % 2][e, 1] = cells[rows:]
        return sums[0] + cells[:rows], sums[1] + cells[rows:]

    def reweigh(v, e, flux, sums):
        signal = windows[v % 2][e, 0]
        depth = windows[v % 2][e, 1]
        residual = signal - flux * depth
        base = depth + 1.0
        weight = base / (base + residual * residual)
        return sums[0] + weight * signal, sums[1] + weight * depth

    def over_exposures(step, start):
        def trip(t, sums):
            for i in range(UNROLL):
                sums = step(t * UNROLL + i, sums)
            return sums

        return lax.fori_loop(0, trips, trip, start)

    zeros = main[total, 0, 0:rows]
    none = (zeros, zeros)

    sums = over_exposures(functools.partial(gather, 0), none)
    for v in range(share):
        flux = sums[0] / (sums[1] + 1.0)

        def weigh(e, sums, v=v, flux=flux):
            return reweigh(v, e, flux, sums)

        def both(e, sums, v=v, weigh=weigh):
            return gather(v + 1, e, sums[:2]) + weigh(e, sums[2:])

        if v + 1 < share:
            sums = over_exposures(both, none + none)
        else:
            sums = none + over_exposures(weigh, none)
        result[v] = sums[2] / jnp.sqrt(sums[3] + 1.0)
    block = rows // chunks
    for step in range(chunks):
        to = partner(own, step, chunks)
        outs[step][...] = result[:, pl.ds(pl.multiple_of(to * block, block), block)]


def join_kernel(chunks, subs, info, *rest):
    pieces = rest[: chunks * subs]
    out, held = rest[chunks * subs :]
    own_chunk, own_sub = info[2], info[3]
    share, rows = held.shape[2], out.shape[1]
    for u in range(subs):
        for step in range(chunks):
            held[u, step] = pieces[u * chunks + step][...]
    for k in range(subs):
        for c in range(chunks):
            block = held.at[partner(own_sub, k, subs), partner(own_chunk, c, chunks)]
            for v in range(share):
                out[k * share + v, :, c * LANES : (c + 1) * LANES] = block[v, pl.ds(own_sub * rows, rows)]


def per_device(*arguments):
    science, inv_var, psf_rows, psf_cols, row_shift, col_shift, exposure_ok = arguments
    exposures, rows, columns = science.shape
    vels = row_shift.shape[1]
    radius = psf_rows.shape[1] // 2
    strips = lax.axis_size("strip")
    members = lax.axis_size("expo")
    chunks = columns // LANES
    subs = members // chunks
    share = vels // subs
    parts = rows // SHIFT
    strip = lax.axis_index("strip")
    me = lax.axis_index("expo")
    own_chunk = me // subs
    own_sub = me % subs
    info = jnp.stack([strip > 0, strip < strips - 1, own_chunk, own_sub, own_sub * share]).astype(jnp.int32)

    def rows_from(start):
        return jnp.stack([lax.dynamic_slice_in_dim(x, start, radius, 1) for x in (science, inv_var)])

    if strips == 2:
        met = rows_from(jnp.where(strip == 0, rows - radius, 0))
        above = below = lax.ppermute(met, "strip", [(0, 1), (1, 0)])
    else:
        above = lax.ppermute(rows_from(rows - radius), "strip", [(i, i + 1) for i in range(strips - 1)])
        below = lax.ppermute(rows_from(0), "strip", [(i + 1, i) for i in range(strips - 1)])

    map_rows = parts * exposures * 2 * SHIFT
    tap_room = -(-2 * psf_rows.shape[1] // SUBLANES) * SUBLANES
    edge_rows = parts * exposures * SUBLANES
    maps, edges, params, tap_rows = pl.pallas_call(
        functools.partial(inner_kernel, radius),
        out_shape=[
            jax.ShapeDtypeStruct((chunks, map_rows, LANES), jnp.float32),
            jax.ShapeDtypeStruct((chunks, edge_rows, LANES), jnp.float32),
            jax.ShapeDtypeStruct((exposures, LANES), jnp.float32),
            jax.ShapeDtypeStruct((exposures, tap_room, LANES), jnp.float32),
        ],
        in_specs=[HBM] * 7,
        out_specs=[VMEM] * 4,
        scratch_shapes=[
            pltpu.VMEM(science.shape, science.dtype),
            pltpu.VMEM(inv_var.shape, inv_var.dtype),
            pltpu.SMEM(psf_rows.shape, jnp.float32),
            pltpu.SMEM(psf_cols.shape, jnp.float32),
            pltpu.VMEM(row_shift.shape, jnp.int32),
            pltpu.VMEM(col_shift.shape, jnp.int32),
            pltpu.SMEM(exposure_ok.shape, jnp.int32),
            pltpu.VMEM((2, chunks, rows + 2 * SUBLANES, LANES), jnp.float32),
            pltpu.SemaphoreType.DMA((7,)),
        ],
        compiler_params=pltpu.CompilerParams(vmem_limit_bytes=8 << 20),
        cost_estimate=pl.CostEstimate(flops=100_000_000, bytes_accessed=4_000_000, transcendentals=0),
        name="filter_inner",
    )(*[pltpu.with_memory_space_constraint(x, pltpu.HBM) for x in arguments])
    block = exposures * (2 * SHIFT + SUBLANES)
    sent = [
        jax.ShapeDtypeStruct((block + (exposures if p == parts - 1 else 0), LANES), jnp.bfloat16)
        for p in range(parts)
    ]
    sends = pl.pallas_call(
        functools.partial(outer_kernel, radius, chunks),
        out_shape=sent * chunks,
        in_specs=[SMEM] + [VMEM] * 6,
        out_specs=[VMEM] * (chunks * parts),
        scratch_shapes=[
            pltpu.VMEM((2, 2 * radius, columns), jnp.float32),
            pltpu.VMEM((2, chunks, 3 * SUBLANES, LANES), jnp.float32),
            pltpu.VMEM((2, chunks, 2 * exposures, SUBLANES, LANES), jnp.float32),
            pltpu.VMEM((2, chunks, exposures, SUBLANES, LANES), jnp.float32),
        ],
        compiler_params=pltpu.CompilerParams(vmem_limit_bytes=8 << 20),
        name="filter_outer",
    )(info, maps, edges, params, tap_rows, above, below)

    blocks = [[[None] * chunks for _ in range(subs)] for _ in range(parts + 1)]
    up = [((i + 1) % strips, i) for i in range(strips)]
    for step in range(chunks):
        for p in range(parts):
            blocks[p][0][step] = sends[step * parts + p]
            if step:
                blocks[p][0][step] = lax.ppermute(sends[step * parts + p], "expo", chunk_pairs(step, chunks, subs))
        blocks[parts][0][step] = lax.ppermute(blocks[0][0][step], "strip", up)
    for p in range(parts + 1):
        for u in range(1, subs):
            for step in range(chunks):
                blocks[p][u][step] = lax.ppermute(blocks[p][0][step], "expo", sub_pairs(u, chunks, subs))
    blocks = [[block for sub in part for block in sub] for part in blocks]

    groups = len(blocks[0])
    block_rows = rows // chunks
    reach = rows + SHIFT
    piece = jax.ShapeDtypeStruct((share, block_rows, LANES), jnp.float32)
    total = groups * exposures
    pieces = pl.pallas_call(
        functools.partial(stack_kernel, groups, chunks, exposures, rows, vels),
        out_shape=[piece] * chunks,
        in_specs=[SMEM] + [VMEM] * ((parts + 1) * groups),
        out_specs=[VMEM] * chunks,
        scratch_shapes=[
            pltpu.VMEM((total + 1, 2, reach, LANES), jnp.float32),
            pltpu.VMEM((total + 1, 2, reach, LANES), jnp.float32),
            pltpu.VMEM((total + UNROLL, 2, rows, LANES), jnp.float32),
            pltpu.VMEM((total + UNROLL, 2, rows, LANES), jnp.float32),
            pltpu.VMEM((total + exposures, LANES), jnp.int32),
            pltpu.SMEM((total + exposures, LANES), jnp.int32),
            pltpu.SMEM((total + UNROLL,), jnp.int32),
            pltpu.VMEM((share, rows, LANES), jnp.float32),
            pltpu.SemaphoreType.DMA(()),
        ],
        compiler_params=pltpu.CompilerParams(vmem_limit_bytes=24 << 20),
        name="stack_twice",
    )(info, *[block for part in blocks for block in part])

    held = [pieces[0]]
    for step in range(1, chunks):
        held.append(lax.ppermute(pieces[step], "expo", chunk_pairs(step, chunks, subs)))
    groups = [held]
    for u in range(1, subs):
        pairs = sub_pairs(u, chunks, subs)
        groups.append([lax.ppermute(held[step], "expo", pairs) for step in range(chunks)])
    out_rows = block_rows // subs
    likelihood = pl.pallas_call(
        functools.partial(join_kernel, chunks, subs),
        out_shape=jax.ShapeDtypeStruct((vels, out_rows, columns), jnp.float32),
        in_specs=[SMEM] + [VMEM] * (chunks * subs),
        out_specs=VMEM,
        scratch_shapes=[pltpu.VMEM((subs, chunks, share, block_rows, LANES), jnp.float32)],
        compiler_params=pltpu.CompilerParams(vmem_limit_bytes=2 << 20),
        name="join_all",
    )(info, *[block for group in groups for block in group])
    return likelihood[None]


def solution(mesh):
    in_specs = (
        P(("field", "expo"), "strip", None),
        P(("field", "expo"), "strip", None),
        P(("field", "expo"), None),
        P(("field", "expo"), None),
        P(("field", "expo"), None),
        P(("field", "expo"), None),
        P(("field", "expo")),
    )
    out_specs = P("strip", "field", "expo", None)

    return jax.shard_map(per_device, mesh=mesh, in_specs=in_specs, out_specs=out_specs, check_vma=False)
```

```python
import functools

import jax
import jax.numpy as jnp
from jax import lax
from jax.experimental import pallas as pl
from jax.experimental.pallas import tpu as pltpu
from jax.sharding import PartitionSpec as P

SHIFT = 16
LANES = 128
SUBLANES = 8
UNROLL = 18

VMEM = pl.BlockSpec(memory_space=pltpu.VMEM)
HBM = pl.BlockSpec(memory_space=pltpu.HBM)


def whereabouts(subs, first_share):
    strip, strips = lax.axis_index("strip"), lax.axis_size("strip")
    me = lax.axis_index("expo")
    chunk = lax.div(me, subs)
    sub = lax.rem(me, subs)
    return strip > 0, strip < strips - 1, chunk, sub, sub * first_share


def partner(index, step, count):
    if count & (count - 1) == 0:
        return index ^ step
    return (index + step) % count


def chunk_pairs(step, chunks, subs):
    return [
        (j * subs + k, partner(j, step, chunks) * subs + k) for j in range(chunks) for k in range(subs)
    ]


def sub_pairs(step, chunks, subs):
    return [
        (j * subs + k, j * subs + partner(k, step, subs)) for j in range(chunks) for k in range(subs)
    ]


def column_pass(picture, col_tap, taps, e, square):
    tiles = picture.shape[1] // LANES
    lane = lax.broadcasted_iota(jnp.int32, (SUBLANES, LANES), 1)
    zero = jnp.zeros((SUBLANES, LANES), jnp.float32)
    cut = [picture[:, t * LANES : (t + 1) * LANES] for t in range(tiles)]
    totals = None
    for b in range(taps):
        step = b - taps // 2
        tap = col_tap(e, b)
        if square:
            tap = tap * tap
        moved = cut
        if step:
            turned = [pltpu.roll(c, (-step) % LANES, 1) for c in cut]
            if step > 0:
                turned = turned + [zero]
                moved = [jnp.where(lane < LANES - step, turned[t], turned[t + 1]) for t in range(tiles)]
            else:
                turned = [zero] + turned
                moved = [jnp.where(lane >= -step, turned[t + 1], turned[t]) for t in range(tiles)]
        terms = [tap * m for m in moved]
        totals = terms if totals is None else [x + y for x, y in zip(totals, terms)]
    return totals


def row_pass(colpass, row_tap, e, m, first, taps):
    tiles = colpass.shape[1]
    lane = lax.broadcasted_iota(jnp.int32, (SUBLANES, LANES), 1)
    zero = jnp.zeros((SUBLANES, LANES), jnp.float32)
    out = []
    for t in range(tiles):
        total = None
        for a in taps:
            tap = row_tap(e, a)
            if m == 1:
                tap = tap * tap
            term = tap * colpass[m, t, pl.ds(first + a, SUBLANES)]
            total = term if total is None else total + term
        out.append(pltpu.roll(total, SHIFT, 1))
    out = [zero] + out + [zero]
    return [jnp.where(lane < SHIFT, out[t], out[t + 1]) for t in range(tiles + 1)]


def pack_edges(quarters, t):
    lane = lax.broadcasted_iota(jnp.int32, (SUBLANES, LANES), 1)
    packed = jnp.zeros((SUBLANES, LANES), jnp.float32)
    for q, quarter in enumerate(quarters):
        if quarter is None:
            continue
        piece = quarter[t + 1] if q == 0 else pltpu.roll(quarter[t + 1], 2 * SHIFT * q, 1)
        inside = (lane >= 2 * SHIFT * q) & (lane < 2 * SHIFT * (q + 1))
        packed = jnp.where(inside, piece, packed)
    return packed


def inner_kernel(
    radius,
    science_hbm,
    inv_var_hbm,
    row_taps_hbm,
    col_taps_hbm,
    row_shift_hbm,
    col_shift_hbm,
    usable_hbm,
    maps,
    edges,
    params,
    tap_rows,
    science,
    inv_var,
    row_taps,
    col_taps,
    row_shift,
    col_shift,
    usable,
    colpass,
    sems,
):
    exposures, rows, columns = science.shape
    tiles = columns // LANES
    taps = 2 * radius + 1
    vels = row_shift.shape[1]
    pad = SUBLANES
    pairs = (
        (row_taps_hbm, row_taps),
        (col_taps_hbm, col_taps),
        (science_hbm, science),
        (inv_var_hbm, inv_var),
        (row_shift_hbm, row_shift),
        (col_shift_hbm, col_shift),
        (usable_hbm, usable),
    )
    copies = [pltpu.make_async_copy(source, target, sems.at[i]) for i, (source, target) in enumerate(pairs)]
    for copy in copies:
        copy.start()
    colpass[:, :, 0:pad] = jnp.zeros((2, tiles, pad, LANES), jnp.float32)
    colpass[:, :, pad + rows : 2 * pad + rows] = jnp.zeros((2, tiles, pad, LANES), jnp.float32)
    params[...] = jnp.zeros_like(params)
    for copy in copies:
        copy.wait()
    row = lax.broadcasted_iota(jnp.int32, (exposures, 1), 0)
    kept = jnp.zeros((exposures, 1), jnp.int32)
    for e in range(exposures):
        kept = jnp.where(row == e, usable[e], kept)
    params[:, 0:vels] = row_shift[...].astype(jnp.float32)
    params[:, vels : 2 * vels] = col_shift[...].astype(jnp.float32)
    params[:, 2 * vels : 2 * vels + 1] = kept.astype(jnp.float32)
    parts = rows // SHIFT

    def row_tap(e, a):
        return row_taps[e, a]

    def col_tap(e, b):
        return col_taps[e, b]

    def one_exposure(e, carry):
        for a in range(taps):
            tap_rows[e, a : a + 1] = jnp.full((1, LANES), row_taps[e, a])
            tap_rows[e, taps + a : taps + a + 1] = jnp.full((1, LANES), col_taps[e, a])
        inverse_all = inv_var[e].astype(jnp.float32)
        product_all = science[e].astype(jnp.float32) * inverse_all
        for g in range(rows // SUBLANES):
            at = slice(g * SUBLANES, (g + 1) * SUBLANES)
            for m, picture in ((0, product_all[at]), (1, inverse_all[at])):
                for t, total in enumerate(column_pass(picture, col_tap, taps, e, m == 1)):
                    colpass[m, t, pad + g * SUBLANES : pad + (g + 1) * SUBLANES] = total
        for p in range(parts):
            quarters = [
                row_pass(colpass, row_tap, e, m, pad + p * SHIFT + h * SUBLANES - radius, range(taps))
                for m in (0, 1)
                for h in (0, 1)
            ]
            for t in range(tiles):
                for q in range(4):
                    at = p * exposures * 2 * SHIFT + e * 2 * SHIFT + q * SUBLANES
                    maps[t, pl.ds(pl.multiple_of(at, SUBLANES), SUBLANES)] = quarters[q][t]
                at = p * exposures * SUBLANES + e * SUBLANES
                edges[t, pl.ds(pl.multiple_of(at, SUBLANES), SUBLANES)] = pack_edges(quarters, t)
        return carry

    lax.fori_loop(0, exposures, one_exposure, 0, unroll=2)


def outer_kernel(
    radius, chunks, subs, maps, edges, params, tap_rows, above, below, *rest
):
    exposures = params.shape[0]
    tiles = maps.shape[0]
    parts = edges.shape[1] // (exposures * SUBLANES)
    sends, (pixels, colpass, more, more_edges) = rest[: chunks * parts], rest[chunks * parts :]
    taps = 2 * radius + 1
    pad = SUBLANES
    has_above, has_below, own, _, _ = whereabouts(subs, 0)

    colpass[...] = jnp.zeros_like(colpass)

    def row_tap(e, a):
        return tap_rows[e, a : a + 1]

    def col_tap(e, b):
        return tap_rows[e, taps + b : taps + b + 1]

    def one_exposure(e, carry):
        for kind in (0, 1):
            pixels[kind, 0:radius] = jnp.where(has_below, below[kind, e].astype(jnp.float32), 0.0)
            pixels[kind, radius : 2 * radius] = jnp.where(has_above, above[kind, e].astype(jnp.float32), 0.0)
        inverse = pixels[1]
        product = pixels[0] * inverse
        for m, picture in ((0, product), (1, inverse)):
            for t, total in enumerate(column_pass(picture, col_tap, taps, e, m == 1)):
                colpass[m, t, pad : pad + SUBLANES] = total
        upper = [row_pass(colpass, row_tap, e, m, pad + radius, range(radius)) for m in (0, 1)]
        lower = [row_pass(colpass, row_tap, e, m, -radius, range(radius + 1, taps)) for m in (0, 1)]
        for t in range(tiles):
            for m in (0, 1):
                more[0, t, 2 * e + m] = upper[m][t]
                more[1, t, 2 * e + m] = lower[m][t]
            more_edges[0, t, e] = pack_edges([upper[0], None, upper[1], None], t)
            more_edges[1, t, e] = pack_edges([None, lower[0], None, lower[1]], t)
        return carry

    lax.fori_loop(0, exposures, one_exposure, 0, unroll=4)
    main = exposures * 2 * SHIFT
    for step in range(chunks):
        to = partner(own, step, chunks)
        for p in range(parts):
            out = sends[step * parts + p]
            for k in range(2 * exposures):
                first = maps[to, p * main + k * SHIFT : p * main + k * SHIFT + SUBLANES]
                second = maps[to, p * main + k * SHIFT + SUBLANES : p * main + (k + 1) * SHIFT]
                if p == 0:
                    first = first + more[0, to, k]
                if p == parts - 1:
                    second = second + more[1, to, k]
                out[k * SHIFT : (k + 1) * SHIFT] = jnp.concatenate([first, second]).astype(jnp.bfloat16)
            packed = edges[to, p * exposures * SUBLANES : (p + 1) * exposures * SUBLANES]
            if p == 0:
                packed = packed + more_edges[0, to].reshape(packed.shape)
            if p == parts - 1:
                packed = packed + more_edges[1, to].reshape(packed.shape)
            out[main : main + exposures * SUBLANES] = packed.astype(jnp.bfloat16)
            if p == parts - 1:
                tail = main + exposures * SUBLANES
                out[tail : tail + exposures] = params[...].astype(jnp.bfloat16)


def stack_kernel(groups, chunks, subs, exposures, rows, vels, *rest):
    parts = rows // SHIFT
    blocks = [rest[p * groups : (p + 1) * groups] for p in range(parts + 1)]
    rest = rest[(parts + 1) * groups :]
    outs = rest[:chunks]
    main, side, even, odd, whole_params, scalars, order, result, sem = rest[chunks:]
    windows = (even, odd)
    share = result.shape[0]
    _, has_below, own, _, first_vel = whereabouts(subs, share)
    has_below = has_below.astype(jnp.float32)
    main_rows = exposures * 2 * SHIFT
    size = main_rows + exposures * SUBLANES
    total = groups * exposures
    whole_params[total:] = jnp.zeros((exposures, LANES), jnp.int32)
    for g in range(groups):
        whole_params[g * exposures : (g + 1) * exposures] = (
            blocks[parts - 1][g][size : size + exposures].astype(jnp.float32).astype(jnp.int32)
        )
    fetch = pltpu.make_async_copy(whole_params, scalars, sem)
    fetch.start()
    for g in range(groups):
        for p in range(parts + 1):
            packed = blocks[p][g][main_rows:size]
            for q in range(4):
                piece = packed if q == 0 else pltpu.roll(packed, LANES - 2 * SHIFT * q, 1)
                piece = piece.astype(jnp.float32)
                if p == parts:
                    piece = piece * has_below
                at = p * SHIFT + (q % 2) * SUBLANES
                for e in range(exposures):
                    side[g * exposures + e, q // 2, at : at + SUBLANES] = piece[e * SUBLANES : (e + 1) * SUBLANES]
            for k in range(2 * exposures):
                cells = blocks[p][g][k * SHIFT : (k + 1) * SHIFT].astype(jnp.float32)
                if p == parts:
                    cells = cells * has_below
                main[g * exposures + k // 2, k % 2, p * SHIFT : (p + 1) * SHIFT] = cells
    main[total] = jnp.zeros(main.shape[1:], jnp.float32)
    side[total] = jnp.zeros(side.shape[1:], jnp.float32)
    fetch.wait()
    filled = jnp.int32(0)
    for source in range(total):
        order[filled] = source
        filled = filled + scalars[source, 2 * vels]
    for i in range(UNROLL):
        order[filled + i] = total
    trips = (filled + UNROLL - 1) // UNROLL

    lane = lax.broadcasted_iota(jnp.int32, (rows, LANES), 1)

    def gather(v, e, sums):
        source = order[e]
        row_at = scalars[source, first_vel + v]
        col_at = scalars[source, vels + first_vel + v] + SHIFT
        from_side = lane < col_at
        cells = jnp.concatenate(
            [
                jnp.where(from_side, side[source, m, pl.ds(row_at, rows)], main[source, m, pl.ds(row_at, rows)])
                for m in (0, 1)
            ]
        ).astype(jnp.bfloat16)
        cells = pltpu.roll(cells, (LANES - col_at) & (LANES - 1), 1).astype(jnp.float32)
        windows[v % 2][e, 0] = cells[:rows]
        windows[v % 2][e, 1] = cells[rows:]
        return sums[0] + cells[:rows], sums[1] + cells[rows:]

    def reweigh(v, e, flux, sums):
        signal = windows[v % 2][e, 0]
        depth = windows[v % 2][e, 1]
        residual = signal - flux * depth
        base = depth + 1.0
        weight = base / (base + residual * residual)
        return sums[0] + weight * signal, sums[1] + weight * depth

    def over_exposures(step, start):
        def trip(t, sums):
            for i in range(UNROLL):
                sums = step(t * UNROLL + i, sums)
            return sums

        return lax.fori_loop(0, trips, trip, start)

    zeros = main[total, 0, 0:rows]
    none = (zeros, zeros)

    sums = over_exposures(functools.partial(gather, 0), none)
    for v in range(share):
        flux = sums[0] / (sums[1] + 1.0)

        def weigh(e, sums, v=v, flux=flux):
            return reweigh(v, e, flux, sums)

        def both(e, sums, v=v, weigh=weigh):
            return gather(v + 1, e, sums[:2]) + weigh(e, sums[2:])

        if v + 1 < share:
            sums = over_exposures(both, none + none)
        else:
            sums = none + over_exposures(weigh, none)
        result[v] = sums[2] / jnp.sqrt(sums[3] + 1.0)
    block = rows // chunks
    for step in range(chunks):
        to = partner(own, step, chunks)
        outs[step][...] = result[:, pl.ds(pl.multiple_of(to * block, block), block)]


def join_kernel(chunks, subs, *rest):
    pieces = rest[: chunks * subs]
    out, held = rest[chunks * subs :]
    _, _, own_chunk, own_sub, _ = whereabouts(subs, 0)
    share, rows = held.shape[2], out.shape[1]
    for u in range(subs):
        for step in range(chunks):
            held[u, step] = pieces[u * chunks + step][...]
    for k in range(subs):
        for c in range(chunks):
            block = held.at[partner(own_sub, k, subs), partner(own_chunk, c, chunks)]
            for v in range(share):
                out[k * share + v, :, c * LANES : (c + 1) * LANES] = block[v, pl.ds(own_sub * rows, rows)]


def per_device(*arguments):
    science, inv_var, psf_rows, psf_cols, row_shift, col_shift, exposure_ok = arguments
    exposures, rows, columns = science.shape
    vels = row_shift.shape[1]
    radius = psf_rows.shape[1] // 2
    strips = lax.axis_size("strip")
    members = lax.axis_size("expo")
    chunks = columns // LANES
    subs = members // chunks
    share = vels // subs
    parts = rows // SHIFT
    strip = lax.axis_index("strip")

    def rows_from(start):
        return jnp.stack([lax.dynamic_slice_in_dim(x, start, radius, 1) for x in (science, inv_var)])

    if strips == 2:
        met = rows_from(jnp.where(strip == 0, rows - radius, 0))
        above = below = lax.ppermute(met, "strip", [(0, 1), (1, 0)])
    else:
        above = lax.ppermute(rows_from(rows - radius), "strip", [(i, i + 1) for i in range(strips - 1)])
        below = lax.ppermute(rows_from(0), "strip", [(i + 1, i) for i in range(strips - 1)])

    map_rows = parts * exposures * 2 * SHIFT
    tap_room = -(-2 * psf_rows.shape[1] // SUBLANES) * SUBLANES
    edge_rows = parts * exposures * SUBLANES
    maps, edges, params, tap_rows = pl.pallas_call(
        functools.partial(inner_kernel, radius),
        out_shape=[
            jax.ShapeDtypeStruct((chunks, map_rows, LANES), jnp.float32),
            jax.ShapeDtypeStruct((chunks, edge_rows, LANES), jnp.float32),
            jax.ShapeDtypeStruct((exposures, LANES), jnp.float32),
            jax.ShapeDtypeStruct((exposures, tap_room, LANES), jnp.float32),
        ],
        in_specs=[HBM] * 7,
        out_specs=[VMEM] * 4,
        scratch_shapes=[
            pltpu.VMEM(science.shape, science.dtype),
            pltpu.VMEM(inv_var.shape, inv_var.dtype),
            pltpu.SMEM(psf_rows.shape, jnp.float32),
            pltpu.SMEM(psf_cols.shape, jnp.float32),
            pltpu.VMEM(row_shift.shape, jnp.int32),
            pltpu.VMEM(col_shift.shape, jnp.int32),
            pltpu.SMEM(exposure_ok.shape, jnp.int32),
            pltpu.VMEM((2, chunks, rows + 2 * SUBLANES, LANES), jnp.float32),
            pltpu.SemaphoreType.DMA((7,)),
        ],
        compiler_params=pltpu.CompilerParams(vmem_limit_bytes=8 << 20),
        cost_estimate=pl.CostEstimate(flops=100_000_000, bytes_accessed=4_000_000, transcendentals=0),
        name="filter_inner",
    )(*[pltpu.with_memory_space_constraint(x, pltpu.HBM) for x in arguments])
    block = exposures * (2 * SHIFT + SUBLANES)
    sent = [
        jax.ShapeDtypeStruct((block + (exposures if p == parts - 1 else 0), LANES), jnp.bfloat16)
        for p in range(parts)
    ]
    sends = pl.pallas_call(
        functools.partial(outer_kernel, radius, chunks, subs),
        out_shape=sent * chunks,
        in_specs=[VMEM] * 6,
        out_specs=[VMEM] * (chunks * parts),
        scratch_shapes=[
            pltpu.VMEM((2, 2 * radius, columns), jnp.float32),
            pltpu.VMEM((2, chunks, 3 * SUBLANES, LANES), jnp.float32),
            pltpu.VMEM((2, chunks, 2 * exposures, SUBLANES, LANES), jnp.float32),
            pltpu.VMEM((2, chunks, exposures, SUBLANES, LANES), jnp.float32),
        ],
        compiler_params=pltpu.CompilerParams(vmem_limit_bytes=8 << 20),
        name="filter_outer",
    )(maps, edges, params, tap_rows, above, below)

    blocks = [[[None] * chunks for _ in range(subs)] for _ in range(parts + 1)]
    up = [((i + 1) % strips, i) for i in range(strips)]
    for step in range(chunks):
        for p in range(parts):
            blocks[p][0][step] = sends[step * parts + p]
            if step:
                blocks[p][0][step] = lax.ppermute(sends[step * parts + p], "expo", chunk_pairs(step, chunks, subs))
        blocks[parts][0][step] = lax.ppermute(blocks[0][0][step], "strip", up)
    for p in range(parts + 1):
        for u in range(1, subs):
            for step in range(chunks):
                blocks[p][u][step] = lax.ppermute(blocks[p][0][step], "expo", sub_pairs(u, chunks, subs))
    blocks = [[block for sub in part for block in sub] for part in blocks]

    groups = len(blocks[0])
    block_rows = rows // chunks
    reach = rows + SHIFT
    piece = jax.ShapeDtypeStruct((share, block_rows, LANES), jnp.float32)
    total = groups * exposures
    pieces = pl.pallas_call(
        functools.partial(stack_kernel, groups, chunks, subs, exposures, rows, vels),
        out_shape=[piece] * chunks,
        in_specs=[VMEM] * ((parts + 1) * groups),
        out_specs=[VMEM] * chunks,
        scratch_shapes=[
            pltpu.VMEM((total + 1, 2, reach, LANES), jnp.float32),
            pltpu.VMEM((total + 1, 2, reach, LANES), jnp.float32),
            pltpu.VMEM((total + UNROLL, 2, rows, LANES), jnp.float32),
            pltpu.VMEM((total + UNROLL, 2, rows, LANES), jnp.float32),
            pltpu.VMEM((total + exposures, LANES), jnp.int32),
            pltpu.SMEM((total + exposures, LANES), jnp.int32),
            pltpu.SMEM((total + UNROLL,), jnp.int32),
            pltpu.VMEM((share, rows, LANES), jnp.float32),
            pltpu.SemaphoreType.DMA(()),
        ],
        compiler_params=pltpu.CompilerParams(vmem_limit_bytes=24 << 20),
        name="stack_twice",
    )(*[block for part in blocks for block in part])

    held = [pieces[0]]
    for step in range(1, chunks):
        held.append(lax.ppermute(pieces[step], "expo", chunk_pairs(step, chunks, subs)))
    groups = [held]
    for u in range(1, subs):
        pairs = sub_pairs(u, chunks, subs)
        groups.append([lax.ppermute(held[step], "expo", pairs) for step in range(chunks)])
    out_rows = block_rows // subs
    likelihood = pl.pallas_call(
        functools.partial(join_kernel, chunks, subs),
        out_shape=jax.ShapeDtypeStruct((vels, out_rows, columns), jnp.float32),
        in_specs=[VMEM] * (chunks * subs),
        out_specs=VMEM,
        scratch_shapes=[pltpu.VMEM((subs, chunks, share, block_rows, LANES), jnp.float32)],
        compiler_params=pltpu.CompilerParams(vmem_limit_bytes=2 << 20),
        name="join_all",
    )(*[block for group in groups for block in group])
    return likelihood[None]


def solution(mesh):
    in_specs = (
        P(("field", "expo"), "strip", None),
        P(("field", "expo"), "strip", None),
        P(("field", "expo"), None),
        P(("field", "expo"), None),
        P(("field", "expo"), None),
        P(("field", "expo"), None),
        P(("field", "expo")),
    )
    out_specs = P("strip", "field", "expo", None)

    return jax.shard_map(per_device, mesh=mesh, in_specs=in_specs, out_specs=out_specs, check_vma=False)
```

```python
import functools

import jax
import jax.numpy as jnp
from jax import lax
from jax.experimental import pallas as pl
from jax.experimental.pallas import tpu as pltpu
from jax.sharding import PartitionSpec as P

SHIFT = 16
LANES = 128
SUBLANES = 8
UNROLL = 18

VMEM = pl.BlockSpec(memory_space=pltpu.VMEM)
HBM = pl.BlockSpec(memory_space=pltpu.HBM)


def whereabouts(subs, first_share):
    strip, strips = lax.axis_index("strip"), lax.axis_size("strip")
    me = lax.axis_index("expo")
    chunk = lax.div(me, subs)
    sub = lax.rem(me, subs)
    return strip > 0, strip < strips - 1, chunk, sub, sub * first_share


def partner(index, step, count):
    if count & (count - 1) == 0:
        return index ^ step
    return (index + step) % count


def chunk_pairs(step, chunks, subs):
    return [
        (j * subs + k, partner(j, step, chunks) * subs + k) for j in range(chunks) for k in range(subs)
    ]


def sub_pairs(step, chunks, subs):
    return [
        (j * subs + k, j * subs + partner(k, step, subs)) for j in range(chunks) for k in range(subs)
    ]


def column_pass(picture, col_tap, taps, e, square):
    tiles = picture.shape[1] // LANES
    lane = lax.broadcasted_iota(jnp.int32, (SUBLANES, LANES), 1)
    zero = jnp.zeros((SUBLANES, LANES), jnp.float32)
    cut = [picture[:, t * LANES : (t + 1) * LANES] for t in range(tiles)]
    totals = None
    for b in range(taps):
        step = b - taps // 2
        tap = col_tap(e, b, square)
        moved = cut
        if step:
            turned = [pltpu.roll(c, (-step) % LANES, 1) for c in cut]
            if step > 0:
                turned = turned + [zero]
                moved = [jnp.where(lane < LANES - step, turned[t], turned[t + 1]) for t in range(tiles)]
            else:
                turned = [zero] + turned
                moved = [jnp.where(lane >= -step, turned[t + 1], turned[t]) for t in range(tiles)]
        terms = [tap * m for m in moved]
        totals = terms if totals is None else [x + y for x, y in zip(totals, terms)]
    return totals


def row_pass(colpass, row_tap, e, m, first, taps):
    tiles = colpass.shape[1]
    lane = lax.broadcasted_iota(jnp.int32, (SUBLANES, LANES), 1)
    zero = jnp.zeros((SUBLANES, LANES), jnp.float32)
    out = []
    for t in range(tiles):
        total = None
        for a in taps:
            tap = row_tap(e, a, m)
            term = tap * colpass[m, t, pl.ds(first + a, SUBLANES)]
            total = term if total is None else total + term
        out.append(pltpu.roll(total, SHIFT, 1))
    out = [zero] + out + [zero]
    return [jnp.where(lane < SHIFT, out[t], out[t + 1]) for t in range(tiles + 1)]


def pack_edges(quarters, t):
    lane = lax.broadcasted_iota(jnp.int32, (SUBLANES, LANES), 1)
    packed = jnp.zeros((SUBLANES, LANES), jnp.float32)
    for q, quarter in enumerate(quarters):
        if quarter is None:
            continue
        piece = quarter[t + 1] if q == 0 else pltpu.roll(quarter[t + 1], 2 * SHIFT * q, 1)
        inside = (lane >= 2 * SHIFT * q) & (lane < 2 * SHIFT * (q + 1))
        packed = jnp.where(inside, piece, packed)
    return packed


def fetch_kernel(
    radius,
    swap,
    science_hbm,
    inv_var_hbm,
    row_taps_hbm,
    col_taps_hbm,
    row_shift_hbm,
    col_shift_hbm,
    usable_hbm,
    science,
    inv_var,
    tap_rows,
    params,
    *rest,
):
    margins, (row_taps, col_taps, row_shift, col_shift, usable, sems) = rest[:-6], rest[-6:]
    exposures, rows, _ = science.shape
    taps = 2 * radius + 1
    vels = row_shift.shape[1]
    pairs = (
        (science_hbm, science),
        (inv_var_hbm, inv_var),
        (row_taps_hbm, row_taps),
        (col_taps_hbm, col_taps),
        (row_shift_hbm, row_shift),
        (col_shift_hbm, col_shift),
        (usable_hbm, usable),
    )
    copies = [pltpu.make_async_copy(source, target, sems.at[i]) for i, (source, target) in enumerate(pairs)]
    for copy in copies:
        copy.start()
    params[...] = jnp.zeros_like(params)
    for copy in copies:
        copy.wait()
    for kind, cells in enumerate((science, inv_var)):
        for e in range(exposures):
            head = cells[e, 0:SUBLANES].astype(jnp.float32)[:radius]
            tail = cells[e, rows - SUBLANES : rows].astype(jnp.float32)[SUBLANES - radius :]
            if swap:
                margins[0][kind, e] = jnp.where(lax.axis_index("strip") == 0, tail, head).astype(jnp.bfloat16)
            else:
                margins[0][kind, e] = tail.astype(jnp.bfloat16)
                margins[1][kind, e] = head.astype(jnp.bfloat16)
    row = lax.broadcasted_iota(jnp.int32, (exposures, 1), 0)
    kept = jnp.zeros((exposures, 1), jnp.int32)
    for e in range(exposures):
        kept = jnp.where(row == e, usable[e], kept)
        for a in range(taps):
            for i, tap in enumerate((row_taps[e, a], col_taps[e, a])):
                tap = jnp.full((1, LANES), tap)
                tap_rows[e, i * taps + a : i * taps + a + 1] = tap
                tap_rows[e, (2 + i) * taps + a : (2 + i) * taps + a + 1] = tap * tap
    params[:, 0:vels] = row_shift[...].astype(jnp.float32)
    params[:, vels : 2 * vels] = col_shift[...].astype(jnp.float32)
    params[:, 2 * vels : 2 * vels + 1] = kept.astype(jnp.float32)


def tap_readers(tap_rows, taps):
    def row_tap(e, a, square):
        at = 2 * taps * square + a
        return tap_rows[e, at : at + 1]

    def col_tap(e, b, square):
        at = 2 * taps * square + taps + b
        return tap_rows[e, at : at + 1]

    return row_tap, col_tap


def inner_kernel(radius, science, inv_var, tap_rows, maps, edges, colpass):
    exposures, rows, columns = science.shape
    tiles = columns // LANES
    taps = 2 * radius + 1
    pad = SUBLANES
    colpass[:, :, 0:pad] = jnp.zeros((2, tiles, pad, LANES), jnp.float32)
    colpass[:, :, pad + rows : 2 * pad + rows] = jnp.zeros((2, tiles, pad, LANES), jnp.float32)
    parts = rows // SHIFT
    row_tap, col_tap = tap_readers(tap_rows, taps)

    def one_exposure(e, carry):
        inverse_all = inv_var[e].astype(jnp.float32)
        product_all = science[e].astype(jnp.float32) * inverse_all
        for g in range(rows // SUBLANES):
            at = slice(g * SUBLANES, (g + 1) * SUBLANES)
            for m, picture in ((0, product_all[at]), (1, inverse_all[at])):
                for t, total in enumerate(column_pass(picture, col_tap, taps, e, m)):
                    colpass[m, t, pad + g * SUBLANES : pad + (g + 1) * SUBLANES] = total
        for p in range(parts):
            quarters = [
                row_pass(colpass, row_tap, e, m, pad + p * SHIFT + h * SUBLANES - radius, range(taps))
                for m in (0, 1)
                for h in (0, 1)
            ]
            for t in range(tiles):
                for q in range(4):
                    at = p * exposures * 2 * SHIFT + e * 2 * SHIFT + q * SUBLANES
                    maps[t, pl.ds(pl.multiple_of(at, SUBLANES), SUBLANES)] = quarters[q][t]
                at = p * exposures * SUBLANES + e * SUBLANES
                edges[t, pl.ds(pl.multiple_of(at, SUBLANES), SUBLANES)] = pack_edges(quarters, t)
        return carry

    lax.fori_loop(0, exposures, one_exposure, 0, unroll=2)


def outer_kernel(
    radius, chunks, subs, maps, edges, params, tap_rows, above, below, *rest
):
    exposures = params.shape[0]
    tiles = maps.shape[0]
    parts = edges.shape[1] // (exposures * SUBLANES)
    sends, (pixels, colpass, more, more_edges) = rest[: chunks * parts], rest[chunks * parts :]
    taps = 2 * radius + 1
    pad = SUBLANES
    has_above, has_below, own, _, _ = whereabouts(subs, 0)

    colpass[...] = jnp.zeros_like(colpass)

    row_tap, col_tap = tap_readers(tap_rows, taps)

    def one_exposure(e, carry):
        for kind in (0, 1):
            pixels[kind, 0:radius] = jnp.where(has_below, below[kind, e].astype(jnp.float32), 0.0)
            pixels[kind, radius : 2 * radius] = jnp.where(has_above, above[kind, e].astype(jnp.float32), 0.0)
        inverse = pixels[1]
        product = pixels[0] * inverse
        for m, picture in ((0, product), (1, inverse)):
            for t, total in enumerate(column_pass(picture, col_tap, taps, e, m)):
                colpass[m, t, pad : pad + SUBLANES] = total
        upper = [row_pass(colpass, row_tap, e, m, pad + radius, range(radius)) for m in (0, 1)]
        lower = [row_pass(colpass, row_tap, e, m, -radius, range(radius + 1, taps)) for m in (0, 1)]
        for t in range(tiles):
            for m in (0, 1):
                more[0, t, 2 * e + m] = upper[m][t]
                more[1, t, 2 * e + m] = lower[m][t]
            more_edges[0, t, e] = pack_edges([upper[0], None, upper[1], None], t)
            more_edges[1, t, e] = pack_edges([None, lower[0], None, lower[1]], t)
        return carry

    lax.fori_loop(0, exposures, one_exposure, 0, unroll=8)
    main = exposures * 2 * SHIFT
    for step in range(chunks):
        to = partner(own, step, chunks)
        for p in range(parts):
            out = sends[step * parts + p]
            for k in range(2 * exposures):
                first = maps[to, p * main + k * SHIFT : p * main + k * SHIFT + SUBLANES]
                second = maps[to, p * main + k * SHIFT + SUBLANES : p * main + (k + 1) * SHIFT]
                if p == 0:
                    first = first + more[0, to, k]
                if p == parts - 1:
                    second = second + more[1, to, k]
                out[k * SHIFT : (k + 1) * SHIFT] = jnp.concatenate([first, second]).astype(jnp.bfloat16)
            packed = edges[to, p * exposures * SUBLANES : (p + 1) * exposures * SUBLANES]
            if p == 0:
                packed = packed + more_edges[0, to].reshape(packed.shape)
            if p == parts - 1:
                packed = packed + more_edges[1, to].reshape(packed.shape)
            out[main : main + exposures * SUBLANES] = packed.astype(jnp.bfloat16)
            if p == parts - 1:
                tail = main + exposures * SUBLANES
                out[tail : tail + exposures] = params[...].astype(jnp.bfloat16)


def stack_kernel(groups, chunks, subs, exposures, rows, vels, *rest):
    parts = rows // SHIFT
    blocks = [rest[p * groups : (p + 1) * groups] for p in range(parts + 1)]
    rest = rest[(parts + 1) * groups :]
    outs = rest[:chunks]
    main, side, even, odd, whole_params, scalars, order, result, sem = rest[chunks:]
    windows = (even, odd)
    share = result.shape[0]
    _, has_below, own, _, first_vel = whereabouts(subs, share)
    has_below = has_below.astype(jnp.float32)
    main_rows = exposures * 2 * SHIFT
    size = main_rows + exposures * SUBLANES
    total = groups * exposures
    whole_params[total:] = jnp.zeros((exposures, LANES), jnp.int32)
    for g in range(groups):
        whole_params[g * exposures : (g + 1) * exposures] = (
            blocks[parts - 1][g][size : size + exposures].astype(jnp.float32).astype(jnp.int32)
        )
    fetch = pltpu.make_async_copy(whole_params, scalars, sem)
    fetch.start()
    for g in range(groups):
        for p in range(parts + 1):
            packed = blocks[p][g][main_rows:size]
            for q in range(4):
                piece = packed if q == 0 else pltpu.roll(packed, LANES - 2 * SHIFT * q, 1)
                piece = piece.astype(jnp.float32)
                if p == parts:
                    piece = piece * has_below
                at = p * SHIFT + (q % 2) * SUBLANES
                for e in range(exposures):
                    side[g * exposures + e, q // 2, at : at + SUBLANES] = piece[e * SUBLANES : (e + 1) * SUBLANES]
            for k in range(2 * exposures):
                cells = blocks[p][g][k * SHIFT : (k + 1) * SHIFT].astype(jnp.float32)
                if p == parts:
                    cells = cells * has_below
                main[g * exposures + k // 2, k % 2, p * SHIFT : (p + 1) * SHIFT] = cells
    main[total] = jnp.zeros(main.shape[1:], jnp.float32)
    side[total] = jnp.zeros(side.shape[1:], jnp.float32)
    fetch.wait()
    filled = jnp.int32(0)
    for source in range(total):
        order[filled] = source
        filled = filled + scalars[source, 2 * vels]
    for i in range(UNROLL):
        order[filled + i] = total
    trips = (filled + UNROLL - 1) // UNROLL

    lane = lax.broadcasted_iota(jnp.int32, (rows, LANES), 1)

    def gather(v, e, sums):
        source = order[e]
        row_at = scalars[source, first_vel + v]
        col_at = scalars[source, vels + first_vel + v] + SHIFT
        from_side = lane < col_at
        cells = jnp.concatenate(
            [
                jnp.where(from_side, side[source, m, pl.ds(row_at, rows)], main[source, m, pl.ds(row_at, rows)])
                for m in (0, 1)
            ]
        ).astype(jnp.bfloat16)
        cells = pltpu.roll(cells, (LANES - col_at) & (LANES - 1), 1).astype(jnp.float32)
        windows[v % 2][e, 0] = cells[:rows]
        windows[v % 2][e, 1] = cells[rows:]
        return sums[0] + cells[:rows], sums[1] + cells[rows:]

    def reweigh(v, e, flux, sums):
        signal = windows[v % 2][e, 0]
        depth = windows[v % 2][e, 1]
        residual = signal - flux * depth
        base = depth + 1.0
        weight = base / (base + residual * residual)
        return sums[0] + weight * signal, sums[1] + weight * depth

    def over_exposures(step, start):
        def trip(t, sums):
            for i in range(UNROLL):
                sums = step(t * UNROLL + i, sums)
            return sums

        return lax.fori_loop(0, trips, trip, start)

    zeros = main[total, 0, 0:rows]
    none = (zeros, zeros)

    sums = over_exposures(functools.partial(gather, 0), none)
    for v in range(share):
        flux = sums[0] / (sums[1] + 1.0)

        def weigh(e, sums, v=v, flux=flux):
            return reweigh(v, e, flux, sums)

        def both(e, sums, v=v, weigh=weigh):
            return gather(v + 1, e, sums[:2]) + weigh(e, sums[2:])

        if v + 1 < share:
            sums = over_exposures(both, none + none)
        else:
            sums = none + over_exposures(weigh, none)
        result[v] = sums[2] / jnp.sqrt(sums[3] + 1.0)
    block = rows // chunks
    for step in range(chunks):
        to = partner(own, step, chunks)
        outs[step][...] = result[:, pl.ds(pl.multiple_of(to * block, block), block)]


def join_kernel(chunks, subs, *rest):
    pieces = rest[: chunks * subs]
    out, held = rest[chunks * subs :]
    _, _, own_chunk, own_sub, _ = whereabouts(subs, 0)
    share, rows = held.shape[2], out.shape[1]
    for u in range(subs):
        for step in range(chunks):
            held[u, step] = pieces[u * chunks + step][...]
    for k in range(subs):
        for c in range(chunks):
            block = held.at[partner(own_sub, k, subs), partner(own_chunk, c, chunks)]
            for v in range(share):
                out[k * share + v, :, c * LANES : (c + 1) * LANES] = block[v, pl.ds(own_sub * rows, rows)]


def per_device(*arguments):
    science, inv_var, psf_rows, psf_cols, row_shift, col_shift, exposure_ok = arguments
    exposures, rows, columns = science.shape
    vels = row_shift.shape[1]
    radius = psf_rows.shape[1] // 2
    strips = lax.axis_size("strip")
    members = lax.axis_size("expo")
    chunks = columns // LANES
    subs = members // chunks
    share = vels // subs
    parts = rows // SHIFT
    tap_room = -(-4 * psf_rows.shape[1] // SUBLANES) * SUBLANES
    margin = jax.ShapeDtypeStruct((2, exposures, radius, columns), science.dtype)
    science, inv_var, tap_rows, params, *margins = pl.pallas_call(
        functools.partial(fetch_kernel, radius, strips == 2),
        out_shape=[
            jax.ShapeDtypeStruct(science.shape, science.dtype),
            jax.ShapeDtypeStruct(inv_var.shape, inv_var.dtype),
            jax.ShapeDtypeStruct((exposures, tap_room, LANES), jnp.float32),
            jax.ShapeDtypeStruct((exposures, LANES), jnp.float32),
        ]
        + [margin] * (1 if strips == 2 else 2),
        in_specs=[HBM] * 7,
        out_specs=[VMEM] * (5 if strips == 2 else 6),
        scratch_shapes=[
            pltpu.SMEM(psf_rows.shape, jnp.float32),
            pltpu.SMEM(psf_cols.shape, jnp.float32),
            pltpu.VMEM(row_shift.shape, jnp.int32),
            pltpu.VMEM(col_shift.shape, jnp.int32),
            pltpu.SMEM(exposure_ok.shape, jnp.int32),
            pltpu.SemaphoreType.DMA((7,)),
        ],
        compiler_params=pltpu.CompilerParams(vmem_limit_bytes=4 << 20),
        name="fetch",
    )(*[pltpu.with_memory_space_constraint(x, pltpu.HBM) for x in arguments])
    if strips == 2:
        above = below = lax.ppermute(margins[0], "strip", [(0, 1), (1, 0)])
    else:
        above = lax.ppermute(margins[0], "strip", [(i, i + 1) for i in range(strips - 1)])
        below = lax.ppermute(margins[1], "strip", [(i + 1, i) for i in range(strips - 1)])

    map_rows = parts * exposures * 2 * SHIFT
    edge_rows = parts * exposures * SUBLANES
    maps, edges = pl.pallas_call(
        functools.partial(inner_kernel, radius),
        out_shape=[
            jax.ShapeDtypeStruct((chunks, map_rows, LANES), jnp.float32),
            jax.ShapeDtypeStruct((chunks, edge_rows, LANES), jnp.float32),
        ],
        in_specs=[VMEM] * 3,
        out_specs=[VMEM] * 2,
        scratch_shapes=[pltpu.VMEM((2, chunks, rows + 2 * SUBLANES, LANES), jnp.float32)],
        compiler_params=pltpu.CompilerParams(vmem_limit_bytes=8 << 20),
        cost_estimate=pl.CostEstimate(flops=100_000_000, bytes_accessed=4_000_000, transcendentals=0),
        name="filter_inner",
    )(science, inv_var, tap_rows)
    block = exposures * (2 * SHIFT + SUBLANES)
    sent = [
        jax.ShapeDtypeStruct((block + (exposures if p == parts - 1 else 0), LANES), jnp.bfloat16)
        for p in range(parts)
    ]
    sends = pl.pallas_call(
        functools.partial(outer_kernel, radius, chunks, subs),
        out_shape=sent * chunks,
        in_specs=[VMEM] * 6,
        out_specs=[VMEM] * (chunks * parts),
        scratch_shapes=[
            pltpu.VMEM((2, 2 * radius, columns), jnp.float32),
            pltpu.VMEM((2, chunks, 3 * SUBLANES, LANES), jnp.float32),
            pltpu.VMEM((2, chunks, 2 * exposures, SUBLANES, LANES), jnp.float32),
            pltpu.VMEM((2, chunks, exposures, SUBLANES, LANES), jnp.float32),
        ],
        compiler_params=pltpu.CompilerParams(vmem_limit_bytes=8 << 20),
        name="filter_outer",
    )(maps, edges, params, tap_rows, above, below)

    blocks = [[[None] * chunks for _ in range(subs)] for _ in range(parts + 1)]
    up = [((i + 1) % strips, i) for i in range(strips)]
    for step in range(chunks):
        for p in range(parts):
            blocks[p][0][step] = sends[step * parts + p]
            if step:
                blocks[p][0][step] = lax.ppermute(sends[step * parts + p], "expo", chunk_pairs(step, chunks, subs))
        blocks[parts][0][step] = lax.ppermute(blocks[0][0][step], "strip", up)
    for p in range(parts + 1):
        for u in range(1, subs):
            for step in range(chunks):
                blocks[p][u][step] = lax.ppermute(blocks[p][0][step], "expo", sub_pairs(u, chunks, subs))
    blocks = [[block for sub in part for block in sub] for part in blocks]

    groups = len(blocks[0])
    block_rows = rows // chunks
    reach = rows + SHIFT
    piece = jax.ShapeDtypeStruct((share, block_rows, LANES), jnp.float32)
    total = groups * exposures
    pieces = pl.pallas_call(
        functools.partial(stack_kernel, groups, chunks, subs, exposures, rows, vels),
        out_shape=[piece] * chunks,
        in_specs=[VMEM] * ((parts + 1) * groups),
        out_specs=[VMEM] * chunks,
        scratch_shapes=[
            pltpu.VMEM((total + 1, 2, reach, LANES), jnp.float32),
            pltpu.VMEM((total + 1, 2, reach, LANES), jnp.float32),
            pltpu.VMEM((total + UNROLL, 2, rows, LANES), jnp.float32),
            pltpu.VMEM((total + UNROLL, 2, rows, LANES), jnp.float32),
            pltpu.VMEM((total + exposures, LANES), jnp.int32),
            pltpu.SMEM((total + exposures, LANES), jnp.int32),
            pltpu.SMEM((total + UNROLL,), jnp.int32),
            pltpu.VMEM((share, rows, LANES), jnp.float32),
            pltpu.SemaphoreType.DMA(()),
        ],
        compiler_params=pltpu.CompilerParams(vmem_limit_bytes=24 << 20),
        name="stack_twice",
    )(*[block for part in blocks for block in part])

    held = [pieces[0]]
    for step in range(1, chunks):
        held.append(lax.ppermute(pieces[step], "expo", chunk_pairs(step, chunks, subs)))
    groups = [held]
    for u in range(1, subs):
        pairs = sub_pairs(u, chunks, subs)
        groups.append([lax.ppermute(held[step], "expo", pairs) for step in range(chunks)])
    out_rows = block_rows // subs
    likelihood = pl.pallas_call(
        functools.partial(join_kernel, chunks, subs),
        out_shape=jax.ShapeDtypeStruct((vels, out_rows, columns), jnp.float32),
        in_specs=[VMEM] * (chunks * subs),
        out_specs=VMEM,
        scratch_shapes=[pltpu.VMEM((subs, chunks, share, block_rows, LANES), jnp.float32)],
        compiler_params=pltpu.CompilerParams(vmem_limit_bytes=2 << 20),
        name="join_all",
    )(*[block for group in groups for block in group])
    return likelihood[None]


def solution(mesh):
    in_specs = (
        P(("field", "expo"), "strip", None),
        P(("field", "expo"), "strip", None),
        P(("field", "expo"), None),
        P(("field", "expo"), None),
        P(("field", "expo"), None),
        P(("field", "expo"), None),
        P(("field", "expo")),
    )
    out_specs = P("strip", "field", "expo", None)

    return jax.shard_map(per_device, mesh=mesh, in_specs=in_specs, out_specs=out_specs, check_vma=False)
```
